256 devices in a mesh: patch: 64 (over z, y, x_hi), sub: 4 (over x_lo, core).
Axes of the slice: x: 4 (x_hi: 2, x_lo: 2; x = x_hi * 2 + x_lo), y: 4, z: 8, core: 2. Of those that a mesh axis runs over, the one named last changes fastest.
Arguments:
- pieces_image: float32 [4, 2048, 8, 256], P('sub', 'patch'), may hold values from -6 to 6
- pieces_variance: float32 [4, 2048, 8, 256], P('sub', 'patch'), may hold values from 0.5 to 2
- piece_patch: int32 [4, 2048, 1], P('sub', 'patch'), may hold values from 0 to 63; in each aligned block of 32 rows (0 to 31, 32 to 63, ..., all dimensions but the last counted through in order) at most 2 rows name the same one
- piece_cell: int32 [4, 2048], P('sub', 'patch'), may hold values from 0 to 31
- stamp_row: int32 [64, 48], P('patch', 'sub'), may hold values from 0 to 63
- stamp_col: int32 [64, 48], P('patch', 'sub'), may hold values from 0 to 255
- stamp_count: int32 [64, 4], P('patch', 'sub'), may hold values from 2 to 12, as said below
- warp_offsets: int32 [4], replicated, may hold values from 0 to 8
Outputs:
- difference: float32 [4, 64, 256, 256], P(None, 'patch', 'sub')
- significance: float32 [4, 64, 256, 256], P(None, 'patch', 'sub')
The draws below stay inside these ranges and needn't reach their ends.
Inputs may be any that keep to these rules, and one draw needn't show every extreme that they name: `piece_patch`: the pieces of one device name the same patch at most 2 times, and in every draw some device names some patch exactly 2 times. `stamp_count`: stamps of a sub-tile whose index is this count or more are unused.
All inputs are finite; a program needn't handle non-finite values.
Results may differ from the reference program's by a relative error of at most 0.0003.
Values sent between devices are 32-bit elements; how exact they have to be, the bound alone decides.
A program may use at most 64 MiB of HBM per device.

```python
import math
import jax
import jax.numpy as jnp
import numpy as np
from jax import lax

V = 4
NCELL = 8
RT = 64
CW = 256
NS = 12
NB = 40
KR = 10
PR = 10
SH = 15
WARP = 4
CR = 8
NP = 32
CAP = 2
N_PATCH = 64
N_SUB = 4


def draw_stamp_count(key, part):
    position = jnp.arange(N_SUB).astype(jnp.int32)
    lowest = jnp.maximum(position * NS // N_SUB + 1, 2)
    highest = (position + 1) * NS // N_SUB + 1
    return jax.random.randint(key, (N_PATCH, N_SUB), lowest[None, :], highest[None, :]).astype(jnp.int32)


def draw_stamp_row(key, part):
    first_key, second_key, third_key = jax.random.split(key, 3)
    reach = min(SH, RT)
    general = jax.random.randint(first_key, (N_PATCH, N_SUB, NS), 0, RT).astype(jnp.int32)
    near_top = jax.random.randint(second_key, (N_PATCH, N_SUB, 1), 0, reach).astype(jnp.int32)
    near_bottom = jax.random.randint(third_key, (N_PATCH, N_SUB, 1), RT - reach, RT).astype(jnp.int32)
    values = jnp.concatenate([near_top, near_bottom, general[:, :, 2:]], axis=2)
    return values.reshape(N_PATCH, N_SUB * NS)


def draw_warp_offsets(key, part):
    first_key, second_key = jax.random.split(key)
    middle = jax.random.randint(first_key, (V - 2,), 0, 2 * WARP + 1).astype(jnp.int32)
    values = jnp.concatenate([jnp.array([0, 2 * WARP], jnp.int32), middle])
    return values[jax.random.permutation(second_key, V)]


def set_ends(values, stream_key, least, top_value):
    shape = values.shape
    place = [jax.random.randint(jax.random.fold_in(stream_key, axis), (), 0, shape[axis]) for axis in range(len(shape))]
    values = values.at[tuple(place)].set(least)
    longest = shape.index(max(shape))
    place[longest] = (place[longest] + 1) % shape[longest]
    return values.at[tuple(place)].set(top_value)


def level_of(key, shape, shards, least, high):
    factor_of, own = 1.0, jax.random.fold_in(key, 6)
    for dim, shards_of in shards:
        heights = jnp.exp(jax.random.uniform(jax.random.fold_in(own, dim), (shards_of,), jnp.float32, least / len(shards), high / len(shards)))
        factor_of = factor_of * jnp.repeat(heights, shape[dim] // shards_of).reshape([-1 if axis == dim else 1 for axis in range(len(shape))])
    return factor_of


def deal_out(rng, own, number, rows, amount, top, bound, skew):
    order = jax.random.permutation(rng, amount)
    crowded, common = portions_of(amount, rows * top, bound, skew, True), portions_of(amount, rows * top, bound, skew, False)
    places = jnp.arange(amount)

    def named(sizes, rotation):
        used = int((sizes > 0).sum())
        fixed = max(1, used // 4)
        passed = fixed + (places - fixed + rotation * (used - fixed)) % max(1, amount - fixed)
        return jnp.zeros((amount,), jnp.int32).at[order[jnp.where(places < fixed, places, passed)]].set(jnp.asarray(sizes, jnp.int32))

    sizes = jnp.where(number % 4 == 0, named(crowded, number // 4), named(common, number - number // 4 - 1))
    mixed = jax.random.permutation(jax.random.fold_in(own, 3), amount)
    giver, taker = mixed[0:amount // 2 * 2:2], mixed[1:amount // 2 * 2:2]
    room = jnp.minimum(sizes[giver] - 1, bound - sizes[taker]) // 2
    room = jnp.where((giver == order[0]) | (taker == order[0]) | (sizes[taker] == 0), 0, jnp.maximum(room, 0))
    passed = jax.random.randint(jax.random.fold_in(own, 4), (amount // 2,), 0, 1 << 20) % (room + 1)
    sizes = sizes.at[giver].add(-passed).at[taker].add(passed)
    labels = jnp.searchsorted(jnp.cumsum(sizes), jnp.arange(rows * top), side="right").astype(jnp.int32)
    grid = labels.reshape(top, rows).T
    grid = grid[jax.random.permutation(jax.random.fold_in(own, 1), rows)]
    rotation = jax.random.randint(jax.random.fold_in(own, 2), (rows, 1), 0, top)
    return jnp.take_along_axis(grid, (jnp.arange(top)[None, :] + rotation) % top, axis=1)


def portions_of(count, total, limit, skew, full):
    loads = [(1 << 20) // math.isqrt(rank ** skew) + 1 for rank in range(1, count + 1)]
    largest = limit if full else min(limit, max(-(-total // count), total * loads[0] // sum(loads)))
    least = 1 if total - largest >= count - 1 else 0
    given, spare = [largest] + [least] * (count - 1), total - largest - least * (count - 1)
    while spare > 0:
        free = [i for i in range(1, count) if given[i] < largest] or [i for i in range(1, count) if given[i] < limit]
        mass, budget = sum([loads[i] for i in free]), spare
        for i in free:
            extra = min(limit - given[i], max(1, budget * loads[i] // mass), spare)
            given[i] = given[i] + extra
            spare = spare - extra
    return np.array(given)


def centred(rng, extent, deviation, most, cuts=(), kind=jnp.bfloat16):
    values = deviation * jax.random.normal(rng, extent, jnp.float32)
    if cuts:
        values = values * level_of(rng, extent, cuts, -0.22, 0.18)
    return jnp.clip(values, -most, most).astype(kind)


def setup_inputs(seed: int = 0) -> dict:
    seeds = jax.random.split(jax.random.key(seed), 9)
    pieces_image = centred(seeds[0], (N_SUB, NP * N_PATCH, CR, CW), 1.0, 6.0, ((0, 4), (1, 64)), jnp.float32)
    pieces_variance = jnp.clip(jnp.exp(math.log(2.0) - 1.3862944 * jax.random.uniform(seeds[1], (N_SUB, NP * N_PATCH, CR, CW), jnp.float32) ** level_of(seeds[1], (N_SUB, NP * N_PATCH, CR, CW), ((0, 4), (1, 64)), -0.2, 0.2)), 0.5, 2.0)
    piece_patch_keys = jax.random.split(jax.random.fold_in(seeds[2], 1), N_SUB * (NP * N_PATCH) // NP)
    piece_patch_turns = jax.random.permutation(jax.random.fold_in(seeds[2], 3), N_SUB * (NP * N_PATCH) // NP)
    piece_patch = jax.vmap(lambda own, number: deal_out(jax.random.fold_in(seeds[2], 2), own, number, NP, N_PATCH, 1, CAP, 2))(piece_patch_keys, piece_patch_turns).reshape((N_SUB, NP * N_PATCH, 1))
    piece_cell = set_ends(jax.random.randint(seeds[3], (N_SUB, NP * N_PATCH), 0, V * NCELL), jax.random.fold_in(seeds[3], 1), 0, (V * NCELL) - 1).astype(jnp.int32)
    stamp_row = draw_stamp_row(jax.random.fold_in(seeds[8], 71), 0)
    stamp_col = set_ends(jax.random.randint(seeds[5], (N_PATCH, N_SUB * NS), 0, CW), jax.random.fold_in(seeds[5], 1), 0, CW - 1).astype(jnp.int32)
    stamp_count = draw_stamp_count(jax.random.fold_in(seeds[8], 71), 0)
    warp_offsets = draw_warp_offsets(jax.random.fold_in(seeds[8], 71), 0)
    return dict(pieces_image=pieces_image, pieces_variance=pieces_variance, piece_patch=piece_patch, piece_cell=piece_cell, stamp_row=stamp_row, stamp_col=stamp_col, stamp_count=stamp_count, warp_offsets=warp_offsets)


SIGMAS = (0.75, 1.5, 3.0)
DEGREES = (4, 4, 3)
PSF_SIGMA = 2.0
SKY_VAR = 0.1
RIDGE = 0.5
EPS = 1e-05
HIGH = lax.Precision.HIGHEST

def hermite(degree, argument):
    previous = jnp.ones_like(argument)
    if degree == 0:
        return previous
    current = argument
    for term_no in range(1, degree):
        previous, current = (current, argument * current - term_no * previous)
    return current

def shapes_at(offset):
    result = []
    for spread, degree in zip(SIGMAS, DEGREES):
        scaled = offset / spread
        envelope = jnp.exp(-0.5 * scaled * scaled)
        for term_no in range(degree + 1):
            result.append(hermite(term_no, scaled) * envelope)
    return jnp.stack(result)

def basis_taps():
    offset = jnp.arange(-KR, KR + 1).astype(jnp.float32)
    unscaled = shapes_at(offset)
    return unscaled / jnp.sqrt(lax.optimization_barrier(jnp.sum(unscaled * unscaled, axis=1, keepdims=True)))

def psf_value(offset, power):
    support = jnp.arange(-PR, PR + 1).astype(jnp.float32)
    summed = jnp.sum(jnp.exp(-0.5 * (support / PSF_SIGMA) ** 2))
    return (jnp.exp(-0.5 * (offset / PSF_SIGMA) ** 2) / summed) ** power

def group_pairs():
    result = []
    first_tap = 0
    for degree in DEGREES:
        members = []
        for row_tap in range(degree + 1):
            for col_tap in range(degree + 1 - row_tap):
                members.append((first_tap + row_tap, first_tap + col_tap))
        result.append(members)
        first_tap += degree + 1
    return result

def filter_columns(image, filter_taps):
    radius = (filter_taps.shape[1] - 1) // 2
    col_count = image.shape[-1]
    padded = jnp.pad(image, [(0, 0)] * (image.ndim - 1) + [(radius, radius)])
    result = jnp.zeros((filter_taps.shape[0],) + image.shape, jnp.float32)
    expand = (-1,) + (1,) * image.ndim
    for tap_no in range(2 * radius + 1):
        result = result + filter_taps[:, tap_no].reshape(expand) * padded[..., tap_no:tap_no + col_count][None]
    return result

def filter_rows(image, filter_taps):
    radius = (filter_taps.shape[1] - 1) // 2
    row_count = image.shape[-2]
    padded = jnp.pad(image, [(0, 0)] * (image.ndim - 2) + [(radius, radius), (0, 0)])
    result = jnp.zeros((filter_taps.shape[0],) + image.shape, jnp.float32)
    expand = (-1,) + (1,) * image.ndim
    for tap_no in range(2 * radius + 1):
        result = result + filter_taps[:, tap_no].reshape(expand) * padded[..., tap_no:tap_no + row_count, :][None]
    return result

def solve_kernel(gram_matrix, right_side, normalizer):
    gram_matrix = gram_matrix / normalizer
    right_side = right_side / normalizer
    scaling = 1.0 / jnp.sqrt(jnp.diagonal(gram_matrix) + EPS)
    system = gram_matrix * scaling[:, None] * scaling[None, :] + RIDGE * jnp.eye(gram_matrix.shape[0], dtype=jnp.float32)
    factor = jnp.linalg.cholesky(system)
    return jax.scipy.linalg.cho_solve((factor, True), right_side * scaling) * scaling

def reference(pieces_image, pieces_variance, piece_patch, piece_cell, stamp_row, stamp_col, stamp_count, warp_offsets):
    slot_count = V * NCELL
    sub_index = jnp.arange(N_SUB).astype(jnp.int32)[:, None]
    segment = ((sub_index * N_PATCH + piece_patch[:, :, 0]) * slot_count + piece_cell).reshape(-1)
    segment_total = N_SUB * N_PATCH * slot_count
    piece_total = N_SUB * NP * N_PATCH
    image_sum = jax.ops.segment_sum(pieces_image.reshape(piece_total, CR * CW), segment, num_segments=segment_total)
    variance_sum = jax.ops.segment_sum(pieces_variance.reshape(piece_total, CR * CW), segment, num_segments=segment_total)
    row_count = N_SUB * RT

    def arrange(flat_sum):
        sectioned = flat_sum.reshape(N_SUB, N_PATCH, V, RT, CW).transpose(1, 2, 0, 3, 4)
        padded = jnp.pad(sectioned.reshape(N_PATCH, V, row_count, CW), ((0, 0), (0, 0), (0, 0), (WARP, WARP)))
        return jax.vmap(lambda visit_plane, offset: lax.dynamic_slice_in_dim(visit_plane, offset, CW, axis=2), in_axes=(1, 0), out_axes=1)(padded, warp_offsets)
    science_all = arrange(image_sum)
    variance_all = arrange(variance_sum)
    filter_taps = basis_taps()
    pairs = [pair for members in group_pairs() for pair in members]
    support = jnp.arange(-PR, PR + 1).astype(jnp.float32)
    psf_one = psf_value(support, 1)[None]
    psf_two = psf_value(support, 2)[None]
    normalizer = N_SUB * NS * (2 * SH + 1) ** 2

    def one_patch(inputs):
        science, variance, rows_here, cols_here, counts_here = inputs
        template = lax.optimization_barrier(jnp.sum(science, axis=0)) / V
        template_var = lax.optimization_barrier(jnp.sum(variance, axis=0)) / (V * V)
        filtered = filter_columns(template, filter_taps)
        design = jnp.stack([filter_rows(filtered[col_tap], filter_taps[row_tap:row_tap + 1])[0] for row_tap, col_tap in pairs] + [jnp.ones((row_count, CW), jnp.float32)]).reshape(NB + 1, row_count * CW)
        centre_rows = (jnp.arange(N_SUB).astype(jnp.int32)[:, None] * RT + rows_here.reshape(N_SUB, NS)).reshape(-1)
        live = (jnp.arange(NS).astype(jnp.int32)[None, :] < counts_here[:, None]).reshape(-1)
        row_in = ((jnp.abs(jnp.arange(row_count).astype(jnp.int32)[None, :] - centre_rows[:, None]) <= SH) & live[:, None]).astype(jnp.float32)
        col_in = (jnp.abs(jnp.arange(CW).astype(jnp.int32)[None, :] - cols_here[:, None]) <= SH).astype(jnp.float32)
        stamp_mask = jnp.minimum(jnp.dot(row_in.T.astype(jnp.float32), col_in.astype(jnp.float32), precision=HIGH, preferred_element_type=jnp.float32), 1.0)
        diff_list = []
        sig_list = []
        for visit_no in range(V):
            total_var = variance[visit_no] + template_var + SKY_VAR
            weight = (stamp_mask / total_var).reshape(-1)
            weighted = design * weight[None, :]
            gram_matrix = jnp.einsum('kp,lp->kl', weighted, design, precision=HIGH)
            right_side = jnp.einsum('kp,p->k', weighted, science[visit_no].reshape(-1), precision=HIGH)
            coefficients = solve_kernel(gram_matrix, right_side, normalizer)
            model = jnp.einsum('k,kp->p', coefficients, design, precision=HIGH).reshape(row_count, CW)
            difference = science[visit_no] - model
            numerator = filter_rows(filter_columns(difference / total_var, psf_one)[0], psf_one)[0]
            denominator = filter_rows(filter_columns(1.0 / total_var, psf_two)[0], psf_two)[0]
            diff_list.append(difference)
            sig_list.append(numerator / jnp.sqrt(denominator))
        return (jnp.stack(diff_list), jnp.stack(sig_list))
    diffs, sigs = lax.map(one_patch, (science_all, variance_all, stamp_row, stamp_col, stamp_count))
    return (diffs.transpose(1, 0, 2, 3), sigs.transpose(1, 0, 2, 3))
```

```python
import functools
import math

import jax
import jax.numpy as jnp
import numpy as np
from jax import lax
from jax.experimental import pallas as pl
from jax.experimental.pallas import tpu as pltpu
from jax.sharding import PartitionSpec as P

V = 4
NCELL = 8
CR = 8
RT = 64
CW = 256
KR = 10
PR = 10
SH = 15
WARP = 4
NB = 40
NP = 32
SIGMAS = (0.75, 1.5, 3.0)
DEGREES = (4, 4, 3)
PSF_SIGMA = 2.0
SKY_VAR = 0.1
RIDGE = 0.5
EPS = 1e-05
HIGH = lax.Precision.HIGHEST

NT = 14
XR = 48
TE = 128
CE = 96
TH = 24
SR = 16
HALO = TH + 2 * V * SR
VMEM_LIMIT = 56 * 1024 * 1024
WHOLE = pl.BlockSpec(memory_space=pltpu.VMEM)
SCALARS = pl.BlockSpec(memory_space=pltpu.SMEM)


def tap_values():
    u = np.arange(-KR, KR + 1).astype(np.float64)
    rows = []
    for sigma, degree in zip(SIGMAS, DEGREES):
        t = u / sigma
        env = np.exp(-0.5 * t * t)
        he = [np.ones_like(t), t]
        for n in range(1, degree):
            he.append(t * he[n] - n * he[n - 1])
        for n in range(degree + 1):
            h = he[n] * env
            rows.append(h / np.sqrt(np.sum(h * h)))
    return np.stack(rows)


def psf_values():
    u = np.arange(-PR, PR + 1).astype(np.float64)
    g = np.exp(-0.5 * (u / PSF_SIGMA) ** 2)
    return g / g.sum()


def split_np(a):
    a = a.astype(np.float32)
    hi = a.astype(jnp.bfloat16)
    lo = (a - hi.astype(np.float32)).astype(jnp.bfloat16)
    return hi, lo


def band(taps, rows, cols, first):
    radius = (len(taps) - 1) // 2
    out = np.zeros((rows, cols))
    for r in range(rows):
        for u in range(-radius, radius + 1):
            c = r + first + u
            if 0 <= c < cols:
                out[r, c] = taps[u + radius]
    return out


def constants():
    taps = tap_values()
    bands = np.concatenate([band(taps[j], CE, TE, SR) for j in range(NT)], axis=0)
    hi, lo = split_np(bands)
    row_bands = np.concatenate([hi, lo], axis=1)
    p = psf_values()
    cols, rows = [], []
    for f in (p, p * p):
        cols += list(split_np(band(f, CW, CW, 0)))
        h, l = split_np(band(f, RT, CE, SR))
        rows.append(np.concatenate([h, l, h], axis=1))
    return row_bands, np.stack(cols), np.stack(rows)


def members_of():
    result, first_tap, first = [], 0, 0
    for degree in DEGREES:
        index = {}
        for i in range(degree + 1):
            for j in range(degree + 1 - i):
                index[(i, j)] = first + len(index)
        result.append((first_tap, degree, index))
        first_tap += degree + 1
        first += len(index)
    return result


def split(x):
    hi = x.astype(jnp.bfloat16)
    return hi, (x - hi.astype(jnp.float32)).astype(jnp.bfloat16)


def mm(a, b):
    return jnp.dot(a, b, preferred_element_type=jnp.float32)


def pack_kernel(patch, cell, image, variance, out, out_cell, count):
    def clear(n, _):
        out_cell[n] = -1
        return 0

    def clear_count(n, _):
        count[n] = 0
        return 0

    slots = out.shape[0]
    lax.fori_loop(0, slots, clear, 0)
    lax.fori_loop(0, slots // 2, clear_count, 0)

    def place(n, _):
        q = patch[n]
        rank = count[q]
        count[q] = rank + 1
        slot = 2 * q + rank
        out_cell[slot] = cell[n]
        out[slot, 0:CR, :] = image[n]
        out[slot, CR : 2 * CR, :] = variance[n]
        return 0

    lax.fori_loop(0, image.shape[0], place, 0)


def combine_kernel(cells, warp, got, science, variance, template, up, down, acc):
    acc[...] = jnp.zeros_like(acc)

    def add(n, _):
        c = cells[n]
        c = jnp.where(c < 0, V * NCELL, c)
        acc[c] += got[n]
        return 0

    lax.fori_loop(0, got.shape[0], add, 0)
    col = lax.broadcasted_iota(jnp.int32, (CR, CW), 1)
    for v in range(V):
        off = warp[v]
        turn = jnp.where(off <= WARP, WARP - off, CW + WARP - off)
        source = col + (off - WARP)
        inside = (source >= 0) & (source < CW)
        for c in range(NCELL):
            rows = slice(c * CR, (c + 1) * CR)
            a = acc[v * NCELL + c, 0:CR, :]
            b = acc[v * NCELL + c, CR : 2 * CR, :]
            science[v, rows, :] = jnp.where(inside, pltpu.roll(a, turn, 1), 0.0)
            variance[v, rows, :] = jnp.where(inside, pltpu.roll(b, turn, 1), 0.0)
    template[...] = (science[0] + science[1] + science[2] + science[3]) / V
    up[0:TH, :] = template[0:TH, :]
    down[0:TH, :] = template[RT - TH : RT, :]
    for v in range(V):
        s_at, w_at = TH + v * SR, TH + (V + v) * SR
        up[s_at : s_at + SR, :] = science[v, 0:SR, :]
        up[w_at : w_at + SR, :] = variance[v, 0:SR, :]
        down[s_at : s_at + SR, :] = science[v, RT - SR : RT, :]
        down[w_at : w_at + SR, :] = variance[v, RT - SR : RT, :]


def gram_kernel(
    science, variance, template, above, below, mask, row_bands,
    basis, gram, text, filt, xleft, xright, weight, acc,
):
    taps = tap_values()

    def put(k, image):
        at = pl.ds(k, RT, stride=XR)
        xleft[at, :] = image[:, 0:128]
        xright[at, :] = image[:, 128:CW]

    zero8 = jnp.zeros((8, CW), jnp.float32)
    text[0:8, :] = zero8
    text[8:32, :] = above[0:TH, :]
    text[32:96, :] = template[...]
    text[96:120, :] = below[0:TH, :]
    text[120:128, :] = zero8
    col = lax.broadcasted_iota(jnp.int32, (8, CW), 1)

    def columns(i, _):
        rows = pl.ds(pl.multiple_of(i * 8, 8), 8)
        t = text[rows, :]
        sums = [None] * NT
        for u in range(0, KR + 1):
            if u:
                plus = jnp.where(col < CW - u, pltpu.roll(t, CW - u, 1), 0.0)
                minus = jnp.where(col >= u, pltpu.roll(t, u, 1), 0.0)
                even, odd = plus + minus, plus - minus
            first = 0
            for degree in DEGREES:
                for n in range(degree + 1):
                    j = first + n
                    h = float(np.float32(taps[j, KR + u]))
                    if u == 0:
                        sums[j] = t * h if n % 2 == 0 else None
                    else:
                        term = (even if n % 2 == 0 else odd) * h
                        sums[j] = term if sums[j] is None else sums[j] + term
                first += degree + 1
        for j in range(NT):
            filt[j, rows, :] = sums[j]
        return 0

    lax.fori_loop(0, TE // 8, columns, 0)

    for first_tap, degree, index in members_of():
        for j in range(degree + 1):
            count = degree + 1 - j
            lhs = row_bands[first_tap * CE : (first_tap + count) * CE, :]
            fh, fl = split(filt[first_tap + j])
            y = mm(lhs, jnp.concatenate([fh, fh], axis=0)) + mm(lhs[:, 0:TE], fl)
            for i in range(count):
                k = index[(i, j)]
                image = y[i * CE : (i + 1) * CE, :]
                basis[k] = image
                put(k, image[SR : SR + RT, :])
    put(NB, jnp.ones((RT, CW), jnp.float32))
    for v in range(V):
        put(NB + 1 + v, science[v])
    for n in range(NB + 1 + V, XR):
        put(n, jnp.zeros((RT, CW), jnp.float32))

    q = (variance[0] + variance[1] + variance[2] + variance[3]) / (V * V)
    m = mask[...]
    for v in range(V):
        weight[v] = m / (variance[v] + q + SKY_VAR)

    acc[...] = jnp.zeros_like(acc)
    step = 4

    def rows_of(i, _):
        lefts, rights = [], []
        for r0 in range(step):
            r = i * step + r0
            at = pl.ds(pl.multiple_of(r * XR, 8), XR)
            x = jnp.concatenate([xleft[at, :], xright[at, :]], axis=1)
            xh, xl = split(x)
            rights.append(jnp.concatenate([xh, xl, jnp.zeros((32, CW), jnp.bfloat16)], axis=0))
            his, los = [], []
            for v in range(V):
                lh, ll = split(x * weight[v, pl.ds(r, 1), :])
                his.append(lh)
                los.append(ll)
            lefts.append(jnp.concatenate(his + los, axis=0))
        left = jnp.concatenate(lefts, axis=1)
        right = jnp.concatenate(rights, axis=1)
        acc[...] += lax.dot_general(
            left, right, (((1,), (1,)), ((), ())), preferred_element_type=jnp.float32
        )
        return 0

    lax.fori_loop(0, RT // step, rows_of, 0)
    high = acc[0 : V * XR, :]
    total = high + pltpu.roll(high, 128 - XR, 1) + acc[V * XR : 2 * V * XR, :]
    lane = lax.broadcasted_iota(jnp.int32, total.shape, 1)
    total = jnp.where(lane < XR, total, 0.0)
    gram[...] = total[0 : 2 * XR, :] + pltpu.roll(total[2 * XR : 4 * XR, :], 64, 1)


def pick(x, index):
    return jnp.take_along_axis(x, index, axis=1, mode="promise_in_bounds")


def final_kernel(
    normalizer, sub, gathered, basis, science, variance, above, below, cols, rows,
    difference, significance, coef, dplane, iplane,
):
    total = gathered[0] + gathered[1] + gathered[2] + gathered[3]
    total = total * (1.0 / normalizer)
    row = lax.broadcasted_iota(jnp.int32, (XR, 128), 0)
    lane = lax.broadcasted_iota(jnp.int32, (XR, 128), 1)
    part = lane // 64
    j = lane - part * 64
    base = part * 64
    halves, scales = [], []
    for half in range(2):
        a = total[half * XR : (half + 1) * XR, :]
        v = half + 2 * part
        e_col = lax.rsqrt(pick(a, base + row) + EPS)
        diag = jnp.sum(jnp.where(row == j, a, 0.0), axis=0, keepdims=True)
        e_row = lax.rsqrt(diag + EPS)
        scaled = a * e_col
        system = jnp.where(j <= NB, scaled * e_row, jnp.where(j == NB + 1 + v, scaled, 0.0))
        system = system + jnp.where(row == j, RIDGE, 0.0)
        halves.append(system)
        scales.append(e_col)
    for k in range(NB + 1):
        for half in range(2):
            a = halves[half]
            pivot_row = jnp.broadcast_to(a[k : k + 1, :], (XR, 128))
            pivot = pick(pivot_row, base + k)
            column = pick(a, base + k)
            column = jnp.where(row == k, pivot - 1.0, column)
            halves[half] = a - column * (pivot_row / pivot)
    for half in range(2):
        v = half + 2 * part
        a = pick(halves[half], base + NB + 1 + v) * scales[half]
        coef[half * XR : (half + 1) * XR, :] = pick(a, lane * 0)
        coef[(half + 2) * XR : (half + 3) * XR, :] = pick(a, lane * 0 + 64)

    me = sub[0]

    def block(b, _):
        at = pl.multiple_of(b * 8, 8)
        grow = lax.broadcasted_iota(jnp.int32, (8, CW), 0) + (b * 8 - SR)
        valid = ((grow >= 0) | (me > 0)) & ((grow < RT) | (me < 3))
        edge_a, edge_b = b < 2, b >= 10
        inner = pl.ds(pl.multiple_of(jnp.clip(b - 2, 0, 7) * 8, 8), 8)
        top = jnp.clip(b, 0, 1) * 8
        low = jnp.clip(b - 10, 0, 1) * 8

        def pull(own, first, v):
            at_a = pl.ds(pl.multiple_of(first + v * SR + top, 8), 8)
            at_b = pl.ds(pl.multiple_of(first + v * SR + low, 8), 8)
            return jnp.where(edge_a, above[at_a, :], jnp.where(edge_b, below[at_b, :], own[v, inner, :]))

        s = [pull(science, TH, v) for v in range(V)]
        w = [pull(variance, TH + V * SR, v) for v in range(V)]
        q = (w[0] + w[1] + w[2] + w[3]) / (V * V)
        acc = [s[v] - jnp.concatenate([coef[v * XR + NB : v * XR + NB + 1, :]] * 2, axis=1) for v in range(V)]
        for k in range(NB):
            c = basis[k, pl.ds(at, 8), :]
            for v in range(V):
                a = coef[v * XR + k : v * XR + k + 1, :]
                acc[v] = acc[v] - c * jnp.concatenate([a, a], axis=1)
        for v in range(V):
            inverse = jnp.where(valid, 1.0 / (w[v] + q + SKY_VAR), 0.0)
            plane = pl.ds(pl.multiple_of(v * CE + b * 8, 8), 8)
            dplane[plane, :] = acc[v] * inverse
            iplane[plane, :] = inverse

        @pl.when((b >= 2) & (b < 10))
        def _():
            for v in range(V):
                difference[v, inner, :] = acc[v]

        return 0

    lax.fori_loop(0, CE // 8, block, 0)
    filtered = []
    for n, plane in enumerate((dplane, iplane)):
        hi, lo = split(plane[...])
        ph, plo = cols[2 * n], cols[2 * n + 1]
        y = mm(hi, ph) + mm(lo, ph) + mm(hi, plo)
        yh, yl = split(y)
        outs = []
        for v in range(V):
            a = slice(v * CE, (v + 1) * CE)
            outs.append(mm(rows[n], jnp.concatenate([yh[a], yh[a], yl[a]], axis=0)))
        filtered.append(outs)
    for v in range(V):
        significance[v] = filtered[0][v] * lax.rsqrt(filtered[1][v])


def shape(*dims, dtype=jnp.float32):
    return jax.ShapeDtypeStruct(dims, dtype)


def params():
    return pltpu.CompilerParams(vmem_limit_bytes=VMEM_LIMIT)


def local(
    pieces_image, pieces_variance, piece_patch, piece_cell,
    stamp_row, stamp_col, stamp_count, warp_offsets,
):
    patches = lax.axis_size("patch")
    subtiles = lax.axis_size("sub")
    slot_total = 2 * patches
    me = lax.axis_index("sub")
    up_pairs = [(i + 1, i) for i in range(subtiles - 1)]
    down_pairs = [(i, i + 1) for i in range(subtiles - 1)]

    slots = stamp_row.shape[1]
    my_first = me * RT
    live_here = (jnp.arange(slots) < stamp_count[0, 0]).astype(jnp.int32)
    table = jnp.stack([stamp_row[0] + my_first, stamp_col[0], live_here])
    near = jnp.concatenate(
        [lax.ppermute(table, "sub", down_pairs), table, lax.ppermute(table, "sub", up_pairs)], axis=1
    )
    my_rows = my_first + jnp.arange(RT)
    row_in = (
        (jnp.abs(my_rows[None, :] - near[0][:, None]) <= SH) & (near[2][:, None] > 0)
    ).astype(jnp.bfloat16)
    col_in = (jnp.abs(jnp.arange(CW)[None, :] - near[1][:, None]) <= SH).astype(jnp.bfloat16)
    mask = jnp.minimum(jnp.dot(row_in.T, col_in, preferred_element_type=jnp.float32), 1.0)

    sent, sent_cell = pl.pallas_call(
        pack_kernel,
        out_shape=(shape(slot_total, 2 * CR, CW), shape(slot_total, dtype=jnp.int32)),
        in_specs=[SCALARS, SCALARS, WHOLE, WHOLE],
        out_specs=(WHOLE, SCALARS),
        scratch_shapes=[pltpu.SMEM((patches,), jnp.int32)],
        compiler_params=params(),
        name="pack",
    )(piece_patch.reshape(-1), piece_cell.reshape(-1), pieces_image[0], pieces_variance[0])
    got_cell = lax.all_to_all(
        sent_cell.reshape(patches, 2), "patch", split_axis=0, concat_axis=0, tiled=True
    )
    got = lax.all_to_all(
        sent.reshape(patches, 4 * CR, CW), "patch", split_axis=0, concat_axis=0, tiled=True
    )
    field = shape(V, RT, CW)
    science, variance, template, up, down = pl.pallas_call(
        combine_kernel,
        out_shape=(field, field, shape(RT, CW), shape(HALO, CW), shape(HALO, CW)),
        in_specs=[SCALARS, SCALARS, WHOLE],
        out_specs=(WHOLE,) * 5,
        scratch_shapes=[pltpu.VMEM((V * NCELL + 1, 2 * CR, CW), jnp.float32)],
        compiler_params=params(),
        name="combine",
    )(got_cell.reshape(-1), warp_offsets, got.reshape(slot_total, 2 * CR, CW))
    above = lax.ppermute(down, "sub", down_pairs)
    below = lax.ppermute(up, "sub", up_pairs)

    row_bands, cols, rows = constants()
    basis, gram = pl.pallas_call(
        gram_kernel,
        out_shape=(shape(NB, CE, CW), shape(2 * XR, 128)),
        in_specs=[WHOLE] * 7,
        out_specs=(WHOLE,) * 2,
        scratch_shapes=[
            pltpu.VMEM((TE, CW), jnp.float32),
            pltpu.VMEM((NT, TE, CW), jnp.float32),
            pltpu.VMEM((RT * XR, 128), jnp.float32),
            pltpu.VMEM((RT * XR, 128), jnp.float32),
            pltpu.VMEM((V, RT, CW), jnp.float32),
            pltpu.VMEM((2 * V * XR, 128), jnp.float32),
        ],
        compiler_params=params(),
        name="gram",
    )(science, variance, template, above, below, mask, jnp.asarray(row_bands))
    copies = jnp.broadcast_to(gram, (subtiles, *gram.shape))
    gathered = lax.all_to_all(copies, "sub", split_axis=0, concat_axis=0, tiled=True)

    normalizer = float(subtiles * slots * (2 * SH + 1) ** 2)
    difference, significance = pl.pallas_call(
        functools.partial(final_kernel, normalizer),
        out_shape=(field, field),
        in_specs=[SCALARS] + [WHOLE] * 8,
        out_specs=(WHOLE,) * 2,
        scratch_shapes=[
            pltpu.VMEM((V * XR, 128), jnp.float32),
            pltpu.VMEM((V * CE, CW), jnp.float32),
            pltpu.VMEM((V * CE, CW), jnp.float32),
        ],
        compiler_params=params(),
        name="final",
    )(
        me.reshape(1).astype(jnp.int32), gathered, basis, science, variance, above, below,
        jnp.asarray(cols), jnp.asarray(rows),
    )
    return (difference[:, None], significance[:, None])


def solution(mesh):
    in_specs = (
        P("sub", "patch", None, None),
        P("sub", "patch", None, None),
        P("sub", "patch", None),
        P("sub", "patch"),
        P("patch", "sub"),
        P("patch", "sub"),
        P("patch", "sub"),
        P(),
    )
    out_specs = (P(None, "patch", "sub", None), P(None, "patch", "sub", None))
    return jax.shard_map(local, mesh=mesh, in_specs=in_specs, out_specs=out_specs, check_vma=False)
```

```python
import functools
import math

import jax
import jax.numpy as jnp
import numpy as np
from jax import lax
from jax.experimental import pallas as pl
from jax.experimental.pallas import tpu as pltpu
from jax.sharding import PartitionSpec as P

V = 4
NCELL = 8
CR = 8
RT = 64
CW = 256
KR = 10
PR = 10
SH = 15
WARP = 4
NB = 40
NP = 32
SIGMAS = (0.75, 1.5, 3.0)
DEGREES = (4, 4, 3)
PSF_SIGMA = 2.0
SKY_VAR = 0.1
RIDGE = 0.5
EPS = 1e-05
MESH = pl.DeviceIdType.MESH

NT = 14
XR = 48
TE = 128
CE = 96
TH = 24
SR = 16
HALO = TH + V * SR
VMEM_LIMIT = 16 * 1024 * 1024
WHOLE = pl.BlockSpec(memory_space=pltpu.VMEM)
SCALARS = pl.BlockSpec(memory_space=pltpu.SMEM)


def tap_values():
    u = np.arange(-KR, KR + 1).astype(np.float64)
    rows = []
    for sigma, degree in zip(SIGMAS, DEGREES):
        t = u / sigma
        env = np.exp(-0.5 * t * t)
        he = [np.ones_like(t), t]
        for n in range(1, degree):
            he.append(t * he[n] - n * he[n - 1])
        for n in range(degree + 1):
            h = he[n] * env
            rows.append(h / np.sqrt(np.sum(h * h)))
    return np.stack(rows)


def psf_values():
    u = np.arange(-PR, PR + 1).astype(np.float64)
    g = np.exp(-0.5 * (u / PSF_SIGMA) ** 2)
    return g / g.sum()


def split_np(a):
    a = a.astype(np.float32)
    hi = a.astype(jnp.bfloat16)
    lo = (a - hi.astype(np.float32)).astype(jnp.bfloat16)
    return hi, lo


def band(taps, rows, cols, first):
    radius = (len(taps) - 1) // 2
    out = np.zeros((rows, cols))
    for r in range(rows):
        for u in range(-radius, radius + 1):
            c = r + first + u
            if 0 <= c < cols:
                out[r, c] = taps[u + radius]
    return out


def constants():
    taps = tap_values()
    bands = np.concatenate([band(taps[j], CE, TE, SR) for j in range(NT)], axis=0)
    hi, lo = split_np(bands)
    row_bands = np.concatenate([hi, lo], axis=1)
    p = psf_values()
    cols, rows = [], []
    for f in (p, p * p):
        cols += list(split_np(band(f, CW, CW, 0)))
        h, l = split_np(band(f, RT, CE, SR))
        rows.append(np.concatenate([h, l, h], axis=1))
    return row_bands, np.stack(cols), np.stack(rows)


def members_of():
    result, first_tap, first = [], 0, 0
    for degree in DEGREES:
        index = {}
        for i in range(degree + 1):
            for j in range(degree + 1 - i):
                index[(i, j)] = first + len(index)
        result.append((first_tap, degree, index))
        first_tap += degree + 1
        first += len(index)
    return result


def split(x):
    hi = x.astype(jnp.bfloat16)
    return hi, (x - hi.astype(jnp.float32)).astype(jnp.bfloat16)


def mm(a, b):
    return jnp.dot(a, b, preferred_element_type=jnp.float32)


def pack_kernel(patch, cell, image, variance, out_image, out_variance, out_cell, count, slot_cell):
    patches = out_image.shape[0]

    def clear(n, _):
        count[n] = 0
        slot_cell[2 * n] = -1
        slot_cell[2 * n + 1] = -1
        return 0

    lax.fori_loop(0, patches, clear, 0)

    def place(n, _):
        q = patch[n]
        rank = count[q]
        count[q] = rank + 1
        slot_cell[2 * q + rank] = cell[n]
        rows = pl.ds(pl.multiple_of(rank * CR, CR), CR)
        out_image[q, rows, :] = image[n]
        out_variance[q, rows, :] = variance[n]
        return 0

    lax.fori_loop(0, image.shape[0], place, 0)
    lane = lax.broadcasted_iota(jnp.int32, (1, 128), 1)

    def tell(q, _):
        out_cell[q] = jnp.where(lane == 0, slot_cell[2 * q], slot_cell[2 * q + 1])
        return 0

    lax.fori_loop(0, patches, tell, 0)


def exchange_kernel(cells, stamps, got_cells, got_stamps, send, recv, ring_send, ring_recv, own):
    patches = cells.shape[0]
    subtiles = lax.axis_size("sub")
    me, sub = lax.axis_index("patch"), lax.axis_index("sub")
    right, left = lax.rem(sub + 1, subtiles), lax.rem(sub + subtiles - 1, subtiles)
    barrier = pltpu.get_barrier_semaphore()

    def greet(d, _):
        q = lax.rem(me + d, patches)
        pl.semaphore_signal(barrier, inc=1, device_id={"patch": q}, device_id_type=MESH)
        return 0

    lax.fori_loop(1, patches, greet, 0)
    for s in (left, right):
        pl.semaphore_signal(barrier, inc=1, device_id={"sub": s}, device_id_type=MESH)
    pl.semaphore_wait(barrier, patches + 1)

    def copy(d, to, at):
        return pltpu.make_async_remote_copy(
            src_ref=cells.at[to], dst_ref=got_cells.at[at], send_sem=send.at[d],
            recv_sem=recv.at[d], device_id={"patch": to}, device_id_type=MESH,
        )

    def start(d, _):
        copy(d, lax.rem(me + d, patches), me).start()
        return 0

    lax.fori_loop(1, patches, start, 0)
    rings = [
        pltpu.make_async_remote_copy(
            src_ref=stamps, dst_ref=got_stamps.at[n], send_sem=ring_send.at[n],
            recv_sem=ring_recv.at[n], device_id={"sub": to}, device_id_type=MESH,
        )
        for n, to in enumerate((right, left))
    ]
    for ring in rings:
        ring.start()
    mine = pltpu.make_async_copy(cells.at[me], got_cells.at[me], own)
    mine.start()
    mine.wait()

    def finish(d, _):
        copy(d, lax.rem(me + d, patches), me).wait_send()
        source = lax.rem(me + patches - d, patches)
        copy(d, source, source).wait_recv()
        return 0

    lax.fori_loop(1, patches, finish, 0)
    for ring in rings:
        ring.wait()


def gather_kernel(part, gathered, send, recv, own):
    subtiles = gathered.shape[0]
    sub = lax.axis_index("sub")
    peers = [lax.rem(sub + d, subtiles) for d in range(1, subtiles)]
    barrier = pltpu.get_barrier_semaphore()
    for s in peers:
        pl.semaphore_signal(barrier, inc=1, device_id={"sub": s}, device_id_type=MESH)
    pl.semaphore_wait(barrier, subtiles - 1)
    copies = [
        pltpu.make_async_remote_copy(
            src_ref=part, dst_ref=gathered.at[sub], send_sem=send.at[n], recv_sem=recv.at[n],
            device_id={"sub": s}, device_id_type=MESH,
        )
        for n, s in enumerate(peers)
    ]
    for copy in copies:
        copy.start()
    mine = pltpu.make_async_copy(part, gathered.at[sub], own)
    mine.start()
    mine.wait()
    for n, copy in enumerate(copies):
        copy.wait_send()
        source = lax.rem(sub + subtiles - 1 - n, subtiles)
        pltpu.make_async_remote_copy(
            src_ref=part, dst_ref=gathered.at[source], send_sem=send.at[n], recv_sem=recv.at[n],
            device_id={"sub": source}, device_id_type=MESH,
        ).wait_recv()


def combine(cells, warp, got, out, acc):
    acc[...] = jnp.zeros_like(acc)

    def add(q, _):
        for rank in range(2):
            c = cells[q, 0, rank]
            c = jnp.where(c < 0, V * NCELL, c)
            acc[c] += got[q, rank * CR : (rank + 1) * CR, :]
        return 0

    lax.fori_loop(0, got.shape[0], add, 0)
    col = lax.broadcasted_iota(jnp.int32, (CR, CW), 1)
    for v in range(V):
        off = warp[v]
        turn = jnp.where(off <= WARP, WARP - off, CW + WARP - off)
        source = col + (off - WARP)
        inside = (source >= 0) & (source < CW)
        for c in range(NCELL):
            a = acc[v * NCELL + c]
            out[v, c * CR : (c + 1) * CR, :] = jnp.where(inside, pltpu.roll(a, turn, 1), 0.0)


def image_kernel(cells, warp, got, science, template, up, down, acc):
    combine(cells, warp, got, science, acc)
    template[...] = (science[0] + science[1] + science[2] + science[3]) / V
    up[0:TH, :] = template[0:TH, :]
    down[0:TH, :] = template[RT - TH : RT, :]
    for v in range(V):
        at = TH + v * SR
        up[at : at + SR, :] = science[v, 0:SR, :]
        down[at : at + SR, :] = science[v, RT - SR : RT, :]


def variance_kernel(cells, warp, got, token, variance, up, down, acc):
    combine(cells, warp, got, variance, acc)
    for v in range(V):
        up[v * SR : (v + 1) * SR, :] = variance[v, 0:SR, :]
        down[v * SR : (v + 1) * SR, :] = variance[v, RT - SR : RT, :]


def basis_kernel(
    science, template, above, below, row_bands, basis, xleft, xright, token, text, filt,
):
    token[...] = jnp.zeros_like(token)
    taps = tap_values()

    def put(k, image):
        at = pl.ds(k, RT, stride=XR)
        xleft[at, :] = image[:, 0:128]
        xright[at, :] = image[:, 128:CW]

    zero8 = jnp.zeros((8, CW), jnp.float32)
    text[0:8, :] = zero8
    text[8:32, :] = above[0:TH, :]
    text[32:96, :] = template[...]
    text[96:120, :] = below[0:TH, :]
    text[120:128, :] = zero8
    col = lax.broadcasted_iota(jnp.int32, (8, CW), 1)

    def columns(i, _):
        rows = pl.ds(pl.multiple_of(i * 8, 8), 8)
        t = text[rows, :]
        sums = [None] * NT
        for u in range(0, KR + 1):
            if u:
                plus = jnp.where(col < CW - u, pltpu.roll(t, CW - u, 1), 0.0)
                minus = jnp.where(col >= u, pltpu.roll(t, u, 1), 0.0)
                even, odd = plus + minus, plus - minus
            first = 0
            for degree in DEGREES:
                for n in range(degree + 1):
                    j = first + n
                    h = float(np.float32(taps[j, KR + u]))
                    if u == 0:
                        sums[j] = t * h if n % 2 == 0 else None
                    else:
                        term = (even if n % 2 == 0 else odd) * h
                        sums[j] = term if sums[j] is None else sums[j] + term
                first += degree + 1
        for j in range(NT):
            filt[j, rows, :] = sums[j]
        return 0

    lax.fori_loop(0, TE // 8, columns, 0)

    for first_tap, degree, index in members_of():
        for j in range(degree + 1):
            count = degree + 1 - j
            lhs = row_bands[first_tap * CE : (first_tap + count) * CE, :]
            fh, fl = split(filt[first_tap + j])
            y = mm(lhs, jnp.concatenate([fh, fh], axis=0)) + mm(lhs[:, 0:TE], fl)
            for i in range(count):
                k = index[(i, j)]
                image = y[i * CE : (i + 1) * CE, :]
                basis[k] = image
                put(k, image[SR : SR + RT, :])
    put(NB, jnp.ones((RT, CW), jnp.float32))
    for v in range(V):
        put(NB + 1 + v, science[v])
    for n in range(NB + 1 + V, XR):
        put(n, jnp.zeros((RT, CW), jnp.float32))


def gram_kernel(variance, mask, xleft, xright, gram, weight, acc):
    q = (variance[0] + variance[1] + variance[2] + variance[3]) / (V * V)
    m = mask[...]
    for v in range(V):
        weight[v] = m / (variance[v] + q + SKY_VAR)

    acc[...] = jnp.zeros_like(acc)
    step = 4

    def rows_of(i, _):
        lefts, rights = [], []
        for r0 in range(step):
            r = i * step + r0
            at = pl.ds(pl.multiple_of(r * XR, 8), XR)
            x = jnp.concatenate([xleft[at, :], xright[at, :]], axis=1)
            xh, xl = split(x)
            rights.append(jnp.concatenate([xh, xl, jnp.zeros((32, CW), jnp.bfloat16)], axis=0))
            his, los = [], []
            for v in range(V):
                lh, ll = split(x * weight[v, pl.ds(r, 1), :])
                his.append(lh)
                los.append(ll)
            lefts.append(jnp.concatenate(his + los, axis=0))
        left = jnp.concatenate(lefts, axis=1)
        right = jnp.concatenate(rights, axis=1)
        acc[...] += lax.dot_general(
            left, right, (((1,), (1,)), ((), ())), preferred_element_type=jnp.float32
        )
        return 0

    lax.fori_loop(0, RT // step, rows_of, 0)
    high = acc[0 : V * XR, :]
    total = high + pltpu.roll(high, 128 - XR, 1) + acc[V * XR : 2 * V * XR, :]
    lane = lax.broadcasted_iota(jnp.int32, total.shape, 1)
    total = jnp.where(lane < XR, total, 0.0)
    gram[...] = total[0 : 2 * XR, :] + pltpu.roll(total[2 * XR : 4 * XR, :], 64, 1)


def pick(x, index):
    return jnp.take_along_axis(x, index, axis=1, mode="promise_in_bounds")


def final_kernel(
    normalizer, sub, gathered, basis, science, variance, s_above, s_below, w_above, w_below, cols, rows,
    difference, significance, coef, dplane, iplane,
):
    total = gathered[0] + gathered[1] + gathered[2] + gathered[3]
    total = total * (1.0 / normalizer)
    row = lax.broadcasted_iota(jnp.int32, (XR, 128), 0)
    lane = lax.broadcasted_iota(jnp.int32, (XR, 128), 1)
    part = lane // 64
    j = lane - part * 64
    base = part * 64
    halves, scales = [], []
    for half in range(2):
        a = total[half * XR : (half + 1) * XR, :]
        v = half + 2 * part
        e_col = lax.rsqrt(pick(a, base + row) + EPS)
        diag = jnp.sum(jnp.where(row == j, a, 0.0), axis=0, keepdims=True)
        e_row = lax.rsqrt(diag + EPS)
        scaled = a * e_col
        system = jnp.where(j <= NB, scaled * e_row, jnp.where(j == NB + 1 + v, scaled, 0.0))
        system = system + jnp.where(row == j, RIDGE, 0.0)
        halves.append(system)
        scales.append(e_col)
    for k in range(NB + 1):
        for half in range(2):
            a = halves[half]
            pivot_row = jnp.broadcast_to(a[k : k + 1, :], (XR, 128))
            pivot = pick(pivot_row, base + k)
            column = pick(a, base + k)
            column = jnp.where(row == k, pivot - 1.0, column)
            halves[half] = a - column * (pivot_row / pivot)
    for half in range(2):
        v = half + 2 * part
        a = pick(halves[half], base + NB + 1 + v) * scales[half]
        coef[half * XR : (half + 1) * XR, :] = pick(a, lane * 0)
        coef[(half + 2) * XR : (half + 3) * XR, :] = pick(a, lane * 0 + 64)

    me = sub[0]

    def block(b, _):
        at = pl.multiple_of(b * 8, 8)
        grow = lax.broadcasted_iota(jnp.int32, (8, CW), 0) + (b * 8 - SR)
        valid = ((grow >= 0) | (me > 0)) & ((grow < RT) | (me < 3))
        edge_a, edge_b = b < 2, b >= 10
        inner = pl.ds(pl.multiple_of(jnp.clip(b - 2, 0, 7) * 8, 8), 8)
        top = jnp.clip(b, 0, 1) * 8
        low = jnp.clip(b - 10, 0, 1) * 8

        def pull(own, above, below, first, v):
            at_a = pl.ds(pl.multiple_of(first + v * SR + top, 8), 8)
            at_b = pl.ds(pl.multiple_of(first + v * SR + low, 8), 8)
            return jnp.where(edge_a, above[at_a, :], jnp.where(edge_b, below[at_b, :], own[v, inner, :]))

        s = [pull(science, s_above, s_below, TH, v) for v in range(V)]
        w = [pull(variance, w_above, w_below, 0, v) for v in range(V)]
        q = (w[0] + w[1] + w[2] + w[3]) / (V * V)
        acc = [s[v] - jnp.concatenate([coef[v * XR + NB : v * XR + NB + 1, :]] * 2, axis=1) for v in range(V)]
        for k in range(NB):
            c = basis[k, pl.ds(at, 8), :]
            for v in range(V):
                a = coef[v * XR + k : v * XR + k + 1, :]
                acc[v] = acc[v] - c * jnp.concatenate([a, a], axis=1)
        for v in range(V):
            inverse = jnp.where(valid, 1.0 / (w[v] + q + SKY_VAR), 0.0)
            plane = pl.ds(pl.multiple_of(v * CE + b * 8, 8), 8)
            dplane[plane, :] = acc[v] * inverse
            iplane[plane, :] = inverse

        @pl.when((b >= 2) & (b < 10))
        def _():
            for v in range(V):
                difference[v, inner, :] = acc[v]

        return 0

    lax.fori_loop(0, CE // 8, block, 0)
    filtered = []
    for n, plane in enumerate((dplane, iplane)):
        hi, lo = split(plane[...])
        ph, plo = cols[2 * n], cols[2 * n + 1]
        y = mm(hi, ph) + mm(lo, ph) + mm(hi, plo)
        yh, yl = split(y)
        outs = []
        for v in range(V):
            a = slice(v * CE, (v + 1) * CE)
            outs.append(mm(rows[n], jnp.concatenate([yh[a], yh[a], yl[a]], axis=0)))
        filtered.append(outs)
    for v in range(V):
        significance[v] = filtered[0][v] * lax.rsqrt(filtered[1][v])


def shape(*dims, dtype=jnp.float32):
    return jax.ShapeDtypeStruct(dims, dtype)


def params(**more):
    return pltpu.CompilerParams(vmem_limit_bytes=VMEM_LIMIT, **more)


def costs(us):
    return pl.CostEstimate(flops=int(us * 1e8), bytes_accessed=int(us * 2e6), transcendentals=0)


def local(
    pieces_image, pieces_variance, piece_patch, piece_cell,
    stamp_row, stamp_col, stamp_count, warp_offsets,
):
    patches = lax.axis_size("patch")
    subtiles = lax.axis_size("sub")
    me = lax.axis_index("sub")
    up_pairs = [(i + 1, i) for i in range(subtiles - 1)]
    down_pairs = [(i, i + 1) for i in range(subtiles - 1)]
    slots = stamp_row.shape[1]
    dma = pltpu.SemaphoreType.DMA

    half = shape(patches, 2 * CR, CW)
    sent_image, sent_variance, sent_cell = pl.pallas_call(
        pack_kernel,
        out_shape=(half, half, shape(patches, 1, 128, dtype=jnp.int32)),
        in_specs=[SCALARS, SCALARS, WHOLE, WHOLE],
        out_specs=(WHOLE,) * 3,
        scratch_shapes=[pltpu.SMEM((patches,), jnp.int32), pltpu.SMEM((2 * patches,), jnp.int32)],
        compiler_params=params(),
        name="pack",
    )(piece_patch.reshape(-1), piece_cell.reshape(-1), pieces_image[0], pieces_variance[0])

    table = jnp.concatenate(
        [stamp_row, stamp_col, stamp_count, jnp.zeros((1, 127 - 2 * slots), jnp.int32)], axis=1
    )
    got_cell, got_stamps = pl.pallas_call(
        exchange_kernel,
        out_shape=(shape(patches, 1, 128, dtype=jnp.int32), shape(2, 1, 128, dtype=jnp.int32)),
        in_specs=[WHOLE] * 2,
        out_specs=(WHOLE,) * 2,
        scratch_shapes=[dma((patches,)), dma((patches,)), dma((2,)), dma((2,)), dma],
        compiler_params=params(collective_id=0, has_side_effects=True),
        name="exchange",
    )(sent_cell, table)
    sent_image, sent_variance, got_cell, got_stamps = lax.optimization_barrier(
        (sent_image, sent_variance, got_cell, got_stamps)
    )
    got_image = lax.all_to_all(sent_image, "patch", split_axis=0, concat_axis=0, tiled=True)
    got_variance = lax.all_to_all(sent_variance, "patch", split_axis=0, concat_axis=0, tiled=True)

    near = jnp.concatenate([got_stamps[0], table, got_stamps[1]], axis=0)
    shift = jnp.arange(-1, 2)[:, None]
    present = (me + shift >= 0) & (me + shift < subtiles)
    centre_row = (near[:, 0:slots] + shift * RT).reshape(-1)
    centre_col = near[:, slots : 2 * slots].reshape(-1)
    live = (present & (jnp.arange(slots)[None, :] < near[:, 2 * slots : 2 * slots + 1])).reshape(-1)
    row_in = ((jnp.abs(jnp.arange(RT)[None, :] - centre_row[:, None]) <= SH) & live[:, None]).astype(
        jnp.bfloat16
    )
    col_in = (jnp.abs(jnp.arange(CW)[None, :] - centre_col[:, None]) <= SH).astype(jnp.bfloat16)
    mask = jnp.minimum(jnp.dot(row_in.T, col_in, preferred_element_type=jnp.float32), 1.0)

    field = shape(V, RT, CW)
    cells_acc = [pltpu.VMEM((V * NCELL + 1, CR, CW), jnp.float32)]
    rim = shape(HALO, CW)
    science, template, up, down = pl.pallas_call(
        image_kernel,
        out_shape=(field, shape(RT, CW), rim, rim),
        in_specs=[SCALARS, SCALARS, WHOLE],
        out_specs=(WHOLE,) * 4,
        scratch_shapes=cells_acc,
        compiler_params=params(),
        cost_estimate=costs(3),
        name="image",
    )(got_cell, warp_offsets, got_image)
    s_above = lax.ppermute(down, "sub", down_pairs)
    s_below = lax.ppermute(up, "sub", up_pairs)

    row_bands, cols, rows = constants()
    half_rows = shape(RT * XR, 128)
    basis, xleft, xright, token = pl.pallas_call(
        basis_kernel,
        out_shape=(shape(NB, CE, CW), half_rows, half_rows, shape(8, 128)),
        in_specs=[WHOLE] * 5,
        out_specs=(WHOLE,) * 4,
        scratch_shapes=[
            pltpu.VMEM((TE, CW), jnp.float32),
            pltpu.VMEM((NT, TE, CW), jnp.float32),
        ],
        compiler_params=params(),
        cost_estimate=costs(8),
        name="basis",
    )(science, template, s_above, s_below, jnp.asarray(row_bands))

    rim = shape(V * SR, CW)
    variance, up, down = pl.pallas_call(
        variance_kernel,
        out_shape=(field, rim, rim),
        in_specs=[SCALARS, SCALARS, WHOLE, WHOLE],
        out_specs=(WHOLE,) * 3,
        scratch_shapes=cells_acc,
        compiler_params=params(),
        cost_estimate=costs(3),
        name="variance",
    )(got_cell, warp_offsets, got_variance, token)
    w_above = lax.ppermute(down, "sub", down_pairs)
    w_below = lax.ppermute(up, "sub", up_pairs)

    gram = pl.pallas_call(
        gram_kernel,
        out_shape=shape(2 * XR, 128),
        in_specs=[WHOLE] * 4,
        out_specs=WHOLE,
        scratch_shapes=[
            pltpu.VMEM((V, RT, CW), jnp.float32),
            pltpu.VMEM((2 * V * XR, 128), jnp.float32),
        ],
        compiler_params=params(),
        cost_estimate=costs(7),
        name="gram",
    )(variance, mask, xleft, xright)
    gathered = pl.pallas_call(
        gather_kernel,
        out_shape=shape(subtiles, 2 * XR, 128),
        in_specs=[WHOLE],
        out_specs=WHOLE,
        scratch_shapes=[dma((subtiles - 1,)), dma((subtiles - 1,)), dma],
        compiler_params=params(collective_id=1, has_side_effects=True),
        name="gather",
    )(gram)

    normalizer = float(subtiles * slots * (2 * SH + 1) ** 2)
    difference, significance = pl.pallas_call(
        functools.partial(final_kernel, normalizer),
        out_shape=(field, field),
        in_specs=[SCALARS] + [WHOLE] * 10,
        out_specs=(WHOLE,) * 2,
        scratch_shapes=[
            pltpu.VMEM((V * XR, 128), jnp.float32),
            pltpu.VMEM((V * CE, CW), jnp.float32),
            pltpu.VMEM((V * CE, CW), jnp.float32),
        ],
        compiler_params=params(),
        cost_estimate=costs(10),
        name="final",
    )(
        me.reshape(1).astype(jnp.int32), gathered, basis, science, variance, s_above, s_below,
        w_above, w_below, jnp.asarray(cols), jnp.asarray(rows),
    )
    return (difference[:, None], significance[:, None])


def solution(mesh):
    in_specs = (
        P("sub", "patch", None, None),
        P("sub", "patch", None, None),
        P("sub", "patch", None),
        P("sub", "patch"),
        P("patch", "sub"),
        P("patch", "sub"),
        P("patch", "sub"),
        P(),
    )
    out_specs = (P(None, "patch", "sub", None), P(None, "patch", "sub", None))
    return jax.shard_map(local, mesh=mesh, in_specs=in_specs, out_specs=out_specs, check_vma=False)
```

```python
import functools
import math

import jax
import jax.numpy as jnp
import numpy as np
from jax import lax
from jax.experimental import pallas as pl
from jax.experimental.pallas import tpu as pltpu
from jax.sharding import PartitionSpec as P

V = 4
NCELL = 8
CR = 8
RT = 64
CW = 256
KR = 10
PR = 10
SH = 15
WARP = 4
NB = 40
NP = 32
SIGMAS = (0.75, 1.5, 3.0)
DEGREES = (4, 4, 3)
PSF_SIGMA = 2.0
SKY_VAR = 0.1
RIDGE = 0.5
EPS = 1e-05
MESH = pl.DeviceIdType.MESH

NT = 14
XR = 48
TE = 128
CE = 96
TH = 24
SR = 16
HALO = TH + V * SR
BLOCK = 4 * CR
VMEM_LIMIT = 16 * 1024 * 1024
WHOLE = pl.BlockSpec(memory_space=pltpu.VMEM)
SCALARS = pl.BlockSpec(memory_space=pltpu.SMEM)


def tap_values():
    u = np.arange(-KR, KR + 1).astype(np.float64)
    rows = []
    for sigma, degree in zip(SIGMAS, DEGREES):
        t = u / sigma
        env = np.exp(-0.5 * t * t)
        he = [np.ones_like(t), t]
        for n in range(1, degree):
            he.append(t * he[n] - n * he[n - 1])
        for n in range(degree + 1):
            h = he[n] * env
            rows.append(h / np.sqrt(np.sum(h * h)))
    return np.stack(rows)


def psf_values():
    u = np.arange(-PR, PR + 1).astype(np.float64)
    g = np.exp(-0.5 * (u / PSF_SIGMA) ** 2)
    return g / g.sum()


def split_np(a):
    a = a.astype(np.float32)
    hi = a.astype(jnp.bfloat16)
    lo = (a - hi.astype(np.float32)).astype(jnp.bfloat16)
    return hi, lo


def band(taps, rows, cols, first):
    radius = (len(taps) - 1) // 2
    out = np.zeros((rows, cols))
    for r in range(rows):
        for u in range(-radius, radius + 1):
            c = r + first + u
            if 0 <= c < cols:
                out[r, c] = taps[u + radius]
    return out


def constants():
    taps = tap_values()
    bands = np.concatenate([band(taps[j], CE, TE, SR) for j in range(NT)], axis=0)
    hi, lo = split_np(bands)
    row_bands = np.concatenate([hi, lo], axis=1)
    p = psf_values()
    cols, rows = [], []
    for f in (p, p * p):
        cols += list(split_np(band(f, CW, CW, 0)))
        h, l = split_np(band(f, RT, CE, SR))
        rows.append(np.concatenate([h, l, h], axis=1))
    return row_bands, np.stack(cols), np.stack(rows)


def members_of():
    result, first_tap, first = [], 0, 0
    for degree in DEGREES:
        index = {}
        for i in range(degree + 1):
            for j in range(degree + 1 - i):
                index[(i, j)] = first + len(index)
        result.append((first_tap, degree, index))
        first_tap += degree + 1
        first += len(index)
    return result


def split(x):
    hi = x.astype(jnp.bfloat16)
    return hi, (x - hi.astype(jnp.float32)).astype(jnp.bfloat16)


def mm(a, b):
    return jnp.dot(a, b, preferred_element_type=jnp.float32)


def pack_kernel(patch, cell, image, variance, out_image, out_variance, out_cell, count, slot_cell):
    patches = out_variance.shape[0]
    out_image[...] = jnp.zeros_like(out_image)

    def clear(n, _):
        count[n] = 0
        slot_cell[2 * n] = -1
        slot_cell[2 * n + 1] = -1
        return 0

    lax.fori_loop(0, patches, clear, 0)

    def place(n, _):
        q = patch[n]
        rank = count[q]
        count[q] = rank + 1
        slot_cell[2 * q + rank] = cell[n]
        rows = pl.ds(pl.multiple_of(rank * CR, CR), CR)
        a = image[n]
        for half in range(2):
            at = pl.multiple_of(q * BLOCK + half * 2 * CR + rank * CR, CR)
            out_image[pl.ds(at, CR), :] = a[:, half * 128 : (half + 1) * 128]
        out_variance[q, rows, :] = variance[n]
        return 0

    lax.fori_loop(0, image.shape[0], place, 0)
    lane = lax.broadcasted_iota(jnp.int32, (1, 128), 1)

    def tell(q, _):
        out_cell[q] = jnp.where(lane == 0, slot_cell[2 * q], slot_cell[2 * q + 1])
        return 0

    lax.fori_loop(0, patches, tell, 0)


def stamp_mask(mask, stamps, got_stamps, sub, subtiles, slots):
    row = lax.broadcasted_iota(jnp.int32, (RT, CW), 0)
    col = lax.broadcasted_iota(jnp.int32, (RT, CW), 1)
    flags = [(sub > 0).astype(jnp.int32), 1, (sub < subtiles - 1).astype(jnp.int32)]
    mask[...] = jnp.zeros_like(mask)
    for n, (flag, table) in enumerate(zip(flags, (got_stamps[0], stamps[...], got_stamps[1]))):
        count = table[:, 2 * slots : 2 * slots + 1] * flag
        for k in range(slots):
            near_row = jnp.abs(row - (n - 1) * RT - table[:, k : k + 1]) <= SH
            near_col = jnp.abs(col - table[:, slots + k : slots + k + 1]) <= SH
            mask[...] = jnp.where(near_row & near_col & (count > k), 1.0, mask[...])


def combine_image(cells, warp, got, out, left, right):
    patches = cells.shape[0]
    lane = lax.broadcasted_iota(jnp.int32, (patches, 128), 1)
    table = cells[:, 0, :]
    wide = jnp.concatenate(
        [(table[:, rank : rank + 1] == lane).astype(jnp.float32) for rank in range(2)]
        + [jnp.zeros((128 - 2 * patches, 128), jnp.float32)] * (2 * patches < 128),
        axis=0,
    )
    chosen = jnp.transpose(wide)[0 : V * NCELL, :].astype(jnp.bfloat16)
    for half, ref in enumerate((left, right)):
        for r in range(CR):
            x = jnp.concatenate(
                [
                    got[pl.ds(half * 2 * CR + rank * CR + r, patches, stride=BLOCK), :]
                    for rank in range(2)
                ]
                + [jnp.zeros((128 - 2 * patches, 128), jnp.float32)] * (2 * patches < 128),
                axis=0,
            )
            hi, rest = x.astype(jnp.bfloat16), x
            rest = rest - hi.astype(jnp.float32)
            mid, low = split(rest)
            y = mm(chosen, jnp.concatenate([hi, mid, low], axis=1))
            ref[pl.ds(r, V * NCELL, stride=CR), :] = y[:, 0:128] + y[:, 128:256] + y[:, 256:384]
    col = lax.broadcasted_iota(jnp.int32, (RT, CW), 1)
    for v in range(V):
        rows = slice(v * RT, (v + 1) * RT)
        off = jnp.full((RT, CW), warp[v], jnp.int32)
        a = pltpu.roll(jnp.concatenate([left[rows, :], right[rows, :]], axis=1), WARP, 1)
        for bit in range(4):
            a = jnp.where((off & (1 << bit)) != 0, pltpu.roll(a, CW - (1 << bit), 1), a)
        source = col + off - WARP
        out[v] = jnp.where((source >= 0) & (source < CW), a, 0.0)


def front_kernel(
    slots, sent_image, sent_variance, cells, stamps, warp, row_bands,
    science, basis, xleft, xright, got_variance, got_cells, got_stamps, above, below, mask,
    got_image, left, right, template, up, down, text, filt,
    send, recv, ring_send, ring_recv, own,
):
    patches = cells.shape[0]
    subtiles = lax.axis_size("sub")
    me, sub = lax.axis_index("patch"), lax.axis_index("sub")
    next_sub, last_sub = lax.rem(sub + 1, subtiles), lax.rem(sub + subtiles - 1, subtiles)
    barrier = pltpu.get_barrier_semaphore()

    def greet(d, _):
        q = lax.rem(me + d, patches)
        pl.semaphore_signal(barrier, inc=1, device_id={"patch": q}, device_id_type=MESH)
        return 0

    lax.fori_loop(1, patches, greet, 0)
    for s in (last_sub, next_sub):
        pl.semaphore_signal(barrier, inc=1, device_id={"sub": s}, device_id_type=MESH)
    pl.semaphore_wait(barrier, patches + 1)

    def block(q):
        return pl.ds(pl.multiple_of(q * BLOCK, BLOCK), BLOCK)

    def ends(n, source, to):
        if n == 0:
            return cells.at[to], got_cells.at[source]
        if n == 1:
            return sent_image.at[block(to), :], got_image.at[block(source), :]
        return sent_variance.at[to], got_variance.at[source]

    def copy(n, d, to, source):
        src, dst = ends(n, source, to)
        return pltpu.make_async_remote_copy(
            src_ref=src, dst_ref=dst, send_sem=send.at[n, d], recv_sem=recv.at[n, d],
            device_id={"patch": to}, device_id_type=MESH,
        )

    def ring(n, src, dst):
        return [
            pltpu.make_async_remote_copy(
                src_ref=s, dst_ref=r, send_sem=ring_send.at[n, k], recv_sem=ring_recv.at[n, k],
                device_id={"sub": to}, device_id_type=MESH,
            )
            for k, (s, r, to) in enumerate(zip(src, dst, (next_sub, last_sub)))
        ]

    def start_first(d, _):
        copy(0, d, lax.rem(me + d, patches), me).start()
        copy(1, d, lax.rem(me + d, patches), me).start()
        return 0

    lax.fori_loop(1, patches, start_first, 0)
    table_ring = ring(0, (stamps, stamps), (got_stamps.at[0], got_stamps.at[1]))
    for c in table_ring:
        c.start()

    def start_last(d, _):
        copy(2, d, lax.rem(me + d, patches), me).start()
        return 0

    lax.fori_loop(1, patches, start_last, 0)
    mine = [pltpu.make_async_copy(*ends(n, me, me), own.at[n]) for n in range(3)]
    for c in mine:
        c.start()
    for c in mine:
        c.wait()

    def wait_first(d, _):
        source = lax.rem(me + patches - d, patches)
        copy(0, d, source, source).wait_recv()
        copy(1, d, source, source).wait_recv()
        return 0

    lax.fori_loop(1, patches, wait_first, 0)
    combine_image(got_cells, warp, got_image, science, left, right)
    template[...] = (science[0] + science[1] + science[2] + science[3]) / V
    up[0:TH, :] = template[0:TH, :]
    down[0:TH, :] = template[RT - TH : RT, :]
    for v in range(V):
        at = TH + v * SR
        up[at : at + SR, :] = science[v, 0:SR, :]
        down[at : at + SR, :] = science[v, RT - SR : RT, :]
    rims = ring(1, (down, up), (above, below))
    for c in rims:
        c.start()
    for c in table_ring:
        c.wait()
    stamp_mask(mask, stamps, got_stamps, sub, subtiles, slots)
    for c in rims:
        c.wait()
    above[...] = above[...] * (sub > 0).astype(jnp.float32)
    below[...] = below[...] * (sub < subtiles - 1).astype(jnp.float32)
    basis_images(science, template, above, below, row_bands, basis, xleft, xright, text, filt)

    def finish(d, _):
        source = lax.rem(me + patches - d, patches)
        for n in range(3):
            copy(n, d, lax.rem(me + d, patches), me).wait_send()
        copy(2, d, source, source).wait_recv()
        return 0

    lax.fori_loop(1, patches, finish, 0)


def gather_kernel(part, gathered, send, recv, own):
    subtiles = gathered.shape[0]
    sub = lax.axis_index("sub")
    peers = [lax.rem(sub + d, subtiles) for d in range(1, subtiles)]
    barrier = pltpu.get_barrier_semaphore()
    for s in peers:
        pl.semaphore_signal(barrier, inc=1, device_id={"sub": s}, device_id_type=MESH)
    pl.semaphore_wait(barrier, subtiles - 1)
    copies = [
        pltpu.make_async_remote_copy(
            src_ref=part, dst_ref=gathered.at[sub], send_sem=send.at[n], recv_sem=recv.at[n],
            device_id={"sub": s}, device_id_type=MESH,
        )
        for n, s in enumerate(peers)
    ]
    for copy in copies:
        copy.start()
    mine = pltpu.make_async_copy(part, gathered.at[sub], own)
    mine.start()
    mine.wait()
    for n, copy in enumerate(copies):
        copy.wait_send()
        source = lax.rem(sub + subtiles - 1 - n, subtiles)
        pltpu.make_async_remote_copy(
            src_ref=part, dst_ref=gathered.at[source], send_sem=send.at[n], recv_sem=recv.at[n],
            device_id={"sub": source}, device_id_type=MESH,
        ).wait_recv()


def combine(cells, warp, got, out, acc):
    acc[...] = jnp.zeros_like(acc)

    def add(q, _):
        for rank in range(2):
            c = cells[q, 0, rank]
            c = jnp.where(c < 0, V * NCELL, c)
            acc[c] += got[q, rank * CR : (rank + 1) * CR, :]
        return 0

    lax.fori_loop(0, got.shape[0], add, 0)
    col = lax.broadcasted_iota(jnp.int32, (CR, CW), 1)
    for v in range(V):
        off = warp[v]
        turn = jnp.where(off <= WARP, WARP - off, CW + WARP - off)
        source = col + (off - WARP)
        inside = (source >= 0) & (source < CW)
        for c in range(NCELL):
            a = acc[v * NCELL + c]
            out[v, c * CR : (c + 1) * CR, :] = jnp.where(inside, pltpu.roll(a, turn, 1), 0.0)


def variance_kernel(cells, warp, got, variance, up, down, acc):
    combine(cells, warp, got, variance, acc)
    for v in range(V):
        up[v * SR : (v + 1) * SR, :] = variance[v, 0:SR, :]
        down[v * SR : (v + 1) * SR, :] = variance[v, RT - SR : RT, :]


def basis_images(
    science, template, above, below, row_bands, basis, xleft, xright, text, filt,
):
    taps = tap_values()

    def put(k, image):
        at = pl.ds(k, RT, stride=XR)
        xleft[at, :] = image[:, 0:128]
        xright[at, :] = image[:, 128:CW]

    zero8 = jnp.zeros((8, CW), jnp.float32)
    text[0:8, :] = zero8
    text[8:32, :] = above[0:TH, :]
    text[32:96, :] = template[...]
    text[96:120, :] = below[0:TH, :]
    text[120:128, :] = zero8
    col = lax.broadcasted_iota(jnp.int32, (8, CW), 1)

    def columns(i, _):
        rows = pl.ds(pl.multiple_of(i * 8, 8), 8)
        t = text[rows, :]
        sums = [None] * NT
        for u in range(0, KR + 1):
            if u:
                plus = jnp.where(col < CW - u, pltpu.roll(t, CW - u, 1), 0.0)
                minus = jnp.where(col >= u, pltpu.roll(t, u, 1), 0.0)
                even, odd = plus + minus, plus - minus
            first = 0
            for degree in DEGREES:
                for n in range(degree + 1):
                    j = first + n
                    h = float(np.float32(taps[j, KR + u]))
                    if u == 0:
                        sums[j] = t * h if n % 2 == 0 else None
                    else:
                        term = (even if n % 2 == 0 else odd) * h
                        sums[j] = term if sums[j] is None else sums[j] + term
                first += degree + 1
        for j in range(NT):
            filt[j, rows, :] = sums[j]
        return 0

    lax.fori_loop(0, TE // 8, columns, 0)

    for first_tap, degree, index in members_of():
        for j in range(degree + 1):
            count = degree + 1 - j
            lhs = row_bands[first_tap * CE : (first_tap + count) * CE, :]
            fh, fl = split(filt[first_tap + j])
            y = mm(lhs, jnp.concatenate([fh, fh], axis=0)) + mm(lhs[:, 0:TE], fl)
            for i in range(count):
                k = index[(i, j)]
                image = y[i * CE : (i + 1) * CE, :]
                basis[k] = image
                put(k, image[SR : SR + RT, :])
    put(NB, jnp.ones((RT, CW), jnp.float32))
    for v in range(V):
        put(NB + 1 + v, science[v])
    for n in range(NB + 1 + V, XR):
        put(n, jnp.zeros((RT, CW), jnp.float32))


def gram_kernel(variance, mask, xleft, xright, gram, weight, acc):
    q = (variance[0] + variance[1] + variance[2] + variance[3]) / (V * V)
    m = mask[...]
    for v in range(V):
        weight[v] = m / (variance[v] + q + SKY_VAR)

    acc[...] = jnp.zeros_like(acc)
    step = 4

    def rows_of(i, _):
        lefts, rights = [], []
        for r0 in range(step):
            r = i * step + r0
            at = pl.ds(pl.multiple_of(r * XR, 8), XR)
            x = jnp.concatenate([xleft[at, :], xright[at, :]], axis=1)
            xh, xl = split(x)
            rights.append(jnp.concatenate([xh, xl, jnp.zeros((32, CW), jnp.bfloat16)], axis=0))
            his, los = [], []
            for v in range(V):
                lh, ll = split(x * weight[v, pl.ds(r, 1), :])
                his.append(lh)
                los.append(ll)
            lefts.append(jnp.concatenate(his + los, axis=0))
        left = jnp.concatenate(lefts, axis=1)
        right = jnp.concatenate(rights, axis=1)
        acc[...] += lax.dot_general(
            left, right, (((1,), (1,)), ((), ())), preferred_element_type=jnp.float32
        )
        return 0

    lax.fori_loop(0, RT // step, rows_of, 0)
    high = acc[0 : V * XR, :]
    total = high + pltpu.roll(high, 128 - XR, 1) + acc[V * XR : 2 * V * XR, :]
    lane = lax.broadcasted_iota(jnp.int32, total.shape, 1)
    total = jnp.where(lane < XR, total, 0.0)
    gram[...] = total[0 : 2 * XR, :] + pltpu.roll(total[2 * XR : 4 * XR, :], 64, 1)


def pick(x, index):
    return jnp.take_along_axis(x, index, axis=1, mode="promise_in_bounds")


def final_kernel(
    normalizer, sub, gathered, basis, science, variance, s_above, s_below, w_above, w_below, cols, rows,
    difference, significance, coef, dplane, iplane,
):
    total = gathered[0] + gathered[1] + gathered[2] + gathered[3]
    total = total * (1.0 / normalizer)
    row = lax.broadcasted_iota(jnp.int32, (XR, 128), 0)
    lane = lax.broadcasted_iota(jnp.int32, (XR, 128), 1)
    part = lane // 64
    j = lane - part * 64
    base = part * 64
    halves, scales = [], []
    for half in range(2):
        a = total[half * XR : (half + 1) * XR, :]
        v = half + 2 * part
        e_col = lax.rsqrt(pick(a, base + row) + EPS)
        diag = jnp.sum(jnp.where(row == j, a, 0.0), axis=0, keepdims=True)
        e_row = lax.rsqrt(diag + EPS)
        scaled = a * e_col
        system = jnp.where(j <= NB, scaled * e_row, jnp.where(j == NB + 1 + v, scaled, 0.0))
        system = system + jnp.where(row == j, RIDGE, 0.0)
        halves.append(system)
        scales.append(e_col)
    for k in range(NB + 1):
        for half in range(2):
            a = halves[half]
            pivot_row = jnp.broadcast_to(a[k : k + 1, :], (XR, 128))
            pivot = pick(pivot_row, base + k)
            column = pick(a, base + k)
            column = jnp.where(row == k, pivot - 1.0, column)
            halves[half] = a - column * (pivot_row / pivot)
    for half in range(2):
        v = half + 2 * part
        a = pick(halves[half], base + NB + 1 + v) * scales[half]
        coef[half * XR : (half + 1) * XR, :] = pick(a, lane * 0)
        coef[(half + 2) * XR : (half + 3) * XR, :] = pick(a, lane * 0 + 64)

    me = sub[0]

    def block(b, _):
        at = pl.multiple_of(b * 8, 8)
        grow = lax.broadcasted_iota(jnp.int32, (8, CW), 0) + (b * 8 - SR)
        valid = ((grow >= 0) | (me > 0)) & ((grow < RT) | (me < 3))
        edge_a, edge_b = b < 2, b >= 10
        inner = pl.ds(pl.multiple_of(jnp.clip(b - 2, 0, 7) * 8, 8), 8)
        top = jnp.clip(b, 0, 1) * 8
        low = jnp.clip(b - 10, 0, 1) * 8

        def pull(own, above, below, first, v):
            at_a = pl.ds(pl.multiple_of(first + v * SR + top, 8), 8)
            at_b = pl.ds(pl.multiple_of(first + v * SR + low, 8), 8)
            return jnp.where(edge_a, above[at_a, :], jnp.where(edge_b, below[at_b, :], own[v, inner, :]))

        s = [pull(science, s_above, s_below, TH, v) for v in range(V)]
        w = [pull(variance, w_above, w_below, 0, v) for v in range(V)]
        q = (w[0] + w[1] + w[2] + w[3]) / (V * V)
        acc = [s[v] - jnp.concatenate([coef[v * XR + NB : v * XR + NB + 1, :]] * 2, axis=1) for v in range(V)]
        for k in range(NB):
            c = basis[k, pl.ds(at, 8), :]
            for v in range(V):
                a = coef[v * XR + k : v * XR + k + 1, :]
                acc[v] = acc[v] - c * jnp.concatenate([a, a], axis=1)
        for v in range(V):
            inverse = jnp.where(valid, 1.0 / (w[v] + q + SKY_VAR), 0.0)
            plane = pl.ds(pl.multiple_of(v * CE + b * 8, 8), 8)
            dplane[plane, :] = acc[v] * inverse
            iplane[plane, :] = inverse

        @pl.when((b >= 2) & (b < 10))
        def _():
            for v in range(V):
                difference[v, inner, :] = acc[v]

        return 0

    lax.fori_loop(0, CE // 8, block, 0)
    filtered = []
    for n, plane in enumerate((dplane, iplane)):
        hi, lo = split(plane[...])
        ph, plo = cols[2 * n], cols[2 * n + 1]
        y = mm(hi, ph) + mm(lo, ph) + mm(hi, plo)
        yh, yl = split(y)
        outs = []
        for v in range(V):
            a = slice(v * CE, (v + 1) * CE)
            outs.append(mm(rows[n], jnp.concatenate([yh[a], yh[a], yl[a]], axis=0)))
        filtered.append(outs)
    for v in range(V):
        significance[v] = filtered[0][v] * lax.rsqrt(filtered[1][v])


def shape(*dims, dtype=jnp.float32):
    return jax.ShapeDtypeStruct(dims, dtype)


def params(**more):
    return pltpu.CompilerParams(vmem_limit_bytes=VMEM_LIMIT, **more)


def costs(us):
    return pl.CostEstimate(flops=int(us * 1e8), bytes_accessed=int(us * 2e6), transcendentals=0)


def local(
    pieces_image, pieces_variance, piece_patch, piece_cell,
    stamp_row, stamp_col, stamp_count, warp_offsets,
):
    patches = lax.axis_size("patch")
    subtiles = lax.axis_size("sub")
    me = lax.axis_index("sub")
    up_pairs = [(i + 1, i) for i in range(subtiles - 1)]
    down_pairs = [(i, i + 1) for i in range(subtiles - 1)]
    slots = stamp_row.shape[1]
    dma = pltpu.SemaphoreType.DMA

    half = shape(patches, 2 * CR, CW)
    cell_rows = shape(patches, 1, 128, dtype=jnp.int32)
    sent_image, sent_variance, sent_cell = pl.pallas_call(
        pack_kernel,
        out_shape=(shape(patches * BLOCK, 128), half, cell_rows),
        in_specs=[SCALARS, SCALARS, WHOLE, WHOLE],
        out_specs=(WHOLE,) * 3,
        scratch_shapes=[pltpu.SMEM((patches,), jnp.int32), pltpu.SMEM((2 * patches,), jnp.int32)],
        compiler_params=params(),
        name="pack",
    )(piece_patch.reshape(-1), piece_cell.reshape(-1), pieces_image[0], pieces_variance[0])

    table = jnp.concatenate(
        [stamp_row, stamp_col, stamp_count, jnp.zeros((1, 127 - 2 * slots), jnp.int32)], axis=1
    )
    row_bands, cols, rows = constants()
    field = shape(V, RT, CW)
    rim = shape(HALO, CW)
    half_rows = shape(RT * XR, 128)
    vmem = pltpu.VMEM
    science, basis, xleft, xright, got_variance, got_cell, _, s_above, s_below, mask = pl.pallas_call(
        functools.partial(front_kernel, slots),
        out_shape=(
            field, shape(NB, CE, CW), half_rows, half_rows, half, cell_rows,
            shape(2, 1, 128, dtype=jnp.int32), rim, rim, shape(RT, CW),
        ),
        in_specs=[WHOLE] * 4 + [SCALARS, WHOLE],
        out_specs=(WHOLE,) * 10,
        scratch_shapes=[
            vmem((patches * BLOCK, 128), jnp.float32),
            vmem((V * RT, 128), jnp.float32),
            vmem((V * RT, 128), jnp.float32),
            vmem((RT, CW), jnp.float32),
            vmem((HALO, CW), jnp.float32),
            vmem((HALO, CW), jnp.float32),
            vmem((TE, CW), jnp.float32),
            vmem((NT, TE, CW), jnp.float32),
            dma((3, patches)), dma((3, patches)), dma((2, 2)), dma((2, 2)), dma((3,)),
        ],
        compiler_params=pltpu.CompilerParams(
            vmem_limit_bytes=24 * 1024 * 1024, collective_id=0, has_side_effects=True
        ),
        name="front",
    )(sent_image, sent_variance, sent_cell, table, warp_offsets, jnp.asarray(row_bands))

    rim = shape(V * SR, CW)
    variance, up, down = pl.pallas_call(
        variance_kernel,
        out_shape=(field, rim, rim),
        in_specs=[SCALARS, SCALARS, WHOLE],
        out_specs=(WHOLE,) * 3,
        scratch_shapes=[pltpu.VMEM((V * NCELL + 1, CR, CW), jnp.float32)],
        compiler_params=params(),
        cost_estimate=costs(3),
        name="variance",
    )(got_cell, warp_offsets, got_variance)
    w_above = lax.ppermute(down, "sub", down_pairs)
    w_below = lax.ppermute(up, "sub", up_pairs)

    gram = pl.pallas_call(
        gram_kernel,
        out_shape=shape(2 * XR, 128),
        in_specs=[WHOLE] * 4,
        out_specs=WHOLE,
        scratch_shapes=[
            pltpu.VMEM((V, RT, CW), jnp.float32),
            pltpu.VMEM((2 * V * XR, 128), jnp.float32),
        ],
        compiler_params=params(),
        cost_estimate=costs(7),
        name="gram",
    )(variance, mask, xleft, xright)
    gathered = pl.pallas_call(
        gather_kernel,
        out_shape=shape(subtiles, 2 * XR, 128),
        in_specs=[WHOLE],
        out_specs=WHOLE,
        scratch_shapes=[dma((subtiles - 1,)), dma((subtiles - 1,)), dma],
        compiler_params=params(collective_id=1, has_side_effects=True),
        name="gather",
    )(gram)

    normalizer = float(subtiles * slots * (2 * SH + 1) ** 2)
    difference, significance = pl.pallas_call(
        functools.partial(final_kernel, normalizer),
        out_shape=(field, field),
        in_specs=[SCALARS] + [WHOLE] * 10,
        out_specs=(WHOLE,) * 2,
        scratch_shapes=[
            pltpu.VMEM((V * XR, 128), jnp.float32),
            pltpu.VMEM((V * CE, CW), jnp.float32),
            pltpu.VMEM((V * CE, CW), jnp.float32),
        ],
        compiler_params=params(),
        cost_estimate=costs(10),
        name="final",
    )(
        me.reshape(1).astype(jnp.int32), gathered, basis, science, variance, s_above, s_below,
        w_above, w_below, jnp.asarray(cols), jnp.asarray(rows),
    )
    return (difference[:, None], significance[:, None])


def solution(mesh):
    in_specs = (
        P("sub", "patch", None, None),
        P("sub", "patch", None, None),
        P("sub", "patch", None),
        P("sub", "patch"),
        P("patch", "sub"),
        P("patch", "sub"),
        P("patch", "sub"),
        P(),
    )
    out_specs = (P(None, "patch", "sub", None), P(None, "patch", "sub", None))
    return jax.shard_map(local, mesh=mesh, in_specs=in_specs, out_specs=out_specs, check_vma=False)
```

```python
import functools
import math

import jax
import jax.numpy as jnp
import numpy as np
from jax import lax
from jax.experimental import pallas as pl
from jax.experimental.pallas import tpu as pltpu
from jax.sharding import PartitionSpec as P

V = 4
NCELL = 8
CR = 8
RT = 64
CW = 256
KR = 10
PR = 10
SH = 15
WARP = 4
NB = 40
NP = 32
SIGMAS = (0.75, 1.5, 3.0)
DEGREES = (4, 4, 3)
PSF_SIGMA = 2.0
SKY_VAR = 0.1
RIDGE = 0.5
EPS = 1e-05
MESH = pl.DeviceIdType.MESH

NT = 14
XR = 48
TE = 128
CE = 96
TH = 24
SR = 16
HALO = TH + V * SR
BLOCK = 4 * CR
NS = 12
OFFSETS = 2 * NS + 1
VMEM_LIMIT = 16 * 1024 * 1024
WHOLE = pl.BlockSpec(memory_space=pltpu.VMEM)
SCALARS = pl.BlockSpec(memory_space=pltpu.SMEM)


def tap_values():
    u = np.arange(-KR, KR + 1).astype(np.float64)
    rows = []
    for sigma, degree in zip(SIGMAS, DEGREES):
        t = u / sigma
        env = np.exp(-0.5 * t * t)
        he = [np.ones_like(t), t]
        for n in range(1, degree):
            he.append(t * he[n] - n * he[n - 1])
        for n in range(degree + 1):
            h = he[n] * env
            rows.append(h / np.sqrt(np.sum(h * h)))
    return np.stack(rows)


def psf_values():
    u = np.arange(-PR, PR + 1).astype(np.float64)
    g = np.exp(-0.5 * (u / PSF_SIGMA) ** 2)
    return g / g.sum()


def split_np(a):
    a = a.astype(np.float32)
    hi = a.astype(jnp.bfloat16)
    lo = (a - hi.astype(np.float32)).astype(jnp.bfloat16)
    return hi, lo


def band(taps, rows, cols, first):
    radius = (len(taps) - 1) // 2
    out = np.zeros((rows, cols))
    for r in range(rows):
        for u in range(-radius, radius + 1):
            c = r + first + u
            if 0 <= c < cols:
                out[r, c] = taps[u + radius]
    return out


def constants():
    taps = tap_values()
    bands = np.concatenate([band(taps[j], CE, TE, SR) for j in range(NT)], axis=0)
    hi, lo = split_np(bands)
    row_bands = np.concatenate([hi, lo], axis=1)
    p = psf_values()
    cols, rows = [], []
    for f in (p, p * p):
        cols += list(split_np(band(f, CW, CW, 0)))
        h, l = split_np(band(f, RT, CE, SR))
        rows.append(np.concatenate([h, l, h], axis=1))
    return row_bands, np.stack(cols), np.stack(rows)


def members_of():
    result, first_tap, first = [], 0, 0
    for degree in DEGREES:
        index = {}
        for i in range(degree + 1):
            for j in range(degree + 1 - i):
                index[(i, j)] = first + len(index)
        result.append((first_tap, degree, index))
        first_tap += degree + 1
        first += len(index)
    return result


def split(x):
    hi = x.astype(jnp.bfloat16)
    return hi, (x - hi.astype(jnp.float32)).astype(jnp.bfloat16)


def mm(a, b):
    return jnp.dot(a, b, preferred_element_type=jnp.float32)


def pack_kernel(
    patch, cell, image, variance, row, col, warp, live,
    out_image, out_variance, out_cell, table,
    image_in, variance_in, patch_in, cell_in, row_in, col_in, warp_in,
    count, slot_cell, sems,
):
    patches = out_cell.shape[0]
    slots = row.shape[1]
    pairs = (
        (patch, patch_in), (cell, cell_in), (image.at[0], image_in), (variance.at[0], variance_in),
        (row, row_in), (col, col_in), (warp, warp_in),
    )
    copies = [pltpu.make_async_copy(x, y, sems.at[n]) for n, (x, y) in enumerate(pairs)]
    for c in copies:
        c.start()
    out_image[...] = jnp.zeros_like(out_image)
    out_variance[...] = jnp.zeros_like(out_variance)

    def clear(n, _):
        count[n] = 0
        slot_cell[2 * n] = -1
        slot_cell[2 * n + 1] = -1
        return 0

    lax.fori_loop(0, patches, clear, 0)
    for c in copies:
        c.wait()

    def place(n, _):
        q = patch_in[n]
        rank = count[q]
        count[q] = rank + 1
        slot_cell[2 * q + rank] = cell_in[n]
        for x, y in ((image_in, out_image), (variance_in, out_variance)):
            a = x[n]
            for half in range(2):
                at = pl.multiple_of(q * BLOCK + half * 2 * CR + rank * CR, CR)
                y[pl.ds(at, CR), :] = a[:, half * 128 : (half + 1) * 128]
        return 0

    lax.fori_loop(0, image_in.shape[0], place, 0)
    lane = lax.broadcasted_iota(jnp.int32, (1, 128), 1)

    def tell(q, _):
        out_cell[q] = jnp.where(lane == 0, slot_cell[2 * q], slot_cell[2 * q + 1])
        return 0

    lax.fori_loop(0, patches, tell, 0)
    values = [row_in[0, n] for n in range(slots)] + [col_in[0, n] for n in range(slots)]
    values += [live[0, 0]] + [warp_in[v] for v in range(V)]
    line = jnp.zeros((1, 128), jnp.int32)
    for n, value in enumerate(values):
        line = jnp.where(lane == n, value, line)
    table[...] = line


def stamp_mask(mask, stamps, got_stamps, sub, subtiles, slots):
    row = lax.broadcasted_iota(jnp.int32, (RT, CW), 0)
    col = lax.broadcasted_iota(jnp.int32, (RT, CW), 1)
    flags = [(sub > 0).astype(jnp.int32), 1, (sub < subtiles - 1).astype(jnp.int32)]
    mask[...] = jnp.zeros_like(mask)
    for n, (flag, table) in enumerate(zip(flags, (got_stamps[0], stamps[...], got_stamps[1]))):
        count = table[:, 2 * slots : 2 * slots + 1] * flag
        for k in range(slots):
            near_row = jnp.abs(row - (n - 1) * RT - table[:, k : k + 1]) <= SH
            near_col = jnp.abs(col - table[:, slots + k : slots + k + 1]) <= SH
            mask[...] = jnp.where(near_row & near_col & (count > k), 1.0, mask[...])


def choose(cells):
    patches = cells.shape[0]
    lane = lax.broadcasted_iota(jnp.int32, (patches, 128), 1)
    table = cells[:, 0, :]
    wide = jnp.concatenate(
        [(table[:, rank : rank + 1] == lane).astype(jnp.float32) for rank in range(2)]
        + [jnp.zeros((128 - 2 * patches, 128), jnp.float32)] * (2 * patches < 128),
        axis=0,
    )
    return jnp.transpose(wide)[0 : V * NCELL, :].astype(jnp.bfloat16)


def combine(cells, table, got, out, left, right):
    patches = cells.shape[0]
    chosen = choose(cells)
    for half, ref in enumerate((left, right)):
        for r in range(CR):
            x = jnp.concatenate(
                [
                    got[pl.ds(half * 2 * CR + rank * CR + r, patches, stride=BLOCK), :]
                    for rank in range(2)
                ]
                + [jnp.zeros((128 - 2 * patches, 128), jnp.float32)] * (2 * patches < 128),
                axis=0,
            )
            hi = x.astype(jnp.bfloat16)
            mid, low = split(x - hi.astype(jnp.float32))
            y = mm(chosen, jnp.concatenate([hi, mid, low], axis=1))
            ref[pl.ds(r, V * NCELL, stride=CR), :] = y[:, 0:128] + y[:, 128:256] + y[:, 256:384]
    col = lax.broadcasted_iota(jnp.int32, (RT, CW), 1)
    for v in range(V):
        rows = slice(v * RT, (v + 1) * RT)
        off = jnp.broadcast_to(table[:, OFFSETS + v : OFFSETS + v + 1], (RT, CW))
        a = pltpu.roll(jnp.concatenate([left[rows, :], right[rows, :]], axis=1), WARP, 1)
        for bit in range(4):
            a = jnp.where((off & (1 << bit)) != 0, pltpu.roll(a, CW - (1 << bit), 1), a)
        source = col + off - WARP
        out[v, SR : SR + RT, :] = jnp.where((source >= 0) & (source < CW), a, 0.0)


def smooth(plane, col_hi, col_lo, row_taps):
    hi, lo = split(plane)
    yh, yl = split(mm(hi, col_hi) + mm(lo, col_hi) + mm(hi, col_lo))
    outs = []
    for v in range(V):
        a = slice(v * CE, (v + 1) * CE)
        outs.append(mm(row_taps, jnp.concatenate([yh[a], yh[a], yl[a]], axis=0)))
    return outs


def front_kernel(
    slots, sent_image, sent_variance, cells, stamps, row_bands_in, cols_in, rows_in,
    science, inverse, basis, gathered, root,
    got_image, got_variance, got_cells, got_stamps, left, right, template, up, down, above, below,
    text, filt, xleft, xright, mask, wide, wup, wdown, wabove, wbelow, weight, acc, gram,
    row_bands, cols, rows, send, recv, ring_send, ring_recv, all_send, all_recv, own,
):
    patches = cells.shape[0]
    subtiles = gathered.shape[0]
    me, sub = lax.axis_index("patch"), lax.axis_index("sub")
    peers = [lax.rem(sub + d, subtiles) for d in range(1, subtiles)]
    next_sub, last_sub = peers[0], peers[-1]
    has_above = (sub > 0).astype(jnp.float32)
    has_below = (sub < subtiles - 1).astype(jnp.float32)
    barrier = pltpu.get_barrier_semaphore()

    def greet(d, _):
        q = lax.rem(me + d, patches)
        pl.semaphore_signal(barrier, inc=1, device_id={"patch": q}, device_id_type=MESH)
        return 0

    lax.fori_loop(1, patches, greet, 0)
    for s in peers:
        pl.semaphore_signal(barrier, inc=1, device_id={"sub": s}, device_id_type=MESH)
    pl.semaphore_wait(barrier, patches - 1 + subtiles - 1)

    def block(q):
        return pl.ds(pl.multiple_of(q * BLOCK, BLOCK), BLOCK)

    def ends(n, source, to):
        if n == 0:
            return cells.at[to], got_cells.at[source]
        sent, got = (sent_image, got_image) if n == 1 else (sent_variance, got_variance)
        return sent.at[block(to), :], got.at[block(source), :]

    def copy(n, d, to, source):
        src, dst = ends(n, source, to)
        return pltpu.make_async_remote_copy(
            src_ref=src, dst_ref=dst, send_sem=send.at[n, d], recv_sem=recv.at[n, d],
            device_id={"patch": to}, device_id_type=MESH,
        )

    def ring(n, src, dst):
        return [
            pltpu.make_async_remote_copy(
                src_ref=s, dst_ref=r, send_sem=ring_send.at[n, k], recv_sem=ring_recv.at[n, k],
                device_id={"sub": to}, device_id_type=MESH,
            )
            for k, (s, r, to) in enumerate(zip(src, dst, (next_sub, last_sub)))
        ]

    def start_first(d, _):
        copy(0, d, lax.rem(me + d, patches), me).start()
        copy(1, d, lax.rem(me + d, patches), me).start()
        return 0

    lax.fori_loop(1, patches, start_first, 0)
    table_ring = ring(0, (stamps, stamps), (got_stamps.at[0], got_stamps.at[1]))
    for c in table_ring:
        c.start()

    def start_last(d, _):
        copy(2, d, lax.rem(me + d, patches), me).start()
        return 0

    lax.fori_loop(1, patches, start_last, 0)
    mine = [pltpu.make_async_copy(*ends(n, me, me), own.at[n]) for n in range(3)]
    fixed = ((row_bands_in, row_bands), (cols_in, cols), (rows_in, rows))
    mine += [pltpu.make_async_copy(x, y, own.at[3 + n]) for n, (x, y) in enumerate(fixed)]
    for c in mine:
        c.start()
    for c in mine:
        c.wait()
    for c in table_ring:
        c.wait()
    stamp_mask(mask, stamps, got_stamps, sub, subtiles, slots)

    def wait_first(d, _):
        source = lax.rem(me + patches - d, patches)
        copy(0, d, source, source).wait_recv()
        copy(1, d, source, source).wait_recv()
        return 0

    lax.fori_loop(1, patches, wait_first, 0)
    table = stamps[...]
    combine(got_cells, table, got_image, science, left, right)
    inner = slice(SR, SR + RT)
    template[...] = (science[0, inner] + science[1, inner] + science[2, inner] + science[3, inner]) / V
    up[0:TH, :] = template[0:TH, :]
    down[0:TH, :] = template[RT - TH : RT, :]
    for v in range(V):
        at = TH + v * SR
        up[at : at + SR, :] = science[v, SR : 2 * SR, :]
        down[at : at + SR, :] = science[v, RT : RT + SR, :]
    rims = ring(1, (down, up), (above, below))
    for c in rims:
        c.start()
    for c in rims:
        c.wait()
    above[...] = above[...] * has_above
    below[...] = below[...] * has_below
    for v in range(V):
        at = TH + v * SR
        science[v, 0:SR, :] = above[at : at + SR, :]
        science[v, SR + RT : CE, :] = below[at : at + SR, :]
    basis_images(science, template, above, below, row_bands, basis, xleft, xright, text, filt)

    def wait_last(d, _):
        source = lax.rem(me + patches - d, patches)
        copy(2, d, source, source).wait_recv()
        return 0

    lax.fori_loop(1, patches, wait_last, 0)
    combine(got_cells, table, got_variance, wide, left, right)
    for v in range(V):
        at = slice(v * SR, (v + 1) * SR)
        wup[at, :] = wide[v, SR : 2 * SR, :]
        wdown[at, :] = wide[v, RT : RT + SR, :]
    wrims = ring(2, (wdown, wup), (wabove, wbelow))
    for c in wrims:
        c.start()

    def invert(planes):
        q = (planes[0] + planes[1] + planes[2] + planes[3]) / (V * V)
        return [1.0 / (p + q + SKY_VAR) for p in planes]

    m = mask[...]
    for v, inv in enumerate(invert([wide[v, inner, :] for v in range(V)])):
        inverse[v * CE + SR : v * CE + SR + RT, :] = inv
        weight[v] = m * inv
    gram_of(weight, xleft, xright, acc, gram)
    parts = [
        pltpu.make_async_remote_copy(
            src_ref=gram, dst_ref=gathered.at[sub], send_sem=all_send.at[n], recv_sem=all_recv.at[n],
            device_id={"sub": s}, device_id_type=MESH,
        )
        for n, s in enumerate(peers)
    ]
    for c in parts:
        c.start()
    my_part = pltpu.make_async_copy(gram, gathered.at[sub], own.at[6])
    my_part.start()
    for c in wrims:
        c.wait()
    for ref, first, has in ((wabove, 0, has_above), (wbelow, SR + RT, has_below)):
        planes = [ref[v * SR : (v + 1) * SR, :] for v in range(V)]
        for v, inv in enumerate(invert(planes)):
            inverse[v * CE + first : v * CE + first + SR, :] = inv * has
    for v, den in enumerate(smooth(inverse[...], cols[2], cols[3], rows[1])):
        root[v] = lax.rsqrt(den)
    my_part.wait()
    for n, c in enumerate(parts):
        c.wait_send()
        source = peers[subtiles - 2 - n]
        pltpu.make_async_remote_copy(
            src_ref=gram, dst_ref=gathered.at[source], send_sem=all_send.at[n],
            recv_sem=all_recv.at[n], device_id={"sub": source}, device_id_type=MESH,
        ).wait_recv()

    def finish(d, _):
        for n in range(3):
            copy(n, d, lax.rem(me + d, patches), me).wait_send()
        return 0

    lax.fori_loop(1, patches, finish, 0)


def basis_images(
    science, template, above, below, row_bands, basis, xleft, xright, text, filt,
):
    taps = tap_values()

    def put(k, image):
        at = pl.ds(k, RT, stride=XR)
        xleft[at, :] = image[:, 0:128]
        xright[at, :] = image[:, 128:CW]

    zero8 = jnp.zeros((8, CW), jnp.float32)
    text[0:8, :] = zero8
    text[8:32, :] = above[0:TH, :]
    text[32:96, :] = template[...]
    text[96:120, :] = below[0:TH, :]
    text[120:128, :] = zero8
    col = lax.broadcasted_iota(jnp.int32, (8, CW), 1)

    def columns(i, _):
        rows = pl.ds(pl.multiple_of(i * 8, 8), 8)
        t = text[rows, :]
        sums = [None] * NT
        for u in range(0, KR + 1):
            if u:
                plus = jnp.where(col < CW - u, pltpu.roll(t, CW - u, 1), 0.0)
                minus = jnp.where(col >= u, pltpu.roll(t, u, 1), 0.0)
                even, odd = plus + minus, plus - minus
            first = 0
            for degree in DEGREES:
                for n in range(degree + 1):
                    j = first + n
                    h = float(np.float32(taps[j, KR + u]))
                    if u == 0:
                        sums[j] = t * h if n % 2 == 0 else None
                    else:
                        term = (even if n % 2 == 0 else odd) * h
                        sums[j] = term if sums[j] is None else sums[j] + term
                first += degree + 1
        for j in range(NT):
            filt[j, rows, :] = sums[j]
        return 0

    lax.fori_loop(0, TE // 8, columns, 0)

    for first_tap, degree, index in members_of():
        for j in range(degree + 1):
            count = degree + 1 - j
            lhs = row_bands[first_tap * CE : (first_tap + count) * CE, :]
            fh, fl = split(filt[first_tap + j])
            y = mm(lhs, jnp.concatenate([fh, fh], axis=0)) + mm(lhs[:, 0:TE], fl)
            for i in range(count):
                k = index[(i, j)]
                image = y[i * CE : (i + 1) * CE, :]
                basis[k] = image
                put(k, image[SR : SR + RT, :])
    put(NB, jnp.ones((RT, CW), jnp.float32))
    for v in range(V):
        put(NB + 1 + v, science[v, SR : SR + RT, :])
    for n in range(NB + 1 + V, XR):
        put(n, jnp.zeros((RT, CW), jnp.float32))


def gram_of(weight, xleft, xright, acc, gram):
    acc[...] = jnp.zeros_like(acc)
    step = 4

    def rows_of(i, _):
        lefts, rights = [], []
        for r0 in range(step):
            r = i * step + r0
            at = pl.ds(pl.multiple_of(r * XR, 8), XR)
            x = jnp.concatenate([xleft[at, :], xright[at, :]], axis=1)
            xh, xl = split(x)
            rights.append(jnp.concatenate([xh, xl, jnp.zeros((32, CW), jnp.bfloat16)], axis=0))
            his, los = [], []
            for v in range(V):
                lh, ll = split(x * weight[v, pl.ds(r, 1), :])
                his.append(lh)
                los.append(ll)
            lefts.append(jnp.concatenate(his + los, axis=0))
        left = jnp.concatenate(lefts, axis=1)
        right = jnp.concatenate(rights, axis=1)
        acc[...] += lax.dot_general(
            left, right, (((1,), (1,)), ((), ())), preferred_element_type=jnp.float32
        )
        return 0

    lax.fori_loop(0, RT // step, rows_of, 0)
    high = acc[0 : V * XR, :]
    total = high + pltpu.roll(high, 128 - XR, 1) + acc[V * XR : 2 * V * XR, :]
    lane = lax.broadcasted_iota(jnp.int32, total.shape, 1)
    total = jnp.where(lane < XR, total, 0.0)
    gram[...] = total[0 : 2 * XR, :] + pltpu.roll(total[2 * XR : 4 * XR, :], 64, 1)


def pick(x, index):
    return jnp.take_along_axis(x, index, axis=1, mode="promise_in_bounds")


def final_kernel(
    normalizer, gathered, basis, science, inverse, root, cols_in, rows_in,
    difference, significance, coef, dplane, cols, rows, sems,
):
    copies = [
        pltpu.make_async_copy(x, y, sems.at[n])
        for n, (x, y) in enumerate(((cols_in.at[0:2], cols), (rows_in.at[0], rows)))
    ]
    for c in copies:
        c.start()
    total = gathered[0] + gathered[1] + gathered[2] + gathered[3]
    total = total * (1.0 / normalizer)
    row = lax.broadcasted_iota(jnp.int32, (XR, 128), 0)
    lane = lax.broadcasted_iota(jnp.int32, (XR, 128), 1)
    part = lane // 64
    j = lane - part * 64
    base = part * 64
    halves, scales = [], []
    for half in range(2):
        a = total[half * XR : (half + 1) * XR, :]
        v = half + 2 * part
        e_col = lax.rsqrt(pick(a, base + row) + EPS)
        diag = jnp.sum(jnp.where(row == j, a, 0.0), axis=0, keepdims=True)
        e_row = lax.rsqrt(diag + EPS)
        scaled = a * e_col
        system = jnp.where(j <= NB, scaled * e_row, jnp.where(j == NB + 1 + v, scaled, 0.0))
        system = system + jnp.where(row == j, RIDGE, 0.0)
        halves.append(system)
        scales.append(e_col)
    for k in range(NB + 1):
        for half in range(2):
            a = halves[half]
            pivot_row = jnp.broadcast_to(a[k : k + 1, :], (XR, 128))
            pivot = pick(pivot_row, base + k)
            column = pick(a, base + k)
            column = jnp.where(row == k, pivot - 1.0, column)
            halves[half] = a - column * (pivot_row / pivot)
    for half in range(2):
        v = half + 2 * part
        a = pick(halves[half], base + NB + 1 + v) * scales[half]
        coef[half * XR : (half + 1) * XR, :] = pick(a, lane * 0)
        coef[(half + 2) * XR : (half + 3) * XR, :] = pick(a, lane * 0 + 64)

    def block(b, _):
        at = pl.ds(pl.multiple_of(b * 8, 8), 8)
        sums = []
        for v in range(V):
            a = coef[v * XR + NB : v * XR + NB + 1, :]
            sums.append(science[v, at, :] - jnp.concatenate([a, a], axis=1))
        for k in range(NB):
            c = basis[k, at, :]
            for v in range(V):
                a = coef[v * XR + k : v * XR + k + 1, :]
                sums[v] = sums[v] - c * jnp.concatenate([a, a], axis=1)
        for v in range(V):
            plane = pl.ds(pl.multiple_of(v * CE + b * 8, 8), 8)
            dplane[plane, :] = sums[v] * inverse[plane, :]

        @pl.when((b >= SR // 8) & (b < (SR + RT) // 8))
        def _():
            inner = pl.ds(pl.multiple_of(b * 8 - SR, 8), 8)
            for v in range(V):
                difference[v, inner, :] = sums[v]

        return 0

    lax.fori_loop(0, CE // 8, block, 0)
    for c in copies:
        c.wait()
    for v, num in enumerate(smooth(dplane[...], cols[0], cols[1], rows[...])):
        significance[v] = num * root[v]


def shape(*dims, dtype=jnp.float32):
    return jax.ShapeDtypeStruct(dims, dtype)


def params(**more):
    return pltpu.CompilerParams(vmem_limit_bytes=VMEM_LIMIT, **more)


def local(
    pieces_image, pieces_variance, piece_patch, piece_cell,
    stamp_row, stamp_col, stamp_count, warp_offsets,
):
    patches = lax.axis_size("patch")
    subtiles = lax.axis_size("sub")
    pieces = pieces_image.shape[1]
    slots = stamp_row.shape[1]
    dma, vmem, smem = pltpu.SemaphoreType.DMA, pltpu.VMEM, pltpu.SMEM
    far = pl.BlockSpec(memory_space=pltpu.HBM)

    def keep(*arrays):
        return [pltpu.with_memory_space_constraint(a, pltpu.HBM) for a in arrays]

    f32, i32, bf16 = jnp.float32, jnp.int32, jnp.bfloat16

    sent_shape = shape(patches * BLOCK, 128)
    sent_image, sent_variance, sent_cell, table = pl.pallas_call(
        pack_kernel,
        out_shape=(
            sent_shape, sent_shape, shape(patches, 1, 128, dtype=i32), shape(1, 128, dtype=i32),
        ),
        in_specs=[far] * 7 + [SCALARS],
        out_specs=(WHOLE,) * 4,
        scratch_shapes=[
            vmem((pieces, CR, CW), f32), vmem((pieces, CR, CW), f32),
            smem((pieces,), i32), smem((pieces,), i32),
            smem((1, slots), i32), smem((1, slots), i32), smem((V,), i32),
            smem((patches,), i32), smem((2 * patches,), i32), dma((7,)),
        ],
        compiler_params=params(),
        name="pack",
    )(
        *keep(
            piece_patch.reshape(-1), piece_cell.reshape(-1), pieces_image, pieces_variance,
            stamp_row, stamp_col, warp_offsets,
        ),
        stamp_count,
    )

    row_bands, cols, rows = keep(*[jnp.asarray(x) for x in constants()])
    rim, small_rim = vmem((HALO, CW), f32), vmem((V * SR, CW), f32)
    field = shape(V, RT, CW)
    science, inverse, basis, gathered, root = pl.pallas_call(
        functools.partial(front_kernel, slots),
        out_shape=(
            shape(V, CE, CW), shape(V * CE, CW), shape(NB, CE, CW), shape(subtiles, 2 * XR, 128), field,
        ),
        in_specs=[WHOLE] * 4 + [far] * 3,
        out_specs=(WHOLE,) * 5,
        scratch_shapes=[
            vmem((patches * BLOCK, 128), f32), vmem((patches * BLOCK, 128), f32),
            vmem((patches, 1, 128), i32), vmem((2, 1, 128), i32),
            vmem((V * RT, 128), f32), vmem((V * RT, 128), f32), vmem((RT, CW), f32),
            rim, rim, rim, rim,
            vmem((TE, CW), f32), vmem((NT, TE, CW), f32),
            vmem((RT * XR, 128), f32), vmem((RT * XR, 128), f32), vmem((RT, CW), f32),
            vmem((V, CE, CW), f32), small_rim, small_rim, small_rim, small_rim,
            vmem((V, RT, CW), f32), vmem((2 * V * XR, 128), f32), vmem((2 * XR, 128), f32),
            vmem(row_bands.shape, bf16), vmem(cols.shape, bf16), vmem(rows.shape, bf16),
            dma((3, patches)), dma((3, patches)), dma((3, 2)), dma((3, 2)),
            dma((subtiles - 1,)), dma((subtiles - 1,)), dma((7,)),
        ],
        compiler_params=pltpu.CompilerParams(
            vmem_limit_bytes=32 * 1024 * 1024, collective_id=0, has_side_effects=True
        ),
        name="front",
    )(sent_image, sent_variance, sent_cell, table, row_bands, cols, rows)

    normalizer = float(subtiles * slots * (2 * SH + 1) ** 2)
    difference, significance = pl.pallas_call(
        functools.partial(final_kernel, normalizer),
        out_shape=(field, field),
        in_specs=[WHOLE] * 5 + [far] * 2,
        out_specs=(WHOLE,) * 2,
        scratch_shapes=[
            vmem((V * XR, 128), f32), vmem((V * CE, CW), f32),
            vmem((2, CW, CW), bf16), vmem(rows.shape[1:], bf16), dma((2,)),
        ],
        compiler_params=params(),
        name="final",
    )(gathered, basis, science, inverse, root, cols, rows)
    return (difference[:, None], significance[:, None])


def solution(mesh):
    in_specs = (
        P("sub", "patch", None, None),
        P("sub", "patch", None, None),
        P("sub", "patch", None),
        P("sub", "patch"),
        P("patch", "sub"),
        P("patch", "sub"),
        P("patch", "sub"),
        P(),
    )
    out_specs = (P(None, "patch", "sub", None), P(None, "patch", "sub", None))
    return jax.shard_map(local, mesh=mesh, in_specs=in_specs, out_specs=out_specs, check_vma=False)
```

```python
import functools
import math

import jax
import jax.numpy as jnp
import numpy as np
from jax import lax
from jax.experimental import pallas as pl
from jax.experimental.pallas import tpu as pltpu
from jax.sharding import PartitionSpec as P

V = 4
NCELL = 8
CR = 8
RT = 64
CW = 256
KR = 10
PR = 10
SH = 15
WARP = 4
NB = 40
NP = 32
SIGMAS = (0.75, 1.5, 3.0)
DEGREES = (4, 4, 3)
PSF_SIGMA = 2.0
SKY_VAR = 0.1
RIDGE = 0.5
EPS = 1e-05
MESH = pl.DeviceIdType.MESH

NT = 14
XR = 48
TE = 128
CE = 96
TH = 24
SR = 16
HALO = TH + V * SR
BLOCK = 4 * CR
RC = CR // 2
PART = 4 * RC
NS = 12
OFFSETS = 2 * NS + 1
VMEM_LIMIT = 16 * 1024 * 1024
WHOLE = pl.BlockSpec(memory_space=pltpu.VMEM)
SCALARS = pl.BlockSpec(memory_space=pltpu.SMEM)


def tap_values():
    u = np.arange(-KR, KR + 1).astype(np.float64)
    rows = []
    for sigma, degree in zip(SIGMAS, DEGREES):
        t = u / sigma
        env = np.exp(-0.5 * t * t)
        he = [np.ones_like(t), t]
        for n in range(1, degree):
            he.append(t * he[n] - n * he[n - 1])
        for n in range(degree + 1):
            h = he[n] * env
            rows.append(h / np.sqrt(np.sum(h * h)))
    return np.stack(rows)


def psf_values():
    u = np.arange(-PR, PR + 1).astype(np.float64)
    g = np.exp(-0.5 * (u / PSF_SIGMA) ** 2)
    return g / g.sum()


def split_np(a):
    a = a.astype(np.float32)
    hi = a.astype(jnp.bfloat16)
    lo = (a - hi.astype(np.float32)).astype(jnp.bfloat16)
    return hi, lo


def band(taps, rows, cols, first):
    radius = (len(taps) - 1) // 2
    out = np.zeros((rows, cols))
    for r in range(rows):
        for u in range(-radius, radius + 1):
            c = r + first + u
            if 0 <= c < cols:
                out[r, c] = taps[u + radius]
    return out


def constants():
    taps = tap_values()
    bands = np.concatenate([band(taps[j], CE, TE, SR) for j in range(NT)], axis=0)
    hi, lo = split_np(bands)
    row_bands = np.concatenate([hi, lo], axis=1)
    p = psf_values()
    cols, rows = [], []
    for f in (p, p * p):
        cols += list(split_np(band(f, CW, CW, 0)))
        h, l = split_np(band(f, RT, CE, SR))
        rows.append(np.concatenate([h, l, h], axis=1))
    return row_bands, np.stack(cols), np.stack(rows)


def members_of():
    result, first_tap, first = [], 0, 0
    for degree in DEGREES:
        index = {}
        for i in range(degree + 1):
            for j in range(degree + 1 - i):
                index[(i, j)] = first + len(index)
        result.append((first_tap, degree, index))
        first_tap += degree + 1
        first += len(index)
    return result


def split(x):
    hi = x.astype(jnp.bfloat16)
    return hi, (x - hi.astype(jnp.float32)).astype(jnp.bfloat16)


def mm(a, b):
    return jnp.dot(a, b, preferred_element_type=jnp.float32)


def pack_kernel(
    patch, cell, image, variance, row, col, warp, live,
    out_image, out_first, out_last, out_cell, table,
    image_in, variance_in, patch_in, cell_in, row_in, col_in, warp_in,
    count, slot_cell, sems,
):
    patches = out_cell.shape[0]
    slots = row.shape[1]
    pairs = (
        (patch, patch_in), (cell, cell_in), (image.at[0], image_in), (variance.at[0], variance_in),
        (row, row_in), (col, col_in), (warp, warp_in),
    )
    copies = [pltpu.make_async_copy(x, y, sems.at[n]) for n, (x, y) in enumerate(pairs)]
    for c in copies:
        c.start()
    out_image[...] = jnp.zeros_like(out_image)
    for ref in (out_first, out_last):
        ref[...] = jnp.zeros_like(ref)

    def clear(n, _):
        count[n] = 0
        slot_cell[2 * n] = -1
        slot_cell[2 * n + 1] = -1
        return 0

    lax.fori_loop(0, patches, clear, 0)
    for c in copies:
        c.wait()

    def place(n, _):
        q = patch_in[n]
        rank = count[q]
        count[q] = rank + 1
        slot_cell[2 * q + rank] = cell_in[n]
        a, b = image_in[n], variance_in[n]
        mine = upper == rank
        for half in range(2):
            lanes = slice(half * 128, (half + 1) * 128)
            at = pl.multiple_of(q * BLOCK + half * 2 * CR + rank * CR, CR)
            out_image[pl.ds(at, CR), :] = a[:, lanes]
            at = pl.ds(pl.multiple_of(q * PART + half * CR, CR), CR)
            for k, y in enumerate((out_first, out_last)):
                rows = b[k * RC : (k + 1) * RC, lanes]
                y[at, :] = jnp.where(mine, jnp.concatenate([rows, rows], axis=0), y[at, :])
        return 0

    upper = lax.broadcasted_iota(jnp.int32, (CR, 128), 0) // RC
    lax.fori_loop(0, image_in.shape[0], place, 0)
    lane = lax.broadcasted_iota(jnp.int32, (1, 128), 1)

    def tell(q, _):
        out_cell[q] = jnp.where(lane == 0, slot_cell[2 * q], slot_cell[2 * q + 1])
        return 0

    lax.fori_loop(0, patches, tell, 0)
    values = [row_in[0, n] for n in range(slots)] + [col_in[0, n] for n in range(slots)]
    values += [live[0, 0]] + [warp_in[v] for v in range(V)]
    line = jnp.zeros((1, 128), jnp.int32)
    for n, value in enumerate(values):
        line = jnp.where(lane == n, value, line)
    table[...] = line


def stamp_mask(mask, stamps, got_stamps, sub, subtiles, slots):
    row = lax.broadcasted_iota(jnp.int32, (RT, CW), 0)
    col = lax.broadcasted_iota(jnp.int32, (RT, CW), 1)
    flags = [(sub > 0).astype(jnp.int32), 1, (sub < subtiles - 1).astype(jnp.int32)]
    mask[...] = jnp.zeros_like(mask)
    for n, (flag, table) in enumerate(zip(flags, (got_stamps[0], stamps[...], got_stamps[1]))):
        count = table[:, 2 * slots : 2 * slots + 1] * flag
        for k in range(slots):
            near_row = jnp.abs(row - (n - 1) * RT - table[:, k : k + 1]) <= SH
            near_col = jnp.abs(col - table[:, slots + k : slots + k + 1]) <= SH
            mask[...] = jnp.where(near_row & near_col & (count > k), 1.0, mask[...])


def choose(cells):
    patches = cells.shape[0]
    lane = lax.broadcasted_iota(jnp.int32, (patches, 128), 1)
    table = cells[:, 0, :]
    wide = jnp.concatenate(
        [(table[:, rank : rank + 1] == lane).astype(jnp.float32) for rank in range(2)]
        + [jnp.zeros((128 - 2 * patches, 128), jnp.float32)] * (2 * patches < 128),
        axis=0,
    )
    return jnp.transpose(wide)[0 : V * NCELL, :].astype(jnp.bfloat16)


def combine(chosen, patches, table, got, rows, put_field, left, right):
    for half, ref in enumerate((left, right)):
        for r in range(rows):
            x = jnp.concatenate(
                [
                    got[pl.ds((half * 2 + rank) * rows + r, patches, stride=4 * rows), :]
                    for rank in range(2)
                ]
                + [jnp.zeros((128 - 2 * patches, 128), jnp.float32)] * (2 * patches < 128),
                axis=0,
            )
            hi = x.astype(jnp.bfloat16)
            mid, low = split(x - hi.astype(jnp.float32))
            y = mm(chosen, jnp.concatenate([hi, mid, low], axis=1))
            ref[pl.ds(r, V * NCELL, stride=rows), :] = y[:, 0:128] + y[:, 128:256] + y[:, 256:384]
    size = NCELL * rows
    col = lax.broadcasted_iota(jnp.int32, (size, CW), 1)
    for v in range(V):
        at = slice(v * size, (v + 1) * size)
        off = jnp.broadcast_to(table[:, OFFSETS + v : OFFSETS + v + 1], (size, CW))
        a = pltpu.roll(jnp.concatenate([left[at, :], right[at, :]], axis=1), WARP, 1)
        for bit in range(4):
            a = jnp.where((off & (1 << bit)) != 0, pltpu.roll(a, CW - (1 << bit), 1), a)
        source = col + off - WARP
        put_field(v, jnp.where((source >= 0) & (source < CW), a, 0.0))


def smooth(plane, col_hi, col_lo, row_taps):
    hi, lo = split(plane)
    yh, yl = split(mm(hi, col_hi) + mm(lo, col_hi) + mm(hi, col_lo))
    outs = []
    for v in range(V):
        a = slice(v * CE, (v + 1) * CE)
        outs.append(mm(row_taps, jnp.concatenate([yh[a], yh[a], yl[a]], axis=0)))
    return outs


def front_kernel(
    slots, sent_image, sent_first, sent_last, cells, stamps, row_bands_in, cols_in, rows_in,
    science, inverse, basis, gathered, root,
    got_image, got_first, got_last, got_cells, got_stamps, left, right, template, up, down, above, below,
    text, filt, xleft, xright, mask, half_mask, wide, wup, wdown, wabove, wbelow, weight, acc, gram,
    row_bands, cols, rows, send, recv, ring_send, ring_recv, all_send, all_recv, own,
):
    patches = cells.shape[0]
    subtiles = gathered.shape[0]
    me, sub = lax.axis_index("patch"), lax.axis_index("sub")
    peers = [lax.rem(sub + d, subtiles) for d in range(1, subtiles)]
    next_sub, last_sub = peers[0], peers[-1]
    has_above = (sub > 0).astype(jnp.float32)
    has_below = (sub < subtiles - 1).astype(jnp.float32)
    barrier = pltpu.get_barrier_semaphore()

    def greet(d, _):
        q = lax.rem(me + d, patches)
        pl.semaphore_signal(barrier, inc=1, device_id={"patch": q}, device_id_type=MESH)
        return 0

    lax.fori_loop(1, patches, greet, 0)
    for s in peers:
        pl.semaphore_signal(barrier, inc=1, device_id={"sub": s}, device_id_type=MESH)
    pl.semaphore_wait(barrier, patches - 1 + subtiles - 1)

    pairs = (
        (cells, got_cells, 1), (sent_image, got_image, BLOCK),
        (sent_first, got_first, PART), (sent_last, got_last, PART),
    )

    def ends(n, to, source):
        src, dst, size = pairs[n]
        src_at = pl.ds(pl.multiple_of(to * size, size), size)
        dst_at = pl.ds(pl.multiple_of(source * size, size), size)
        return src.at[src_at], dst.at[dst_at]

    def start(n, d):
        to = lax.rem(me + d, patches)
        src, dst = ends(n, to, me)
        pltpu.make_async_remote_copy(
            src_ref=src, dst_ref=dst, send_sem=send.at[n], recv_sem=recv.at[n],
            device_id={"patch": to}, device_id_type=MESH,
        ).start()

    def whole(n):
        src, dst, size = pairs[n]
        at = pl.ds(0, (patches - 1) * size)
        return pltpu.make_async_remote_copy(
            src_ref=src.at[at], dst_ref=dst.at[at], send_sem=send.at[n], recv_sem=recv.at[n],
            device_id={"patch": lax.rem(me + 1, patches)}, device_id_type=MESH,
        )

    def ring(n, src, dst):
        return [
            pltpu.make_async_remote_copy(
                src_ref=s, dst_ref=r, send_sem=ring_send.at[n, k], recv_sem=ring_recv.at[n, k],
                device_id={"sub": to}, device_id_type=MESH,
            )
            for k, (s, r, to) in enumerate(zip(src, dst, (next_sub, last_sub)))
        ]

    def start_first(d, _):
        start(0, d)
        start(1, d)
        return 0

    lax.fori_loop(1, patches, start_first, 0)
    table_ring = ring(0, (stamps, stamps), (got_stamps.at[0], got_stamps.at[1]))
    for c in table_ring:
        c.start()

    for n in (2, 3):

        def start_chunk(d, _):
            start(n, d)
            return 0

        lax.fori_loop(1, patches, start_chunk, 0)
    mine = [pltpu.make_async_copy(*ends(n, me, me), own.at[n]) for n in range(4)]
    fixed = ((row_bands_in, row_bands), (cols_in, cols), (rows_in, rows))
    mine += [pltpu.make_async_copy(x, y, own.at[4 + n]) for n, (x, y) in enumerate(fixed)]
    for c in mine:
        c.start()
    for c in mine:
        c.wait()
    for c in table_ring:
        c.wait()
    stamp_mask(mask, stamps, got_stamps, sub, subtiles, slots)

    for c in range(NCELL):
        for k in range(2):
            half_mask[k, c * RC : (c + 1) * RC, :] = mask[c * CR + k * RC : c * CR + (k + 1) * RC, :]
    acc[...] = jnp.zeros_like(acc)
    whole(0).wait_recv()
    whole(1).wait_recv()
    table = stamps[...]
    chosen = choose(got_cells)

    def put_science(v, field):
        science[v, SR : SR + RT, :] = field

    combine(chosen, patches, table, got_image, CR, put_science, left, right)
    inner = slice(SR, SR + RT)
    template[...] = (science[0, inner] + science[1, inner] + science[2, inner] + science[3, inner]) / V
    up[0:TH, :] = template[0:TH, :]
    down[0:TH, :] = template[RT - TH : RT, :]
    for v in range(V):
        at = TH + v * SR
        up[at : at + SR, :] = science[v, SR : 2 * SR, :]
        down[at : at + SR, :] = science[v, RT : RT + SR, :]
    rims = ring(1, (down, up), (above, below))
    for c in rims:
        c.start()
    for c in rims:
        c.wait()
    above[...] = above[...] * has_above
    below[...] = below[...] * has_below
    for v in range(V):
        at = TH + v * SR
        science[v, 0:SR, :] = above[at : at + SR, :]
        science[v, SR + RT : CE, :] = below[at : at + SR, :]
    basis_images(science, template, above, below, row_bands, basis, xleft, xright, text, filt)

    whole(0).wait_send()
    whole(1).wait_send()

    def invert(planes):
        q = (planes[0] + planes[1] + planes[2] + planes[3]) / (V * V)
        return [1.0 / (p + q + SKY_VAR) for p in planes]

    def put_wide(v, field):
        wide[v] = field

    wrims = ring(2, (wdown, wup), (wabove, wbelow))
    for k, got in enumerate((got_first, got_last)):
        whole(2 + k).wait_recv()
        combine(chosen, patches, table, got, RC, put_wide, left, right)
        for v in range(V):
            for c in range(SR // CR):
                at = slice(v * SR + c * CR + k * RC, v * SR + c * CR + (k + 1) * RC)
                low = NCELL - SR // CR + c
                wup[at, :] = wide[v, c * RC : (c + 1) * RC, :]
                wdown[at, :] = wide[v, low * RC : (low + 1) * RC, :]
        if k == 1:
            for c in wrims:
                c.start()
        for v, inv in enumerate(invert([wide[v] for v in range(V)])):
            weight[v] = half_mask[k] * inv
            for c in range(NCELL):
                first = v * CE + SR + c * CR + k * RC
                inverse[first : first + RC, :] = inv[c * RC : (c + 1) * RC, :]
        gram_of(k, weight, xleft, xright, acc)
    gram_total(acc, gram)
    parts = [
        pltpu.make_async_remote_copy(
            src_ref=gram, dst_ref=gathered.at[sub], send_sem=all_send.at[n], recv_sem=all_recv.at[n],
            device_id={"sub": s}, device_id_type=MESH,
        )
        for n, s in enumerate(peers)
    ]
    for c in parts:
        c.start()
    my_part = pltpu.make_async_copy(gram, gathered.at[sub], own.at[7])
    my_part.start()
    for c in wrims:
        c.wait()
    for ref, first, has in ((wabove, 0, has_above), (wbelow, SR + RT, has_below)):
        planes = [ref[v * SR : (v + 1) * SR, :] for v in range(V)]
        for v, inv in enumerate(invert(planes)):
            inverse[v * CE + first : v * CE + first + SR, :] = inv * has
    for v, den in enumerate(smooth(inverse[...], cols[2], cols[3], rows[1])):
        root[v] = lax.rsqrt(den)
    my_part.wait()
    for n, c in enumerate(parts):
        c.wait_send()
        source = peers[subtiles - 2 - n]
        pltpu.make_async_remote_copy(
            src_ref=gram, dst_ref=gathered.at[source], send_sem=all_send.at[n],
            recv_sem=all_recv.at[n], device_id={"sub": source}, device_id_type=MESH,
        ).wait_recv()

    whole(2).wait_send()
    whole(3).wait_send()


def basis_images(
    science, template, above, below, row_bands, basis, xleft, xright, text, filt,
):
    taps = tap_values()

    def put(k, image):
        at = pl.ds(k, RT, stride=XR)
        xleft[at, :] = image[:, 0:128]
        xright[at, :] = image[:, 128:CW]

    zero8 = jnp.zeros((8, CW), jnp.float32)
    text[0:8, :] = zero8
    text[8:32, :] = above[0:TH, :]
    text[32:96, :] = template[...]
    text[96:120, :] = below[0:TH, :]
    text[120:128, :] = zero8
    col = lax.broadcasted_iota(jnp.int32, (8, CW), 1)

    def columns(i, _):
        rows = pl.ds(pl.multiple_of(i * 8, 8), 8)
        t = text[rows, :]
        sums = [None] * NT
        for u in range(0, KR + 1):
            if u:
                plus = jnp.where(col < CW - u, pltpu.roll(t, CW - u, 1), 0.0)
                minus = jnp.where(col >= u, pltpu.roll(t, u, 1), 0.0)
                even, odd = plus + minus, plus - minus
            first = 0
            for degree in DEGREES:
                for n in range(degree + 1):
                    j = first + n
                    h = float(np.float32(taps[j, KR + u]))
                    if u == 0:
                        sums[j] = t * h if n % 2 == 0 else None
                    else:
                        term = (even if n % 2 == 0 else odd) * h
                        sums[j] = term if sums[j] is None else sums[j] + term
                first += degree + 1
        for j in range(NT):
            filt[j, rows, :] = sums[j]
        return 0

    lax.fori_loop(0, TE // 8, columns, 0)

    for first_tap, degree, index in members_of():
        for j in range(degree + 1):
            count = degree + 1 - j
            lhs = row_bands[first_tap * CE : (first_tap + count) * CE, :]
            fh, fl = split(filt[first_tap + j])
            y = mm(lhs, jnp.concatenate([fh, fh], axis=0)) + mm(lhs[:, 0:TE], fl)
            for i in range(count):
                k = index[(i, j)]
                image = y[i * CE : (i + 1) * CE, :]
                basis[k] = image
                put(k, image[SR : SR + RT, :])
    put(NB, jnp.ones((RT, CW), jnp.float32))
    for v in range(V):
        put(NB + 1 + v, science[v, SR : SR + RT, :])
    for n in range(NB + 1 + V, XR):
        put(n, jnp.zeros((RT, CW), jnp.float32))


def gram_of(k, weight, xleft, xright, acc):
    def cell(i, _):
        lefts, rights = [], []
        for r0 in range(RC):
            r = i * CR + k * RC + r0
            at = pl.ds(pl.multiple_of(r * XR, 8), XR)
            x = jnp.concatenate([xleft[at, :], xright[at, :]], axis=1)
            xh, xl = split(x)
            rights.append(jnp.concatenate([xh, xl, jnp.zeros((32, CW), jnp.bfloat16)], axis=0))
            his, los = [], []
            for v in range(V):
                lh, ll = split(x * weight[v, pl.ds(i * RC + r0, 1), :])
                his.append(lh)
                los.append(ll)
            lefts.append(jnp.concatenate(his + los, axis=0))
        acc[...] += lax.dot_general(
            jnp.concatenate(lefts, axis=1), jnp.concatenate(rights, axis=1),
            (((1,), (1,)), ((), ())), preferred_element_type=jnp.float32,
        )
        return 0

    lax.fori_loop(0, NCELL, cell, 0)


def gram_total(acc, gram):
    high = acc[0 : V * XR, :]
    total = high + pltpu.roll(high, 128 - XR, 1) + acc[V * XR : 2 * V * XR, :]
    lane = lax.broadcasted_iota(jnp.int32, total.shape, 1)
    total = jnp.where(lane < XR, total, 0.0)
    gram[...] = total[0 : 2 * XR, :] + pltpu.roll(total[2 * XR : 4 * XR, :], 64, 1)


def pick(x, index):
    return jnp.take_along_axis(x, index, axis=1, mode="promise_in_bounds")


def final_kernel(
    normalizer, gathered, basis, science, inverse, root, cols_in, rows_in,
    difference, significance, coef, dplane, cols, rows, sems,
):
    copies = [
        pltpu.make_async_copy(x, y, sems.at[n])
        for n, (x, y) in enumerate(((cols_in.at[0:2], cols), (rows_in.at[0], rows)))
    ]
    for c in copies:
        c.start()
    total = gathered[0] + gathered[1] + gathered[2] + gathered[3]
    total = total * (1.0 / normalizer)
    row = lax.broadcasted_iota(jnp.int32, (XR, 128), 0)
    lane = lax.broadcasted_iota(jnp.int32, (XR, 128), 1)
    part = lane // 64
    j = lane - part * 64
    base = part * 64
    halves, scales = [], []
    for half in range(2):
        a = total[half * XR : (half + 1) * XR, :]
        v = half + 2 * part
        e_col = lax.rsqrt(pick(a, base + row) + EPS)
        diag = jnp.sum(jnp.where(row == j, a, 0.0), axis=0, keepdims=True)
        e_row = lax.rsqrt(diag + EPS)
        scaled = a * e_col
        system = jnp.where(j <= NB, scaled * e_row, jnp.where(j == NB + 1 + v, scaled, 0.0))
        system = system + jnp.where(row == j, RIDGE, 0.0)
        halves.append(system)
        scales.append(e_col)
    for k in range(NB + 1):
        for half in range(2):
            a = halves[half]
            pivot_row = jnp.broadcast_to(a[k : k + 1, :], (XR, 128))
            pivot = pick(pivot_row, base + k)
            column = pick(a, base + k)
            column = jnp.where(row == k, pivot - 1.0, column)
            halves[half] = a - column * (pivot_row / pivot)
    for half in range(2):
        v = half + 2 * part
        a = pick(halves[half], base + NB + 1 + v) * scales[half]
        coef[half * XR : (half + 1) * XR, :] = pick(a, lane * 0)
        coef[(half + 2) * XR : (half + 3) * XR, :] = pick(a, lane * 0 + 64)

    def block(b, _):
        at = pl.ds(pl.multiple_of(b * 8, 8), 8)
        sums = []
        for v in range(V):
            a = coef[v * XR + NB : v * XR + NB + 1, :]
            sums.append(science[v, at, :] - jnp.concatenate([a, a], axis=1))
        for k in range(NB):
            c = basis[k, at, :]
            for v in range(V):
                a = coef[v * XR + k : v * XR + k + 1, :]
                sums[v] = sums[v] - c * jnp.concatenate([a, a], axis=1)
        for v in range(V):
            plane = pl.ds(pl.multiple_of(v * CE + b * 8, 8), 8)
            dplane[plane, :] = sums[v] * inverse[plane, :]

        @pl.when((b >= SR // 8) & (b < (SR + RT) // 8))
        def _():
            inner = pl.ds(pl.multiple_of(b * 8 - SR, 8), 8)
            for v in range(V):
                difference[v, inner, :] = sums[v]

        return 0

    lax.fori_loop(0, CE // 8, block, 0)
    for c in copies:
        c.wait()
    for v, num in enumerate(smooth(dplane[...], cols[0], cols[1], rows[...])):
        significance[v] = num * root[v]


def shape(*dims, dtype=jnp.float32):
    return jax.ShapeDtypeStruct(dims, dtype)


def params(**more):
    return pltpu.CompilerParams(vmem_limit_bytes=VMEM_LIMIT, **more)


def local(
    pieces_image, pieces_variance, piece_patch, piece_cell,
    stamp_row, stamp_col, stamp_count, warp_offsets,
):
    patches = lax.axis_size("patch")
    subtiles = lax.axis_size("sub")
    pieces = pieces_image.shape[1]
    slots = stamp_row.shape[1]
    dma, vmem, smem = pltpu.SemaphoreType.DMA, pltpu.VMEM, pltpu.SMEM
    far = pl.BlockSpec(memory_space=pltpu.HBM)

    def keep(*arrays):
        return [pltpu.with_memory_space_constraint(a, pltpu.HBM) for a in arrays]

    f32, i32, bf16 = jnp.float32, jnp.int32, jnp.bfloat16

    sent_shape, part_shape = shape(patches * BLOCK, 128), shape(patches * PART, 128)
    sent_image, sent_first, sent_last, sent_cell, table = pl.pallas_call(
        pack_kernel,
        out_shape=(
            sent_shape, part_shape, part_shape, shape(patches, 1, 128, dtype=i32),
            shape(1, 128, dtype=i32),
        ),
        in_specs=[far] * 7 + [SCALARS],
        out_specs=(WHOLE,) * 5,
        scratch_shapes=[
            vmem((pieces, CR, CW), f32), vmem((pieces, CR, CW), f32),
            smem((pieces,), i32), smem((pieces,), i32),
            smem((1, slots), i32), smem((1, slots), i32), smem((V,), i32),
            smem((patches,), i32), smem((2 * patches,), i32), dma((7,)),
        ],
        compiler_params=params(),
        name="pack",
    )(
        *keep(
            piece_patch.reshape(-1), piece_cell.reshape(-1), pieces_image, pieces_variance,
            stamp_row, stamp_col, warp_offsets,
        ),
        stamp_count,
    )

    row_bands, cols, rows = keep(*[jnp.asarray(x) for x in constants()])
    rim, small_rim = vmem((HALO, CW), f32), vmem((V * SR, CW), f32)
    field = shape(V, RT, CW)
    science, inverse, basis, gathered, root = pl.pallas_call(
        functools.partial(front_kernel, slots),
        out_shape=(
            shape(V, CE, CW), shape(V * CE, CW), shape(NB, CE, CW), shape(subtiles, 2 * XR, 128), field,
        ),
        in_specs=[WHOLE] * 5 + [far] * 3,
        out_specs=(WHOLE,) * 5,
        scratch_shapes=[
            vmem((patches * BLOCK, 128), f32),
            vmem((patches * PART, 128), f32), vmem((patches * PART, 128), f32),
            vmem((patches, 1, 128), i32), vmem((2, 1, 128), i32),
            vmem((V * RT, 128), f32), vmem((V * RT, 128), f32), vmem((RT, CW), f32),
            rim, rim, rim, rim,
            vmem((TE, CW), f32), vmem((NT, TE, CW), f32),
            vmem((RT * XR, 128), f32), vmem((RT * XR, 128), f32), vmem((RT, CW), f32),
            vmem((2, NCELL * RC, CW), f32), vmem((V, NCELL * RC, CW), f32), small_rim, small_rim, small_rim, small_rim,
            vmem((V, NCELL * RC, CW), f32), vmem((2 * V * XR, 128), f32), vmem((2 * XR, 128), f32),
            vmem(row_bands.shape, bf16), vmem(cols.shape, bf16), vmem(rows.shape, bf16),
            dma((4,)), dma((4,)), dma((3, 2)), dma((3, 2)),
            dma((subtiles - 1,)), dma((subtiles - 1,)), dma((8,)),
        ],
        compiler_params=pltpu.CompilerParams(
            vmem_limit_bytes=32 * 1024 * 1024, collective_id=0, has_side_effects=True
        ),
        name="front",
    )(sent_image, sent_first, sent_last, sent_cell, table, row_bands, cols, rows)

    normalizer = float(subtiles * slots * (2 * SH + 1) ** 2)
    difference, significance = pl.pallas_call(
        functools.partial(final_kernel, normalizer),
        out_shape=(field, field),
        in_specs=[WHOLE] * 5 + [far] * 2,
        out_specs=(WHOLE,) * 2,
        scratch_shapes=[
            vmem((V * XR, 128), f32), vmem((V * CE, CW), f32),
            vmem((2, CW, CW), bf16), vmem(rows.shape[1:], bf16), dma((2,)),
        ],
        compiler_params=params(),
        name="final",
    )(gathered, basis, science, inverse, root, cols, rows)
    return (difference[:, None], significance[:, None])


def solution(mesh):
    in_specs = (
        P("sub", "patch", None, None),
        P("sub", "patch", None, None),
        P("sub", "patch", None),
        P("sub", "patch"),
        P("patch", "sub"),
        P("patch", "sub"),
        P("patch", "sub"),
        P(),
    )
    out_specs = (P(None, "patch", "sub", None), P(None, "patch", "sub", None))
    return jax.shard_map(local, mesh=mesh, in_specs=in_specs, out_specs=out_specs, check_vma=False)
```

```python
import functools
import math

import jax
import jax.numpy as jnp
import numpy as np
from jax import lax
from jax.experimental import pallas as pl
from jax.experimental.pallas import tpu as pltpu
from jax.sharding import PartitionSpec as P

V = 4
NCELL = 8
CR = 8
RT = 64
CW = 256
KR = 10
PR = 10
SH = 15
WARP = 4
NB = 40
NP = 32
SIGMAS = (0.75, 1.5, 3.0)
DEGREES = (4, 4, 3)
PSF_SIGMA = 2.0
SKY_VAR = 0.1
RIDGE = 0.5
EPS = 1e-05
MESH = pl.DeviceIdType.MESH

NT = 14
XR = 48
TE = 128
CE = 96
TH = 24
SR = 16
HALO = TH + V * SR
BLOCK = 4 * CR
RC = CR // 2
PART = 4 * RC
PLANE = 8
NS = 12
OFFSETS = 2 * NS + 1
VMEM_LIMIT = 16 * 1024 * 1024
WHOLE = pl.BlockSpec(memory_space=pltpu.VMEM)
SCALARS = pl.BlockSpec(memory_space=pltpu.SMEM)


def tap_values():
    u = np.arange(-KR, KR + 1).astype(np.float64)
    rows = []
    for sigma, degree in zip(SIGMAS, DEGREES):
        t = u / sigma
        env = np.exp(-0.5 * t * t)
        he = [np.ones_like(t), t]
        for n in range(1, degree):
            he.append(t * he[n] - n * he[n - 1])
        for n in range(degree + 1):
            h = he[n] * env
            rows.append(h / np.sqrt(np.sum(h * h)))
    return np.stack(rows)


def psf_values():
    u = np.arange(-PR, PR + 1).astype(np.float64)
    g = np.exp(-0.5 * (u / PSF_SIGMA) ** 2)
    return g / g.sum()


def split_np(a):
    a = a.astype(np.float32)
    hi = a.astype(jnp.bfloat16)
    lo = (a - hi.astype(np.float32)).astype(jnp.bfloat16)
    return hi, lo


def band(taps, rows, cols, first):
    radius = (len(taps) - 1) // 2
    out = np.zeros((rows, cols))
    for r in range(rows):
        for u in range(-radius, radius + 1):
            c = r + first + u
            if 0 <= c < cols:
                out[r, c] = taps[u + radius]
    return out


def constants():
    taps = tap_values()
    every = [band(taps[j], CE, TE, SR) for j in range(NT)]
    bands = np.concatenate(
        [b[SR : SR + RT] for b in every]
        + [np.concatenate([b[0:SR], b[SR + RT : CE]], axis=0) for b in every],
        axis=0,
    )
    hi, lo = split_np(bands)
    row_bands = np.concatenate([hi, lo], axis=1)
    p = psf_values()
    cols, rows = [], []
    for f in (p, p * p):
        cols += list(split_np(band(f, CW, CW, 0)))
        h, l = split_np(band(f, RT, CE, SR))
        rows.append(np.concatenate([h, l, h], axis=1))
    return row_bands, np.stack(cols), np.stack(rows)


def members_of():
    result, first_tap, first = [], 0, 0
    for degree in DEGREES:
        index = {}
        for i in range(degree + 1):
            for j in range(degree + 1 - i):
                index[(i, j)] = first + len(index)
        result.append((first_tap, degree, index))
        first_tap += degree + 1
        first += len(index)
    return result


def split(x):
    hi = x.astype(jnp.bfloat16)
    return hi, (x - hi.astype(jnp.float32)).astype(jnp.bfloat16)


def mm(a, b):
    return jnp.dot(a, b, preferred_element_type=jnp.float32)


def plan_kernel(
    patch, cell, row, col, warp, live,
    out_index, out_cell, table,
    patch_in, cell_in, row_in, col_in, warp_in, count, slot_cell, slot_index, sems,
):
    patches = out_cell.shape[0]
    pieces = patch.shape[0]
    slots = row.shape[1]
    pairs = ((patch, patch_in), (cell, cell_in), (row, row_in), (col, col_in), (warp, warp_in))
    copies = [pltpu.make_async_copy(x, y, sems.at[n]) for n, (x, y) in enumerate(pairs)]
    for c in copies:
        c.start()

    def clear(n, _):
        count[n] = 0
        for rank in range(2):
            slot_cell[2 * n + rank] = -1
            slot_index[2 * n + rank] = pieces
        return 0

    lax.fori_loop(0, patches, clear, 0)
    for c in copies:
        c.wait()

    def place(n, _):
        q = patch_in[n]
        rank = count[q]
        count[q] = rank + 1
        slot_cell[2 * q + rank] = cell_in[n]
        slot_index[2 * q + rank] = n
        return 0

    lax.fori_loop(0, pieces, place, 0)
    lane = lax.broadcasted_iota(jnp.int32, (1, 128), 1)

    def tell(q, line):
        out_cell[q] = jnp.where(lane == 0, slot_cell[2 * q], slot_cell[2 * q + 1])
        line = jnp.where(lane == 2 * q, slot_index[2 * q], line)
        return jnp.where(lane == 2 * q + 1, slot_index[2 * q + 1], line)

    out_index[...] = lax.fori_loop(0, patches, tell, jnp.zeros((1, 128), jnp.int32))
    values = [row_in[0, n] for n in range(slots)] + [col_in[0, n] for n in range(slots)]
    values += [live[0, 0]] + [warp_in[v] for v in range(V)]
    line = jnp.zeros((1, 128), jnp.int32)
    for n, value in enumerate(values):
        line = jnp.where(lane == n, value, line)
    table[...] = line


def stamp_mask(mask, stamps, got_stamps, sub, subtiles, slots):
    row = lax.broadcasted_iota(jnp.int32, (RT, CW), 0)
    col = lax.broadcasted_iota(jnp.int32, (RT, CW), 1)
    flags = [(sub > 0).astype(jnp.int32), 1, (sub < subtiles - 1).astype(jnp.int32)]
    mask[...] = jnp.zeros_like(mask)
    for n, (flag, table) in enumerate(zip(flags, (got_stamps[0], stamps[...], got_stamps[1]))):
        count = table[:, 2 * slots : 2 * slots + 1] * flag
        for k in range(slots):
            near_row = jnp.abs(row - (n - 1) * RT - table[:, k : k + 1]) <= SH
            near_col = jnp.abs(col - table[:, slots + k : slots + k + 1]) <= SH
            mask[...] = jnp.where(near_row & near_col & (count > k), 1.0, mask[...])


def choose(cells):
    patches = cells.shape[0]
    lane = lax.broadcasted_iota(jnp.int32, (patches, 128), 1)
    table = cells[:, 0, :]
    wide = jnp.concatenate(
        [(table[:, rank : rank + 1] == lane).astype(jnp.float32) for rank in range(2)]
        + [jnp.zeros((128 - 2 * patches, 128), jnp.float32)] * (2 * patches < 128),
        axis=0,
    )
    return jnp.transpose(wide)[0 : V * NCELL, :].astype(jnp.bfloat16)


def combine(chosen, patches, table, got, rows, put_field, left, right):
    for half, ref in enumerate((left, right)):
        for r in range(rows):
            x = jnp.concatenate(
                [
                    got[pl.ds((half * 2 + rank) * rows + r, patches, stride=4 * rows), :]
                    for rank in range(2)
                ]
                + [jnp.zeros((128 - 2 * patches, 128), jnp.float32)] * (2 * patches < 128),
                axis=0,
            )
            hi = x.astype(jnp.bfloat16)
            mid, low = split(x - hi.astype(jnp.float32))
            y = mm(chosen, jnp.concatenate([hi, mid, low], axis=1))
            ref[pl.ds(r, V * NCELL, stride=rows), :] = y[:, 0:128] + y[:, 128:256] + y[:, 256:384]
    size = NCELL * rows
    col = lax.broadcasted_iota(jnp.int32, (size, CW), 1)
    for v in range(V):
        at = slice(v * size, (v + 1) * size)
        off = jnp.broadcast_to(table[:, OFFSETS + v : OFFSETS + v + 1], (size, CW))
        a = pltpu.roll(jnp.concatenate([left[at, :], right[at, :]], axis=1), WARP, 1)
        for bit in range(4):
            a = jnp.where((off & (1 << bit)) != 0, pltpu.roll(a, CW - (1 << bit), 1), a)
        source = col + off - WARP
        put_field(v, jnp.where((source >= 0) & (source < CW), a, 0.0))


def smooth(plane, col_hi, col_lo, row_taps):
    hi, lo = split(plane)
    yh, yl = split(mm(hi, col_hi) + mm(lo, col_hi) + mm(hi, col_lo))
    outs = []
    for v in range(V):
        a = slice(v * CE, (v + 1) * CE)
        outs.append(mm(row_taps, jnp.concatenate([yh[a], yh[a], yl[a]], axis=0)))
    return outs


def front_kernel(
    slots, index, cells, stamps, image_in, variance_in, row_bands_in, cols_in, rows_in,
    science, inverse, basis, gathered, root,
    held_0, held_1, held_2, held_3, held_4, held_5, near_index, index_of, sent_image, sent_first, sent_last,
    got_image, got_first, got_last, got_cells, got_stamps, left, right, template, up, down, above, below,
    text, filt, xleft, xright, mask, half_mask, wide, wup, wdown, wabove, wbelow, weight, acc, gram,
    row_bands, cols, rows, send, recv, ring_send, ring_recv, all_send, all_recv,
    far_send, far_recv, index_send, index_recv, own,
):
    patches = cells.shape[0]
    subtiles = gathered.shape[0]
    me, sub = lax.axis_index("patch"), lax.axis_index("sub")
    peers = [lax.rem(sub + d, subtiles) for d in range(1, subtiles)]
    next_sub, last_sub = peers[0], peers[-1]
    has_above = (sub > 0).astype(jnp.float32)
    has_below = (sub < subtiles - 1).astype(jnp.float32)
    held = (held_0, held_1, held_2, held_3, held_4, held_5)
    pieces = image_in.shape[1]
    planes = patches // PLANE
    z, flat = me // PLANE, lax.rem(me, PLANE)
    after, before = lax.rem(z + 1, planes), lax.rem(z + planes - 1, planes)
    barrier = pltpu.get_barrier_semaphore()

    def greet(d, _):
        q = lax.rem(me + d, patches)
        pl.semaphore_signal(barrier, inc=1, device_id={"patch": q}, device_id_type=MESH)
        return 0

    lax.fori_loop(1, patches, greet, 0)
    for s in peers:
        pl.semaphore_signal(barrier, inc=1, device_id={"sub": s}, device_id_type=MESH)
    mine = [
        pltpu.make_async_copy(x, y, own.at[n])
        for n, (x, y) in enumerate(
            (
                (image_in.at[0], held[0].at[pl.ds(0, pieces)]),
                (variance_in.at[0], held[3].at[pl.ds(0, pieces)]),
                (index, index_of.at[0]),
                (cells.at[pl.ds(me, 1)], got_cells.at[pl.ds(me, 1)]),
                (row_bands_in, row_bands), (cols_in, cols), (rows_in, rows),
            )
        )
    ]
    for c in mine:
        c.start()
    for n in range(6):
        held[n][pieces] = jnp.zeros((CR, CW), jnp.float32)
    pl.semaphore_wait(barrier, patches - 1 + subtiles - 1)

    far = [
        pltpu.make_async_remote_copy(
            src_ref=x.at[0], dst_ref=held[3 * kind + 1 + side].at[pl.ds(0, pieces)],
            send_sem=far_send.at[2 * kind + side], recv_sem=far_recv.at[2 * kind + side],
            device_id={"patch": to * PLANE + flat}, device_id_type=MESH,
        )
        for kind, x in enumerate((image_in, variance_in))
        for side, to in enumerate((after, before))
    ]
    told = [
        pltpu.make_async_remote_copy(
            src_ref=index, dst_ref=near_index.at[side], send_sem=index_send.at[side],
            recv_sem=index_recv.at[side], device_id={"patch": to * PLANE + flat},
            device_id_type=MESH,
        )
        for side, to in enumerate((after, before))
    ]
    for c in told + far[0:2]:
        c.start()

    pairs = (
        (cells, got_cells, 1), (sent_image, got_image, BLOCK),
        (sent_first, got_first, PART), (sent_last, got_last, PART),
    )

    def rows_at(n, q):
        size = pairs[n][2]
        return pl.ds(pl.multiple_of(q * size, size), size)

    def send_to(n, block, to, source):
        src, dst, _ = pairs[n]
        pltpu.make_async_remote_copy(
            src_ref=src.at[rows_at(n, block)], dst_ref=dst.at[rows_at(n, source)],
            send_sem=send.at[n], recv_sem=recv.at[n],
            device_id={"patch": to}, device_id_type=MESH,
        ).start()

    def whole(n):
        src, dst, size = pairs[n]
        at = pl.ds(0, (patches - (1 if n == 0 else 3)) * size)
        return pltpu.make_async_remote_copy(
            src_ref=src.at[at], dst_ref=dst.at[at], send_sem=send.at[n], recv_sem=recv.at[n],
            device_id={"patch": lax.rem(me + 1, patches)}, device_id_type=MESH,
        )

    sources = [q * PLANE + flat for q in (z, before, after)]
    signs = (0, 1, planes - 1)
    half = planes // 2
    shares = ((1, half, half - 1), (1, half - 1, half))

    def first_block(kind, role):
        return PLANE * sum(shares[kind][0:role])

    def target(role, i):
        plane = lax.rem(z + signs[role] * (i // PLANE), planes)
        return plane * PLANE + lax.rem(i + flat, PLANE)

    def pack(kind, role):
        first = first_block(kind, role)

        def body(i, _):
            q = target(role, i)
            x = [held[3 * kind + role][index_of[role, 0, 2 * q + rank]] for rank in range(2)]
            if kind == 0:
                tall = [jnp.concatenate([a[:, h : h + 128] for a in x], axis=0) for h in (0, 128)]
                values = [(1, jnp.concatenate(tall, axis=0))]
            else:
                values = []
                for k in range(2):
                    cut = slice(k * RC, (k + 1) * RC)
                    tall = [jnp.concatenate([a[cut, h : h + 128] for a in x], axis=0) for h in (0, 128)]
                    values.append((2 + k, jnp.concatenate(tall, axis=0)))
            for n, value in values:
                pairs[n][0][rows_at(n, first + i), :] = value

            @pl.when(q == me)
            def _():
                for n, value in values:
                    pairs[n][1][rows_at(n, sources[role]), :] = value

            return 0

        lax.fori_loop(0, PLANE * shares[kind][role], body, 0)

    def dispatch(n, role):
        kind = min(n - 1, 1)
        first = first_block(kind, role)

        def body(i, _):
            q = target(role, i)

            @pl.when(q != me)
            def _():
                send_to(n, first + i, q, sources[role])

            return 0

        lax.fori_loop(0, PLANE * shares[kind][role], body, 0)

    def ring(n, src, dst):
        return [
            pltpu.make_async_remote_copy(
                src_ref=s, dst_ref=r, send_sem=ring_send.at[n, k], recv_sem=ring_recv.at[n, k],
                device_id={"sub": to}, device_id_type=MESH,
            )
            for k, (s, r, to) in enumerate(zip(src, dst, (next_sub, last_sub)))
        ]

    def tell_cells(d, _):
        q = lax.rem(me + d, patches)
        send_to(0, q, q, me)
        return 0

    lax.fori_loop(1, patches, tell_cells, 0)
    table_ring = ring(0, (stamps, stamps), (got_stamps.at[0], got_stamps.at[1]))
    for c in table_ring + far[2:4]:
        c.start()
    for c in mine:
        c.wait()
    pack(0, 0)
    pack(1, 0)
    dispatch(1, 0)
    moves = []
    for side, c in enumerate(told):
        c.wait()
        moves.append(pltpu.make_async_copy(near_index.at[side], index_of.at[1 + side], own.at[side]))
        moves[side].start()
    for c in moves:
        c.wait()
    for c in far[0:2]:
        c.wait_recv()
    for role in (1, 2):
        pack(0, role)
        dispatch(1, role)
    for c in far[2:4]:
        c.wait_recv()
    for role in (1, 2):
        pack(1, role)
        dispatch(2, role)
    dispatch(2, 0)
    for role in (1, 2, 0):
        dispatch(3, role)
    for c in far:
        c.wait_send()
    for c in table_ring:
        c.wait()
    stamp_mask(mask, stamps, got_stamps, sub, subtiles, slots)

    for c in range(NCELL):
        for k in range(2):
            half_mask[k, c * RC : (c + 1) * RC, :] = mask[c * CR + k * RC : c * CR + (k + 1) * RC, :]
    acc[...] = jnp.zeros_like(acc)
    for at in (slice(0, 16), slice(112, TE)):
        filt[:, at, :] = jnp.zeros((NT, 16, CW), jnp.float32)
        text[at, :] = jnp.zeros((16, CW), jnp.float32)
    for k in (NB,) + tuple(range(NB + 1 + V, XR)):
        for ref in (xleft, xright):
            ref[pl.ds(k, RT, stride=XR), :] = jnp.full((RT, 128), float(k == NB), jnp.float32)
    whole(0).wait_recv()
    whole(1).wait_recv()
    table = stamps[...]
    chosen = choose(got_cells)

    def put_science(v, field):
        science[v, SR : SR + RT, :] = field

    combine(chosen, patches, table, got_image, CR, put_science, left, right)
    inner = slice(SR, SR + RT)
    template[...] = (science[0, inner] + science[1, inner] + science[2, inner] + science[3, inner]) / V
    up[0:TH, :] = template[0:TH, :]
    down[0:TH, :] = template[RT - TH : RT, :]
    for v in range(V):
        at = TH + v * SR
        up[at : at + SR, :] = science[v, SR : 2 * SR, :]
        down[at : at + SR, :] = science[v, RT : RT + SR, :]
    rims = ring(1, (down, up), (above, below))
    for c in rims:
        c.start()
    text[32:96, :] = template[...]
    filter_columns(text, filt, (8, lambda i: i + 4))
    for c in rims:
        c.wait()
    text[8:32, :] = above[0:TH, :] * has_above
    text[96:120, :] = below[0:TH, :] * has_below
    filter_columns(text, filt, (4, lambda i: i + 2 + 8 * (i // 2)))

    def put(k, image):
        at = pl.ds(k, RT, stride=XR)
        xleft[at, :] = image[:, 0:128]
        xright[at, :] = image[:, 128:CW]

    def keep_inner(k, image):
        basis[k, SR : SR + RT, :] = image
        put(k, image)

    def keep_rim(k, image):
        basis[k, 0:SR, :] = image[0:SR, :]
        basis[k, SR + RT : CE, :] = image[SR : 2 * SR, :]

    filter_rows(row_bands, filt, 0, RT, keep_inner)
    for v in range(V):
        put(NB + 1 + v, science[v, SR : SR + RT, :])
    whole(0).wait_send()
    whole(1).wait_send()

    def invert(planes):
        q = (planes[0] + planes[1] + planes[2] + planes[3]) / (V * V)
        return [1.0 / (p + q + SKY_VAR) for p in planes]

    def put_wide(v, field):
        wide[v] = field

    wrims = ring(2, (wdown, wup), (wabove, wbelow))
    for k, got in enumerate((got_first, got_last)):
        whole(2 + k).wait_recv()
        combine(chosen, patches, table, got, RC, put_wide, left, right)
        for v in range(V):
            for c in range(SR // CR):
                at = slice(v * SR + c * CR + k * RC, v * SR + c * CR + (k + 1) * RC)
                low = NCELL - SR // CR + c
                wup[at, :] = wide[v, c * RC : (c + 1) * RC, :]
                wdown[at, :] = wide[v, low * RC : (low + 1) * RC, :]
        if k == 1:
            for c in wrims:
                c.start()
        for v, inv in enumerate(invert([wide[v] for v in range(V)])):
            weight[v] = half_mask[k] * inv
            for c in range(NCELL):
                first = v * CE + SR + c * CR + k * RC
                inverse[first : first + RC, :] = inv[c * RC : (c + 1) * RC, :]
        gram_of(k, weight, xleft, xright, acc)
    gram_total(acc, gram)
    parts = [
        pltpu.make_async_remote_copy(
            src_ref=gram, dst_ref=gathered.at[sub], send_sem=all_send.at[n], recv_sem=all_recv.at[n],
            device_id={"sub": s}, device_id_type=MESH,
        )
        for n, s in enumerate(peers)
    ]
    for c in parts:
        c.start()
    my_part = pltpu.make_async_copy(gram, gathered.at[sub], own.at[7])
    my_part.start()
    for c in wrims:
        c.wait()
    for ref, first, has in ((wabove, 0, has_above), (wbelow, SR + RT, has_below)):
        planes = [ref[v * SR : (v + 1) * SR, :] for v in range(V)]
        for v, inv in enumerate(invert(planes)):
            inverse[v * CE + first : v * CE + first + SR, :] = inv * has
    for v in range(V):
        at = TH + v * SR
        science[v, 0:SR, :] = above[at : at + SR, :] * has_above
        science[v, SR + RT : CE, :] = below[at : at + SR, :] * has_below
    filter_columns(text, filt, (2, lambda i: 1 + 13 * i))
    filter_rows(row_bands, filt, NT * RT, 2 * SR, keep_rim)
    for v, den in enumerate(smooth(inverse[...], cols[2], cols[3], rows[1])):
        root[v] = lax.rsqrt(den)
    my_part.wait()
    for n, c in enumerate(parts):
        c.wait_send()
        source = peers[subtiles - 2 - n]
        pltpu.make_async_remote_copy(
            src_ref=gram, dst_ref=gathered.at[source], send_sem=all_send.at[n],
            recv_sem=all_recv.at[n], device_id={"sub": source}, device_id_type=MESH,
        ).wait_recv()

    whole(2).wait_send()
    whole(3).wait_send()


def filter_columns(text, filt, blocks):
    taps = tap_values()
    col = lax.broadcasted_iota(jnp.int32, (8, CW), 1)

    def columns(i, _):
        rows = pl.ds(pl.multiple_of(i * 8, 8), 8)
        t = text[rows, :]
        sums = [None] * NT
        for u in range(0, KR + 1):
            if u:
                plus = jnp.where(col < CW - u, pltpu.roll(t, CW - u, 1), 0.0)
                minus = jnp.where(col >= u, pltpu.roll(t, u, 1), 0.0)
                even, odd = plus + minus, plus - minus
            first = 0
            for degree in DEGREES:
                for n in range(degree + 1):
                    j = first + n
                    h = float(np.float32(taps[j, KR + u]))
                    if u == 0:
                        sums[j] = t * h if n % 2 == 0 else None
                    else:
                        term = (even if n % 2 == 0 else odd) * h
                        sums[j] = term if sums[j] is None else sums[j] + term
                first += degree + 1
        for j in range(NT):
            filt[j, rows, :] = sums[j]
        return 0

    count, place = blocks
    lax.fori_loop(0, count, lambda i, _: columns(place(i), _), 0)


def filter_rows(row_bands, filt, first_row, size, keep):
    for first_tap, degree, index in members_of():
        for j in range(degree + 1):
            count = degree + 1 - j
            at = first_row + first_tap * size
            lhs = row_bands[at : at + count * size, :]
            fh, fl = split(filt[first_tap + j])
            y = mm(lhs, jnp.concatenate([fh, fh], axis=0)) + mm(lhs[:, 0:TE], fl)
            for i in range(count):
                keep(index[(i, j)], y[i * size : (i + 1) * size, :])


def gram_of(k, weight, xleft, xright, acc):
    def cell(i, _):
        lefts, rights = [], []
        for r0 in range(RC):
            r = i * CR + k * RC + r0
            at = pl.ds(pl.multiple_of(r * XR, 8), XR)
            x = jnp.concatenate([xleft[at, :], xright[at, :]], axis=1)
            xh, xl = split(x)
            rights.append(jnp.concatenate([xh, xl, jnp.zeros((32, CW), jnp.bfloat16)], axis=0))
            his, los = [], []
            for v in range(V):
                lh, ll = split(x * weight[v, pl.ds(i * RC + r0, 1), :])
                his.append(lh)
                los.append(ll)
            lefts.append(jnp.concatenate(his + los, axis=0))
        acc[...] += lax.dot_general(
            jnp.concatenate(lefts, axis=1), jnp.concatenate(rights, axis=1),
            (((1,), (1,)), ((), ())), preferred_element_type=jnp.float32,
        )
        return 0

    lax.fori_loop(0, NCELL, cell, 0)


def gram_total(acc, gram):
    high = acc[0 : V * XR, :]
    total = high + pltpu.roll(high, 128 - XR, 1) + acc[V * XR : 2 * V * XR, :]
    lane = lax.broadcasted_iota(jnp.int32, total.shape, 1)
    total = jnp.where(lane < XR, total, 0.0)
    gram[...] = total[0 : 2 * XR, :] + pltpu.roll(total[2 * XR : 4 * XR, :], 64, 1)


def pick(x, index):
    return jnp.take_along_axis(x, index, axis=1, mode="promise_in_bounds")


def final_kernel(
    normalizer, gathered, basis, science, inverse, root, cols_in, rows_in,
    difference, significance, coef, dplane, cols, rows, sems,
):
    copies = [
        pltpu.make_async_copy(x, y, sems.at[n])
        for n, (x, y) in enumerate(((cols_in.at[0:2], cols), (rows_in.at[0], rows)))
    ]
    for c in copies:
        c.start()
    total = gathered[0] + gathered[1] + gathered[2] + gathered[3]
    total = total * (1.0 / normalizer)
    row = lax.broadcasted_iota(jnp.int32, (XR, 128), 0)
    lane = lax.broadcasted_iota(jnp.int32, (XR, 128), 1)
    part = lane // 64
    j = lane - part * 64
    base = part * 64
    halves, scales = [], []
    for half in range(2):
        a = total[half * XR : (half + 1) * XR, :]
        v = half + 2 * part
        e_col = lax.rsqrt(pick(a, base + row) + EPS)
        diag = jnp.sum(jnp.where(row == j, a, 0.0), axis=0, keepdims=True)
        e_row = lax.rsqrt(diag + EPS)
        scaled = a * e_col
        system = jnp.where(j <= NB, scaled * e_row, jnp.where(j == NB + 1 + v, scaled, 0.0))
        system = system + jnp.where(row == j, RIDGE, 0.0)
        halves.append(system)
        scales.append(e_col)
    for k in range(NB + 1):
        for half in range(2):
            a = halves[half]
            pivot_row = jnp.broadcast_to(a[k : k + 1, :], (XR, 128))
            pivot = pick(pivot_row, base + k)
            column = pick(a, base + k)
            column = jnp.where(row == k, pivot - 1.0, column)
            halves[half] = a - column * (pivot_row / pivot)
    for half in range(2):
        v = half + 2 * part
        a = pick(halves[half], base + NB + 1 + v) * scales[half]
        coef[half * XR : (half + 1) * XR, :] = pick(a, lane * 0)
        coef[(half + 2) * XR : (half + 3) * XR, :] = pick(a, lane * 0 + 64)

    def block(b, _):
        at = pl.ds(pl.multiple_of(b * 8, 8), 8)
        sums = []
        for v in range(V):
            a = coef[v * XR + NB : v * XR + NB + 1, :]
            sums.append(science[v, at, :] - jnp.concatenate([a, a], axis=1))
        for k in range(NB):
            c = basis[k, at, :]
            for v in range(V):
                a = coef[v * XR + k : v * XR + k + 1, :]
                sums[v] = sums[v] - c * jnp.concatenate([a, a], axis=1)
        for v in range(V):
            plane = pl.ds(pl.multiple_of(v * CE + b * 8, 8), 8)
            dplane[plane, :] = sums[v] * inverse[plane, :]

        @pl.when((b >= SR // 8) & (b < (SR + RT) // 8))
        def _():
            inner = pl.ds(pl.multiple_of(b * 8 - SR, 8), 8)
            for v in range(V):
                difference[v, inner, :] = sums[v]

        return 0

    lax.fori_loop(0, CE // 8, block, 0)
    for c in copies:
        c.wait()
    for v, num in enumerate(smooth(dplane[...], cols[0], cols[1], rows[...])):
        significance[v] = num * root[v]


def shape(*dims, dtype=jnp.float32):
    return jax.ShapeDtypeStruct(dims, dtype)


def params(**more):
    return pltpu.CompilerParams(vmem_limit_bytes=VMEM_LIMIT, **more)


def local(
    pieces_image, pieces_variance, piece_patch, piece_cell,
    stamp_row, stamp_col, stamp_count, warp_offsets,
):
    patches = lax.axis_size("patch")
    subtiles = lax.axis_size("sub")
    pieces = pieces_image.shape[1]
    slots = stamp_row.shape[1]
    dma, vmem, smem = pltpu.SemaphoreType.DMA, pltpu.VMEM, pltpu.SMEM
    far = pl.BlockSpec(memory_space=pltpu.HBM)

    def keep(*arrays):
        return [pltpu.with_memory_space_constraint(a, pltpu.HBM) for a in arrays]

    f32, i32, bf16 = jnp.float32, jnp.int32, jnp.bfloat16

    sent_shape, part_shape = vmem((patches * BLOCK, 128), f32), vmem((patches * PART, 128), f32)
    pieces_image, pieces_variance = keep(pieces_image, pieces_variance)
    line = shape(1, 128, dtype=i32)
    index, sent_cell, table = pl.pallas_call(
        plan_kernel,
        out_shape=(line, shape(patches, 1, 128, dtype=i32), line),
        in_specs=[far] * 5 + [SCALARS],
        out_specs=(WHOLE,) * 3,
        scratch_shapes=[
            smem((pieces,), i32), smem((pieces,), i32),
            smem((1, slots), i32), smem((1, slots), i32), smem((V,), i32),
            smem((patches,), i32), smem((2 * patches,), i32), smem((2 * patches,), i32), dma((5,)),
        ],
        compiler_params=params(),
        name="plan",
    )(
        *keep(
            piece_patch.reshape(-1), piece_cell.reshape(-1), stamp_row, stamp_col, warp_offsets,
        ),
        stamp_count,
    )

    row_bands, cols, rows = keep(*[jnp.asarray(x) for x in constants()])
    rim, small_rim = vmem((HALO, CW), f32), vmem((V * SR, CW), f32)
    field = shape(V, RT, CW)
    science, inverse, basis, gathered, root = pl.pallas_call(
        functools.partial(front_kernel, slots),
        out_shape=(
            shape(V, CE, CW), shape(V * CE, CW), shape(NB, CE, CW), shape(subtiles, 2 * XR, 128), field,
        ),
        in_specs=[WHOLE] * 3 + [far] * 5,
        out_specs=(WHOLE,) * 5,
        scratch_shapes=[
            *[vmem((pieces + 1, CR, CW), f32)] * 6, vmem((2, 1, 128), i32), smem((3, 1, 128), i32),
            sent_shape, part_shape, part_shape, sent_shape, part_shape, part_shape,
            vmem((patches, 1, 128), i32), vmem((2, 1, 128), i32),
            vmem((V * RT, 128), f32), vmem((V * RT, 128), f32), vmem((RT, CW), f32),
            rim, rim, rim, rim,
            vmem((TE, CW), f32), vmem((NT, TE, CW), f32),
            vmem((RT * XR, 128), f32), vmem((RT * XR, 128), f32), vmem((RT, CW), f32),
            vmem((2, NCELL * RC, CW), f32), vmem((V, NCELL * RC, CW), f32), small_rim, small_rim, small_rim, small_rim,
            vmem((V, NCELL * RC, CW), f32), vmem((2 * V * XR, 128), f32), vmem((2 * XR, 128), f32),
            vmem(row_bands.shape, bf16), vmem(cols.shape, bf16), vmem(rows.shape, bf16),
            dma((4,)), dma((4,)), dma((3, 2)), dma((3, 2)),
            dma((subtiles - 1,)), dma((subtiles - 1,)),
            dma((4,)), dma((4,)), dma((2,)), dma((2,)), dma((8,)),
        ],
        compiler_params=pltpu.CompilerParams(
            vmem_limit_bytes=32 * 1024 * 1024, collective_id=0, has_side_effects=True
        ),
        name="front",
    )(index, sent_cell, table, pieces_image, pieces_variance, row_bands, cols, rows)

    normalizer = float(subtiles * slots * (2 * SH + 1) ** 2)
    difference, significance = pl.pallas_call(
        functools.partial(final_kernel, normalizer),
        out_shape=(field, field),
        in_specs=[WHOLE] * 5 + [far] * 2,
        out_specs=(WHOLE,) * 2,
        scratch_shapes=[
            vmem((V * XR, 128), f32), vmem((V * CE, CW), f32),
            vmem((2, CW, CW), bf16), vmem(rows.shape[1:], bf16), dma((2,)),
        ],
        compiler_params=params(),
        name="final",
    )(gathered, basis, science, inverse, root, cols, rows)
    return (difference[:, None], significance[:, None])


def solution(mesh):
    in_specs = (
        P("sub", "patch", None, None),
        P("sub", "patch", None, None),
        P("sub", "patch", None),
        P("sub", "patch"),
        P("patch", "sub"),
        P("patch", "sub"),
        P("patch", "sub"),
        P(),
    )
    out_specs = (P(None, "patch", "sub", None), P(None, "patch", "sub", None))
    return jax.shard_map(local, mesh=mesh, in_specs=in_specs, out_specs=out_specs, check_vma=False)
```

```python
import functools
import math

import jax
import jax.numpy as jnp
import numpy as np
from jax import lax
from jax.experimental import pallas as pl
from jax.experimental.pallas import tpu as pltpu
from jax.sharding import PartitionSpec as P

V = 4
NCELL = 8
CR = 8
RT = 64
CW = 256
KR = 10
PR = 10
SH = 15
WARP = 4
NB = 40
NP = 32
SIGMAS = (0.75, 1.5, 3.0)
DEGREES = (4, 4, 3)
PSF_SIGMA = 2.0
SKY_VAR = 0.1
RIDGE = 0.5
EPS = 1e-05
MESH = pl.DeviceIdType.MESH

NT = 14
XR = 48
TE = 128
CE = 96
TH = 24
SR = 16
HALO = TH + V * SR
BLOCK = 4 * CR
RC = CR // 2
PART = 4 * RC
PLANE = 8
NS = 12
OFFSETS = 2 * NS + 1
VMEM_LIMIT = 16 * 1024 * 1024
WHOLE = pl.BlockSpec(memory_space=pltpu.VMEM)
SCALARS = pl.BlockSpec(memory_space=pltpu.SMEM)


def tap_values():
    u = np.arange(-KR, KR + 1).astype(np.float64)
    rows = []
    for sigma, degree in zip(SIGMAS, DEGREES):
        t = u / sigma
        env = np.exp(-0.5 * t * t)
        he = [np.ones_like(t), t]
        for n in range(1, degree):
            he.append(t * he[n] - n * he[n - 1])
        for n in range(degree + 1):
            h = he[n] * env
            rows.append(h / np.sqrt(np.sum(h * h)))
    return np.stack(rows)


def psf_values():
    u = np.arange(-PR, PR + 1).astype(np.float64)
    g = np.exp(-0.5 * (u / PSF_SIGMA) ** 2)
    return g / g.sum()


def split_np(a):
    a = a.astype(np.float32)
    hi = a.astype(jnp.bfloat16)
    lo = (a - hi.astype(np.float32)).astype(jnp.bfloat16)
    return hi, lo


def band(taps, rows, cols, first):
    radius = (len(taps) - 1) // 2
    out = np.zeros((rows, cols))
    for r in range(rows):
        for u in range(-radius, radius + 1):
            c = r + first + u
            if 0 <= c < cols:
                out[r, c] = taps[u + radius]
    return out


def constants():
    taps = tap_values()
    every = [band(taps[j], CE, TE, SR) for j in range(NT)]
    bands = np.concatenate(
        [b[SR : SR + RT] for b in every]
        + [np.concatenate([b[0:SR], b[SR + RT : CE]], axis=0) for b in every],
        axis=0,
    )
    hi, lo = split_np(bands)
    row_bands = np.concatenate([hi, lo], axis=1)
    p = psf_values()
    cols, rows = [], []
    for f in (p, p * p):
        cols += list(split_np(band(f, CW, CW, 0)))
        h, l = split_np(band(f, RT, CE, SR))
        rows.append(np.concatenate([h, l, h], axis=1))
    return row_bands, np.stack(cols), np.stack(rows)


def members_of():
    result, first_tap, first = [], 0, 0
    for degree in DEGREES:
        index = {}
        for i in range(degree + 1):
            for j in range(degree + 1 - i):
                index[(i, j)] = first + len(index)
        result.append((first_tap, degree, index))
        first_tap += degree + 1
        first += len(index)
    return result


def split(x):
    hi = x.astype(jnp.bfloat16)
    return hi, (x - hi.astype(jnp.float32)).astype(jnp.bfloat16)


def mm(a, b):
    return jnp.dot(a, b, preferred_element_type=jnp.float32)


def plan_kernel(
    patch, cell, row, col, warp, live,
    out_index, out_cell, table,
    patch_in, cell_in, row_in, col_in, warp_in, count, slot_cell, slot_index, sems,
):
    patches = out_cell.shape[0]
    pieces = patch.shape[0]
    slots = row.shape[1]
    pairs = ((patch, patch_in), (cell, cell_in), (row, row_in), (col, col_in), (warp, warp_in))
    copies = [pltpu.make_async_copy(x, y, sems.at[n]) for n, (x, y) in enumerate(pairs)]
    for c in copies:
        c.start()

    def clear(n, _):
        count[n] = 0
        for rank in range(2):
            slot_cell[2 * n + rank] = -1
            slot_index[2 * n + rank] = pieces
        return 0

    lax.fori_loop(0, patches, clear, 0)
    for c in copies:
        c.wait()

    def place(n, _):
        q = patch_in[n]
        rank = count[q]
        count[q] = rank + 1
        slot_cell[2 * q + rank] = cell_in[n]
        slot_index[2 * q + rank] = n
        return 0

    lax.fori_loop(0, pieces, place, 0)
    lane = lax.broadcasted_iota(jnp.int32, (1, 128), 1)

    def tell(q, line):
        out_cell[q] = jnp.where(lane == 0, slot_cell[2 * q], slot_cell[2 * q + 1])
        line = jnp.where(lane == 2 * q, slot_index[2 * q], line)
        return jnp.where(lane == 2 * q + 1, slot_index[2 * q + 1], line)

    out_index[...] = lax.fori_loop(0, patches, tell, jnp.zeros((1, 128), jnp.int32))
    values = [row_in[0, n] for n in range(slots)] + [col_in[0, n] for n in range(slots)]
    values += [live[0, 0]] + [warp_in[v] for v in range(V)]
    line = jnp.zeros((1, 128), jnp.int32)
    for n, value in enumerate(values):
        line = jnp.where(lane == n, value, line)
    table[...] = line


def stamp_mask(mask, stamps, got_stamps, sub, subtiles, slots):
    row = lax.broadcasted_iota(jnp.int32, (RT, CW), 0)
    col = lax.broadcasted_iota(jnp.int32, (RT, CW), 1)
    flags = [(sub > 0).astype(jnp.int32), 1, (sub < subtiles - 1).astype(jnp.int32)]
    mask[...] = jnp.zeros_like(mask)
    for n, (flag, table) in enumerate(zip(flags, (got_stamps[0], stamps[...], got_stamps[1]))):
        count = table[:, 2 * slots : 2 * slots + 1] * flag
        for k in range(slots):
            near_row = jnp.abs(row - (n - 1) * RT - table[:, k : k + 1]) <= SH
            near_col = jnp.abs(col - table[:, slots + k : slots + k + 1]) <= SH
            mask[...] = jnp.where(near_row & near_col & (count > k), 1.0, mask[...])


def choose(cells):
    patches = cells.shape[0]
    lane = lax.broadcasted_iota(jnp.int32, (patches, 128), 1)
    table = cells[:, 0, :]
    wide = jnp.concatenate(
        [(table[:, rank : rank + 1] == lane).astype(jnp.float32) for rank in range(2)]
        + [jnp.zeros((128 - 2 * patches, 128), jnp.float32)] * (2 * patches < 128),
        axis=0,
    )
    return jnp.transpose(wide)[0 : V * NCELL, :].astype(jnp.bfloat16)


def combine(chosen, patches, table, got, rows, put_field, left, right):
    for half, ref in enumerate((left, right)):
        for r in range(rows):
            x = jnp.concatenate(
                [
                    got[pl.ds((half * 2 + rank) * rows + r, patches, stride=4 * rows), :]
                    for rank in range(2)
                ]
                + [jnp.zeros((128 - 2 * patches, 128), jnp.float32)] * (2 * patches < 128),
                axis=0,
            )
            hi = x.astype(jnp.bfloat16)
            mid, low = split(x - hi.astype(jnp.float32))
            y = mm(chosen, jnp.concatenate([hi, mid, low], axis=1))
            ref[pl.ds(r, V * NCELL, stride=rows), :] = y[:, 0:128] + y[:, 128:256] + y[:, 256:384]
    size = NCELL * rows
    col = lax.broadcasted_iota(jnp.int32, (size, CW), 1)
    for v in range(V):
        at = slice(v * size, (v + 1) * size)
        off = jnp.broadcast_to(table[:, OFFSETS + v : OFFSETS + v + 1], (size, CW))
        a = pltpu.roll(jnp.concatenate([left[at, :], right[at, :]], axis=1), WARP, 1)
        for bit in range(4):
            a = jnp.where((off & (1 << bit)) != 0, pltpu.roll(a, CW - (1 << bit), 1), a)
        source = col + off - WARP
        put_field(v, jnp.where((source >= 0) & (source < CW), a, 0.0))


def smooth(plane, col_hi, col_lo, row_taps):
    hi, lo = split(plane)
    yh, yl = split(mm(hi, col_hi) + mm(lo, col_hi) + mm(hi, col_lo))
    outs = []
    for v in range(V):
        a = slice(v * CE, (v + 1) * CE)
        outs.append(mm(row_taps, jnp.concatenate([yh[a], yh[a], yl[a]], axis=0)))
    return outs


def front_kernel(
    slots, index, cells, stamps, image_in, variance_in, row_bands_in, cols_in, rows_in,
    science, inverse, basis, gathered, root,
    held_0, held_1, held_2, held_3, held_4, held_5, near_index, index_of, sent_image, sent_first, sent_last,
    got_image, got_first, got_last, got_cells, got_stamps, left, right, template, up, down, above, below,
    text, filt, xleft, xright, mask, half_mask, wide, wup, wdown, wabove, wbelow, weight, acc, gram,
    row_bands, cols, rows, send, recv, ring_send, ring_recv, all_send, all_recv,
    far_send, far_recv, index_send, index_recv, own,
):
    patches = cells.shape[0]
    subtiles = gathered.shape[0]
    me, sub = lax.axis_index("patch"), lax.axis_index("sub")
    peers = [lax.rem(sub + d, subtiles) for d in range(1, subtiles)]
    next_sub, last_sub = peers[0], peers[-1]
    has_above = (sub > 0).astype(jnp.float32)
    has_below = (sub < subtiles - 1).astype(jnp.float32)
    held = (held_0, held_1, held_2, held_3, held_4, held_5)
    pieces = image_in.shape[1]
    planes = patches // PLANE
    z, flat = me // PLANE, lax.rem(me, PLANE)
    after, before = lax.rem(z + 1, planes), lax.rem(z + planes - 1, planes)
    barrier = pltpu.get_barrier_semaphore()

    def greet(d, _):
        q = lax.rem(me + d, patches)
        pl.semaphore_signal(barrier, inc=1, device_id={"patch": q}, device_id_type=MESH)
        return 0

    lax.fori_loop(1, patches, greet, 0)
    for s in peers:
        pl.semaphore_signal(barrier, inc=1, device_id={"sub": s}, device_id_type=MESH)
    mine = [
        pltpu.make_async_copy(x, y, own.at[n])
        for n, (x, y) in enumerate(
            (
                (image_in.at[0], held[0].at[pl.ds(0, pieces)]),
                (variance_in.at[0], held[3].at[pl.ds(0, pieces)]),
                (index, index_of.at[0]),
                (cells.at[pl.ds(me, 1)], got_cells.at[pl.ds(me, 1)]),
                (row_bands_in, row_bands), (cols_in, cols), (rows_in, rows),
            )
        )
    ]
    for c in mine:
        c.start()
    for n in range(6):
        held[n][pieces] = jnp.zeros((CR, CW), jnp.float32)
    pl.semaphore_wait(barrier, patches - 1 + subtiles - 1)

    far = [
        pltpu.make_async_remote_copy(
            src_ref=x.at[0], dst_ref=held[3 * kind + 1 + side].at[pl.ds(0, pieces)],
            send_sem=far_send.at[2 * kind + side], recv_sem=far_recv.at[2 * kind + side],
            device_id={"patch": to * PLANE + flat}, device_id_type=MESH,
        )
        for kind, x in enumerate((image_in, variance_in))
        for side, to in enumerate((after, before))
    ]
    told = [
        pltpu.make_async_remote_copy(
            src_ref=index, dst_ref=near_index.at[side], send_sem=index_send.at[side],
            recv_sem=index_recv.at[side], device_id={"patch": to * PLANE + flat},
            device_id_type=MESH,
        )
        for side, to in enumerate((after, before))
    ]
    for c in told + far[0:2]:
        c.start()

    pairs = (
        (cells, got_cells, 1), (sent_image, got_image, BLOCK),
        (sent_first, got_first, PART), (sent_last, got_last, PART),
    )

    def rows_at(n, q):
        size = pairs[n][2]
        return pl.ds(pl.multiple_of(q * size, size), size)

    def send_to(n, block, to, source):
        src, dst, _ = pairs[n]
        pltpu.make_async_remote_copy(
            src_ref=src.at[rows_at(n, block)], dst_ref=dst.at[rows_at(n, source)],
            send_sem=send.at[n], recv_sem=recv.at[n],
            device_id={"patch": to}, device_id_type=MESH,
        ).start()

    def whole(n):
        src, dst, size = pairs[n]
        at = pl.ds(0, (patches - (1 if n == 0 else 3)) * size)
        return pltpu.make_async_remote_copy(
            src_ref=src.at[at], dst_ref=dst.at[at], send_sem=send.at[n], recv_sem=recv.at[n],
            device_id={"patch": lax.rem(me + 1, patches)}, device_id_type=MESH,
        )

    sources = [q * PLANE + flat for q in (z, before, after)]
    signs = (0, 1, planes - 1)
    half = planes // 2
    shares = ((1, half, half - 1), (1, half - 1, half))

    def first_block(kind, role):
        return PLANE * sum(shares[kind][0:role])

    def target(role, i):
        plane = lax.rem(z + signs[role] * (i // PLANE), planes)
        return plane * PLANE + lax.rem(i + flat, PLANE)

    def pack(kind, role):
        first = first_block(kind, role)

        def body(i, _):
            q = target(role, i)
            x = [held[3 * kind + role][index_of[role, 0, 2 * q + rank]] for rank in range(2)]
            if kind == 0:
                tall = [jnp.concatenate([a[:, h : h + 128] for a in x], axis=0) for h in (0, 128)]
                values = [(1, jnp.concatenate(tall, axis=0))]
            else:
                values = []
                for k in range(2):
                    cut = slice(k * RC, (k + 1) * RC)
                    tall = [jnp.concatenate([a[cut, h : h + 128] for a in x], axis=0) for h in (0, 128)]
                    values.append((2 + k, jnp.concatenate(tall, axis=0)))
            for n, value in values:
                pairs[n][0][rows_at(n, first + i), :] = value

            @pl.when(q == me)
            def _():
                for n, value in values:
                    pairs[n][1][rows_at(n, sources[role]), :] = value

            return 0

        lax.fori_loop(0, PLANE * shares[kind][role], body, 0)

    def dispatch(n, role):
        kind = min(n - 1, 1)
        first = first_block(kind, role)

        def body(i, _):
            q = target(role, i)

            @pl.when(q != me)
            def _():
                send_to(n, first + i, q, sources[role])

            return 0

        lax.fori_loop(0, PLANE * shares[kind][role], body, 0)

    def ring(n, src, dst):
        return [
            pltpu.make_async_remote_copy(
                src_ref=s, dst_ref=r, send_sem=ring_send.at[n, k], recv_sem=ring_recv.at[n, k],
                device_id={"sub": to}, device_id_type=MESH,
            )
            for k, (s, r, to) in enumerate(zip(src, dst, (next_sub, last_sub)))
        ]

    def tell_cells(d, _):
        q = lax.rem(me + d, patches)
        send_to(0, q, q, me)
        return 0

    lax.fori_loop(1, patches, tell_cells, 0)
    table_ring = ring(0, (stamps, stamps), (got_stamps.at[0], got_stamps.at[1]))
    for c in table_ring + far[2:4]:
        c.start()
    for c in mine:
        c.wait()
    pack(0, 0)
    pack(1, 0)
    dispatch(1, 0)
    moves = []
    for side, c in enumerate(told):
        c.wait()
        moves.append(pltpu.make_async_copy(near_index.at[side], index_of.at[1 + side], own.at[side]))
        moves[side].start()
    for c in moves:
        c.wait()
    for c in far[0:2]:
        c.wait_recv()
    for role in (1, 2):
        pack(0, role)
        dispatch(1, role)
    for c in far[2:4]:
        c.wait_recv()
    for role in (1, 2):
        pack(1, role)
        dispatch(2, role)
    dispatch(2, 0)
    for role in (1, 2, 0):
        dispatch(3, role)
    for c in far:
        c.wait_send()
    for c in table_ring:
        c.wait()
    stamp_mask(mask, stamps, got_stamps, sub, subtiles, slots)

    for c in range(NCELL):
        for k in range(2):
            half_mask[k, c * RC : (c + 1) * RC, :] = mask[c * CR + k * RC : c * CR + (k + 1) * RC, :]
    acc[...] = jnp.zeros_like(acc)
    for at in (slice(0, 16), slice(112, TE)):
        filt[:, at, :] = jnp.zeros((NT, 16, CW), jnp.float32)
        text[at, :] = jnp.zeros((16, CW), jnp.float32)
    for k in (NB,) + tuple(range(NB + 1 + V, XR)):
        for ref in (xleft, xright):
            ref[pl.ds(k, RT, stride=XR), :] = jnp.full((RT, 128), float(k == NB), jnp.float32)
    whole(0).wait_recv()
    whole(1).wait_recv()
    table = stamps[...]
    chosen = choose(got_cells)

    def put_science(v, field):
        science[v, SR : SR + RT, :] = field

    combine(chosen, patches, table, got_image, CR, put_science, left, right)
    inner = slice(SR, SR + RT)
    template[...] = (science[0, inner] + science[1, inner] + science[2, inner] + science[3, inner]) / V
    up[0:TH, :] = template[0:TH, :]
    down[0:TH, :] = template[RT - TH : RT, :]
    for v in range(V):
        at = TH + v * SR
        up[at : at + SR, :] = science[v, SR : 2 * SR, :]
        down[at : at + SR, :] = science[v, RT : RT + SR, :]
    rims = ring(1, (down, up), (above, below))
    for c in rims:
        c.start()
    text[32:96, :] = template[...]
    filter_columns(text, filt, (8, lambda i: i + 4))
    for c in rims:
        c.wait()
    text[8:32, :] = above[0:TH, :] * has_above
    text[96:120, :] = below[0:TH, :] * has_below
    filter_columns(text, filt, (4, lambda i: i + 2 + 8 * (i // 2)))

    def put(k, image):
        at = pl.ds(k, RT, stride=XR)
        xleft[at, :] = image[:, 0:128]
        xright[at, :] = image[:, 128:CW]

    def keep_inner(k, image):
        basis[k, SR : SR + RT, :] = image
        put(k, image)

    def keep_rim(k, image):
        basis[k, 0:SR, :] = image[0:SR, :]
        basis[k, SR + RT : CE, :] = image[SR : 2 * SR, :]

    filter_rows(row_bands, filt, 0, RT, keep_inner)
    for v in range(V):
        put(NB + 1 + v, science[v, SR : SR + RT, :])
    whole(0).wait_send()
    whole(1).wait_send()

    def invert(planes):
        q = (planes[0] + planes[1] + planes[2] + planes[3]) / (V * V)
        return [1.0 / (p + q + SKY_VAR) for p in planes]

    def put_wide(v, field):
        wide[v] = field

    wrims = ring(2, (wdown, wup), (wabove, wbelow))
    for k, got in enumerate((got_first, got_last)):
        whole(2 + k).wait_recv()
        combine(chosen, patches, table, got, RC, put_wide, left, right)
        for v in range(V):
            for c in range(SR // CR):
                at = slice(v * SR + c * CR + k * RC, v * SR + c * CR + (k + 1) * RC)
                low = NCELL - SR // CR + c
                wup[at, :] = wide[v, c * RC : (c + 1) * RC, :]
                wdown[at, :] = wide[v, low * RC : (low + 1) * RC, :]
        if k == 1:
            for c in wrims:
                c.start()
        for v, inv in enumerate(invert([wide[v] for v in range(V)])):
            weight[v] = half_mask[k] * inv
            for c in range(NCELL):
                first = v * CE + SR + c * CR + k * RC
                inverse[first : first + RC, :] = inv[c * RC : (c + 1) * RC, :]
        gram_of(k, weight, xleft, xright, acc)
    gram_total(acc, gram)
    parts = [
        pltpu.make_async_remote_copy(
            src_ref=gram, dst_ref=gathered.at[sub], send_sem=all_send.at[n], recv_sem=all_recv.at[n],
            device_id={"sub": s}, device_id_type=MESH,
        )
        for n, s in enumerate(peers)
    ]
    for c in parts:
        c.start()
    my_part = pltpu.make_async_copy(gram, gathered.at[sub], own.at[7])
    my_part.start()
    for c in wrims:
        c.wait()
    for ref, first, has in ((wabove, 0, has_above), (wbelow, SR + RT, has_below)):
        planes = [ref[v * SR : (v + 1) * SR, :] for v in range(V)]
        for v, inv in enumerate(invert(planes)):
            inverse[v * CE + first : v * CE + first + SR, :] = inv * has
    for v in range(V):
        at = TH + v * SR
        science[v, 0:SR, :] = above[at : at + SR, :] * has_above
        science[v, SR + RT : CE, :] = below[at : at + SR, :] * has_below
    filter_columns(text, filt, (2, lambda i: 1 + 13 * i))
    filter_rows(row_bands, filt, NT * RT, 2 * SR, keep_rim)
    for v, den in enumerate(smooth(inverse[...], cols[2], cols[3], rows[1])):
        root[v] = lax.rsqrt(den)
    my_part.wait()
    for n, c in enumerate(parts):
        c.wait_send()
        source = peers[subtiles - 2 - n]
        pltpu.make_async_remote_copy(
            src_ref=gram, dst_ref=gathered.at[source], send_sem=all_send.at[n],
            recv_sem=all_recv.at[n], device_id={"sub": source}, device_id_type=MESH,
        ).wait_recv()

    whole(2).wait_send()
    whole(3).wait_send()


def filter_columns(text, filt, blocks):
    taps = tap_values()
    col = lax.broadcasted_iota(jnp.int32, (8, CW), 1)

    def columns(i, _):
        rows = pl.ds(pl.multiple_of(i * 8, 8), 8)
        t = text[rows, :]
        sums = [None] * NT
        for u in range(0, KR + 1):
            if u:
                plus = jnp.where(col < CW - u, pltpu.roll(t, CW - u, 1), 0.0)
                minus = jnp.where(col >= u, pltpu.roll(t, u, 1), 0.0)
                even, odd = plus + minus, plus - minus
            first = 0
            for degree in DEGREES:
                for n in range(degree + 1):
                    j = first + n
                    h = float(np.float32(taps[j, KR + u]))
                    if u == 0:
                        sums[j] = t * h if n % 2 == 0 else None
                    else:
                        term = (even if n % 2 == 0 else odd) * h
                        sums[j] = term if sums[j] is None else sums[j] + term
                first += degree + 1
        for j in range(NT):
            filt[j, rows, :] = sums[j]
        return 0

    count, place = blocks
    lax.fori_loop(0, count, lambda i, _: columns(place(i), _), 0, unroll=2)


def filter_rows(row_bands, filt, first_row, size, keep):
    for first_tap, degree, index in members_of():
        for j in range(degree + 1):
            count = degree + 1 - j
            at = first_row + first_tap * size
            lhs = row_bands[at : at + count * size, :]
            fh, fl = split(filt[first_tap + j])
            y = mm(lhs, jnp.concatenate([fh, fh], axis=0)) + mm(lhs[:, 0:TE], fl)
            for i in range(count):
                keep(index[(i, j)], y[i * size : (i + 1) * size, :])


def gram_of(k, weight, xleft, xright, acc):
    def cell(i, _):
        lefts, rights = [], []
        for r0 in range(RC):
            r = i * CR + k * RC + r0
            at = pl.ds(pl.multiple_of(r * XR, 8), XR)
            x = jnp.concatenate([xleft[at, :], xright[at, :]], axis=1)
            xh, xl = split(x)
            rights.append(jnp.concatenate([xh, xl, jnp.zeros((32, CW), jnp.bfloat16)], axis=0))
            his, los = [], []
            for v in range(V):
                lh, ll = split(x * weight[v, pl.ds(i * RC + r0, 1), :])
                his.append(lh)
                los.append(ll)
            lefts.append(jnp.concatenate(his + los, axis=0))
        acc[...] += lax.dot_general(
            jnp.concatenate(lefts, axis=1), jnp.concatenate(rights, axis=1),
            (((1,), (1,)), ((), ())), preferred_element_type=jnp.float32,
        )
        return 0

    lax.fori_loop(0, NCELL, cell, 0, unroll=4)


def gram_total(acc, gram):
    high = acc[0 : V * XR, :]
    total = high + pltpu.roll(high, 128 - XR, 1) + acc[V * XR : 2 * V * XR, :]
    lane = lax.broadcasted_iota(jnp.int32, total.shape, 1)
    total = jnp.where(lane < XR, total, 0.0)
    gram[...] = total[0 : 2 * XR, :] + pltpu.roll(total[2 * XR : 4 * XR, :], 64, 1)


def pick(x, index):
    return jnp.take_along_axis(x, index, axis=1, mode="promise_in_bounds")


def final_kernel(
    normalizer, gathered, basis, science, inverse, root, cols_in, rows_in,
    difference, significance, coef, dplane, cols, rows, sems,
):
    copies = [
        pltpu.make_async_copy(x, y, sems.at[n])
        for n, (x, y) in enumerate(((cols_in.at[0:2], cols), (rows_in.at[0], rows)))
    ]
    for c in copies:
        c.start()
    total = gathered[0] + gathered[1] + gathered[2] + gathered[3]
    total = total * (1.0 / normalizer)
    row = lax.broadcasted_iota(jnp.int32, (XR, 128), 0)
    lane = lax.broadcasted_iota(jnp.int32, (XR, 128), 1)
    part = lane // 64
    j = lane - part * 64
    base = part * 64
    halves, scales = [], []
    for half in range(2):
        a = total[half * XR : (half + 1) * XR, :]
        v = half + 2 * part
        e_col = lax.rsqrt(pick(a, base + row) + EPS)
        diag = jnp.sum(jnp.where(row == j, a, 0.0), axis=0, keepdims=True)
        e_row = lax.rsqrt(diag + EPS)
        scaled = a * e_col
        system = jnp.where(j <= NB, scaled * e_row, jnp.where(j == NB + 1 + v, scaled, 0.0))
        system = system + jnp.where(row == j, RIDGE, 0.0)
        halves.append(system)
        scales.append(e_col)
    for k in range(0, NB, 2):
        for half in range(2):
            m = halves[half]
            top = jnp.broadcast_to(m[k : k + 1, :], (XR, 128))
            low = jnp.broadcast_to(m[k + 1 : k + 2, :], (XR, 128))
            a, b, d = pick(top, base + k), pick(top, base + k + 1), pick(low, base + k + 1)
            scale = 1.0 / (a * d - b * b)
            left, right = pick(m, base + k), pick(m, base + k + 1)
            left = jnp.where(row == k, a - 1.0, left)
            right = jnp.where(row == k + 1, d - 1.0, right)
            halves[half] = m - left * ((d * top - b * low) * scale) - right * ((a * low - b * top) * scale)
    for k in (NB,):
        for half in range(2):
            a = halves[half]
            pivot_row = jnp.broadcast_to(a[k : k + 1, :], (XR, 128))
            pivot = pick(pivot_row, base + k)
            column = pick(a, base + k)
            column = jnp.where(row == k, pivot - 1.0, column)
            halves[half] = a - column * (pivot_row / pivot)
    for half in range(2):
        v = half + 2 * part
        a = pick(halves[half], base + NB + 1 + v) * scales[half]
        coef[half * XR : (half + 1) * XR, :] = pick(a, lane * 0)
        coef[(half + 2) * XR : (half + 3) * XR, :] = pick(a, lane * 0 + 64)

    def block(b, _):
        at = pl.ds(pl.multiple_of(b * 8, 8), 8)
        sums = []
        for v in range(V):
            a = coef[v * XR + NB : v * XR + NB + 1, :]
            sums.append(science[v, at, :] - jnp.concatenate([a, a], axis=1))
        for k in range(NB):
            c = basis[k, at, :]
            for v in range(V):
                a = coef[v * XR + k : v * XR + k + 1, :]
                sums[v] = sums[v] - c * jnp.concatenate([a, a], axis=1)
        for v in range(V):
            plane = pl.ds(pl.multiple_of(v * CE + b * 8, 8), 8)
            dplane[plane, :] = sums[v] * inverse[plane, :]

        @pl.when((b >= SR // 8) & (b < (SR + RT) // 8))
        def _():
            inner = pl.ds(pl.multiple_of(b * 8 - SR, 8), 8)
            for v in range(V):
                difference[v, inner, :] = sums[v]

        return 0

    lax.fori_loop(0, CE // 8, block, 0)
    for c in copies:
        c.wait()
    for v, num in enumerate(smooth(dplane[...], cols[0], cols[1], rows[...])):
        significance[v] = num * root[v]


def shape(*dims, dtype=jnp.float32):
    return jax.ShapeDtypeStruct(dims, dtype)


def params(**more):
    return pltpu.CompilerParams(vmem_limit_bytes=VMEM_LIMIT, **more)


def local(
    pieces_image, pieces_variance, piece_patch, piece_cell,
    stamp_row, stamp_col, stamp_count, warp_offsets,
):
    patches = lax.axis_size("patch")
    subtiles = lax.axis_size("sub")
    pieces = pieces_image.shape[1]
    slots = stamp_row.shape[1]
    dma, vmem, smem = pltpu.SemaphoreType.DMA, pltpu.VMEM, pltpu.SMEM
    far = pl.BlockSpec(memory_space=pltpu.HBM)

    def keep(*arrays):
        return [pltpu.with_memory_space_constraint(a, pltpu.HBM) for a in arrays]

    f32, i32, bf16 = jnp.float32, jnp.int32, jnp.bfloat16

    sent_shape, part_shape = vmem((patches * BLOCK, 128), f32), vmem((patches * PART, 128), f32)
    pieces_image, pieces_variance = keep(pieces_image, pieces_variance)
    line = shape(1, 128, dtype=i32)
    index, sent_cell, table = pl.pallas_call(
        plan_kernel,
        out_shape=(line, shape(patches, 1, 128, dtype=i32), line),
        in_specs=[far] * 5 + [SCALARS],
        out_specs=(WHOLE,) * 3,
        scratch_shapes=[
            smem((pieces,), i32), smem((pieces,), i32),
            smem((1, slots), i32), smem((1, slots), i32), smem((V,), i32),
            smem((patches,), i32), smem((2 * patches,), i32), smem((2 * patches,), i32), dma((5,)),
        ],
        compiler_params=params(),
        name="plan",
    )(
        *keep(
            piece_patch.reshape(-1), piece_cell.reshape(-1), stamp_row, stamp_col, warp_offsets,
        ),
        stamp_count,
    )

    row_bands, cols, rows = keep(*[jnp.asarray(x) for x in constants()])
    rim, small_rim = vmem((HALO, CW), f32), vmem((V * SR, CW), f32)
    field = shape(V, RT, CW)
    science, inverse, basis, gathered, root = pl.pallas_call(
        functools.partial(front_kernel, slots),
        out_shape=(
            shape(V, CE, CW), shape(V * CE, CW), shape(NB, CE, CW), shape(subtiles, 2 * XR, 128), field,
        ),
        in_specs=[WHOLE] * 3 + [far] * 5,
        out_specs=(WHOLE,) * 5,
        scratch_shapes=[
            *[vmem((pieces + 1, CR, CW), f32)] * 6, vmem((2, 1, 128), i32), smem((3, 1, 128), i32),
            sent_shape, part_shape, part_shape, sent_shape, part_shape, part_shape,
            vmem((patches, 1, 128), i32), vmem((2, 1, 128), i32),
            vmem((V * RT, 128), f32), vmem((V * RT, 128), f32), vmem((RT, CW), f32),
            rim, rim, rim, rim,
            vmem((TE, CW), f32), vmem((NT, TE, CW), f32),
            vmem((RT * XR, 128), f32), vmem((RT * XR, 128), f32), vmem((RT, CW), f32),
            vmem((2, NCELL * RC, CW), f32), vmem((V, NCELL * RC, CW), f32), small_rim, small_rim, small_rim, small_rim,
            vmem((V, NCELL * RC, CW), f32), vmem((2 * V * XR, 128), f32), vmem((2 * XR, 128), f32),
            vmem(row_bands.shape, bf16), vmem(cols.shape, bf16), vmem(rows.shape, bf16),
            dma((4,)), dma((4,)), dma((3, 2)), dma((3, 2)),
            dma((subtiles - 1,)), dma((subtiles - 1,)),
            dma((4,)), dma((4,)), dma((2,)), dma((2,)), dma((8,)),
        ],
        compiler_params=pltpu.CompilerParams(
            vmem_limit_bytes=32 * 1024 * 1024, collective_id=0, has_side_effects=True
        ),
        name="front",
    )(index, sent_cell, table, pieces_image, pieces_variance, row_bands, cols, rows)

    normalizer = float(subtiles * slots * (2 * SH + 1) ** 2)
    difference, significance = pl.pallas_call(
        functools.partial(final_kernel, normalizer),
        out_shape=(field, field),
        in_specs=[WHOLE] * 5 + [far] * 2,
        out_specs=(WHOLE,) * 2,
        scratch_shapes=[
            vmem((V * XR, 128), f32), vmem((V * CE, CW), f32),
            vmem((2, CW, CW), bf16), vmem(rows.shape[1:], bf16), dma((2,)),
        ],
        compiler_params=params(),
        name="final",
    )(gathered, basis, science, inverse, root, cols, rows)
    return (difference[:, None], significance[:, None])


def solution(mesh):
    in_specs = (
        P("sub", "patch", None, None),
        P("sub", "patch", None, None),
        P("sub", "patch", None),
        P("sub", "patch"),
        P("patch", "sub"),
        P("patch", "sub"),
        P("patch", "sub"),
        P(),
    )
    out_specs = (P(None, "patch", "sub", None), P(None, "patch", "sub", None))
    return jax.shard_map(local, mesh=mesh, in_specs=in_specs, out_specs=out_specs, check_vma=False)
```

```python
import functools
import math

import jax
import jax.numpy as jnp
import numpy as np
from jax import lax
from jax.experimental import pallas as pl
from jax.experimental.pallas import tpu as pltpu
from jax.sharding import PartitionSpec as P

V = 4
NCELL = 8
CR = 8
RT = 64
CW = 256
KR = 10
PR = 10
SH = 15
WARP = 4
NB = 40
NP = 32
SIGMAS = (0.75, 1.5, 3.0)
DEGREES = (4, 4, 3)
PSF_SIGMA = 2.0
SKY_VAR = 0.1
RIDGE = 0.5
EPS = 1e-05
MESH = pl.DeviceIdType.MESH

NT = 14
XR = 48
TE = 128
CE = 96
TH = 24
SR = 16
HALO = TH + V * SR
BLOCK = 4 * CR
RC = CR // 2
PART = 4 * RC
PLANE = 8
NS = 12
OFFSETS = 2 * NS + 1
VMEM_LIMIT = 16 * 1024 * 1024
WHOLE = pl.BlockSpec(memory_space=pltpu.VMEM)
SCALARS = pl.BlockSpec(memory_space=pltpu.SMEM)


def tap_values():
    u = np.arange(-KR, KR + 1).astype(np.float64)
    rows = []
    for sigma, degree in zip(SIGMAS, DEGREES):
        t = u / sigma
        env = np.exp(-0.5 * t * t)
        he = [np.ones_like(t), t]
        for n in range(1, degree):
            he.append(t * he[n] - n * he[n - 1])
        for n in range(degree + 1):
            h = he[n] * env
            rows.append(h / np.sqrt(np.sum(h * h)))
    return np.stack(rows)


def psf_values():
    u = np.arange(-PR, PR + 1).astype(np.float64)
    g = np.exp(-0.5 * (u / PSF_SIGMA) ** 2)
    return g / g.sum()


def split_np(a):
    a = a.astype(np.float32)
    hi = a.astype(jnp.bfloat16)
    lo = (a - hi.astype(np.float32)).astype(jnp.bfloat16)
    return hi, lo


def band(taps, rows, cols, first):
    radius = (len(taps) - 1) // 2
    out = np.zeros((rows, cols))
    for r in range(rows):
        for u in range(-radius, radius + 1):
            c = r + first + u
            if 0 <= c < cols:
                out[r, c] = taps[u + radius]
    return out


def constants():
    taps = tap_values()
    every = [band(taps[j], CE, TE, SR) for j in range(NT)]
    bands = np.concatenate(
        [b[SR : SR + RT] for b in every]
        + [np.concatenate([b[0:SR], b[SR + RT : CE]], axis=0) for b in every],
        axis=0,
    )
    hi, lo = split_np(bands)
    row_bands = np.concatenate([hi, lo], axis=1)
    p = psf_values()
    cols, rows = [], []
    for f in (p, p * p):
        cols += list(split_np(band(f, CW, CW, 0)))
        h, l = split_np(band(f, RT, CE, SR))
        rows.append(np.concatenate([h, l, h], axis=1))
    return row_bands, np.stack(cols), np.stack(rows)


def members_of():
    result, first_tap, first = [], 0, 0
    for degree in DEGREES:
        index = {}
        for i in range(degree + 1):
            for j in range(degree + 1 - i):
                index[(i, j)] = first + len(index)
        result.append((first_tap, degree, index))
        first_tap += degree + 1
        first += len(index)
    return result


def split(x):
    hi = x.astype(jnp.bfloat16)
    return hi, (x - hi.astype(jnp.float32)).astype(jnp.bfloat16)


def mm(a, b):
    return jnp.dot(a, b, preferred_element_type=jnp.float32)


def plan_kernel(
    patch, cell, row, col, warp, live,
    out_index, out_cell, table,
    patch_in, cell_in, row_in, col_in, warp_in, count, slot_cell, slot_index, sems,
):
    patches = out_cell.shape[0]
    pieces = patch.shape[0]
    slots = row.shape[1]
    pairs = ((patch, patch_in), (cell, cell_in), (row, row_in), (col, col_in), (warp, warp_in))
    copies = [pltpu.make_async_copy(x, y, sems.at[n]) for n, (x, y) in enumerate(pairs)]
    for c in copies:
        c.start()

    def clear(n, _):
        count[n] = 0
        for rank in range(2):
            slot_cell[2 * n + rank] = -1
            slot_index[2 * n + rank] = pieces
        return 0

    lax.fori_loop(0, patches, clear, 0)
    for c in copies:
        c.wait()

    def place(n, _):
        q = patch_in[n]
        rank = count[q]
        count[q] = rank + 1
        slot_cell[2 * q + rank] = cell_in[n]
        slot_index[2 * q + rank] = n
        return 0

    lax.fori_loop(0, pieces, place, 0)
    lane = lax.broadcasted_iota(jnp.int32, (1, 128), 1)

    def tell(q, line):
        out_cell[q] = jnp.where(lane == 0, slot_cell[2 * q], slot_cell[2 * q + 1])
        line = jnp.where(lane == 2 * q, slot_index[2 * q], line)
        return jnp.where(lane == 2 * q + 1, slot_index[2 * q + 1], line)

    out_index[...] = lax.fori_loop(0, patches, tell, jnp.zeros((1, 128), jnp.int32))
    values = [row_in[0, n] for n in range(slots)] + [col_in[0, n] for n in range(slots)]
    values += [live[0, 0]] + [warp_in[v] for v in range(V)]
    line = jnp.zeros((1, 128), jnp.int32)
    for n, value in enumerate(values):
        line = jnp.where(lane == n, value, line)
    table[...] = line


def stamp_mask(mask, stamps, got_stamps, sub, subtiles, slots):
    row = lax.broadcasted_iota(jnp.int32, (RT, CW), 0)
    col = lax.broadcasted_iota(jnp.int32, (RT, CW), 1)
    flags = [(sub > 0).astype(jnp.int32), 1, (sub < subtiles - 1).astype(jnp.int32)]
    mask[...] = jnp.zeros_like(mask)
    for n, (flag, table) in enumerate(zip(flags, (got_stamps[0], stamps[...], got_stamps[1]))):
        count = table[:, 2 * slots : 2 * slots + 1] * flag
        for k in range(slots):
            near_row = jnp.abs(row - (n - 1) * RT - table[:, k : k + 1]) <= SH
            near_col = jnp.abs(col - table[:, slots + k : slots + k + 1]) <= SH
            mask[...] = jnp.where(near_row & near_col & (count > k), 1.0, mask[...])


def choose(cells):
    patches = cells.shape[0]
    lane = lax.broadcasted_iota(jnp.int32, (patches, 128), 1)
    table = cells[:, 0, :]
    wide = jnp.concatenate(
        [(table[:, rank : rank + 1] == lane).astype(jnp.float32) for rank in range(2)]
        + [jnp.zeros((128 - 2 * patches, 128), jnp.float32)] * (2 * patches < 128),
        axis=0,
    )
    return jnp.transpose(wide)[0 : V * NCELL, :].astype(jnp.bfloat16)


def combine(chosen, patches, table, got, rows, put_field, left, right):
    for half, ref in enumerate((left, right)):
        for r in range(rows):
            x = jnp.concatenate(
                [
                    got[pl.ds((half * 2 + rank) * rows + r, patches, stride=4 * rows), :]
                    for rank in range(2)
                ]
                + [jnp.zeros((128 - 2 * patches, 128), jnp.float32)] * (2 * patches < 128),
                axis=0,
            )
            hi = x.astype(jnp.bfloat16)
            mid, low = split(x - hi.astype(jnp.float32))
            y = mm(chosen, jnp.concatenate([hi, mid, low], axis=1))
            ref[pl.ds(r, V * NCELL, stride=rows), :] = y[:, 0:128] + y[:, 128:256] + y[:, 256:384]
    size = NCELL * rows
    col = lax.broadcasted_iota(jnp.int32, (size, CW), 1)
    for v in range(V):
        at = slice(v * size, (v + 1) * size)
        off = jnp.broadcast_to(table[:, OFFSETS + v : OFFSETS + v + 1], (size, CW))
        a = pltpu.roll(jnp.concatenate([left[at, :], right[at, :]], axis=1), WARP, 1)
        for bit in range(4):
            a = jnp.where((off & (1 << bit)) != 0, pltpu.roll(a, CW - (1 << bit), 1), a)
        source = col + off - WARP
        put_field(v, jnp.where((source >= 0) & (source < CW), a, 0.0))


def smooth(plane, col_hi, col_lo, row_taps):
    hi, lo = split(plane)
    yh, yl = split(mm(hi, col_hi) + mm(lo, col_hi) + mm(hi, col_lo))
    outs = []
    for v in range(V):
        a = slice(v * CE, (v + 1) * CE)
        outs.append(mm(row_taps, jnp.concatenate([yh[a], yh[a], yl[a]], axis=0)))
    return outs


def front_kernel(
    slots, index, cells, stamps, image_in, variance_in, row_bands_in, cols_in, rows_in,
    science, inverse, basis, gathered, root,
    held_0, held_1, held_2, held_3, held_4, held_5, near_index, index_of, sent_image, sent_first, sent_last,
    got_image, got_first, got_last, got_cells, got_stamps, left, right, template, up, down, above, below,
    text, filt, xleft, xright, mask, half_mask, wide, wup, wdown, wabove, wbelow, weight, acc, gram,
    row_bands, cols, rows, send, recv, ring_send, ring_recv, all_send, all_recv,
    far_send, far_recv, index_send, index_recv, own,
):
    patches = cells.shape[0]
    subtiles = gathered.shape[0]
    me, sub = lax.axis_index("patch"), lax.axis_index("sub")
    peers = [lax.rem(sub + d, subtiles) for d in range(1, subtiles)]
    next_sub, last_sub = peers[0], peers[-1]
    has_above = (sub > 0).astype(jnp.float32)
    has_below = (sub < subtiles - 1).astype(jnp.float32)
    held = (held_0, held_1, held_2, held_3, held_4, held_5)
    pieces = image_in.shape[1]
    planes = patches // PLANE
    z, flat = me // PLANE, lax.rem(me, PLANE)
    after, before = lax.rem(z + 1, planes), lax.rem(z + planes - 1, planes)
    barrier = pltpu.get_barrier_semaphore()

    def greet(d, _):
        q = lax.rem(me + d, patches)
        pl.semaphore_signal(barrier, inc=1, device_id={"patch": q}, device_id_type=MESH)
        return 0

    lax.fori_loop(1, patches, greet, 0, unroll=9)
    for s in peers:
        pl.semaphore_signal(barrier, inc=1, device_id={"sub": s}, device_id_type=MESH)
    mine = [
        pltpu.make_async_copy(x, y, own.at[n])
        for n, (x, y) in enumerate(
            (
                (image_in.at[0], held[0].at[pl.ds(0, pieces)]),
                (variance_in.at[0], held[3].at[pl.ds(0, pieces)]),
                (index, index_of.at[0]),
                (cells.at[pl.ds(me, 1)], got_cells.at[pl.ds(me, 1)]),
                (row_bands_in, row_bands), (cols_in, cols), (rows_in, rows),
            )
        )
    ]
    for c in mine:
        c.start()
    for n in range(6):
        held[n][pieces] = jnp.zeros((CR, CW), jnp.float32)
    pl.semaphore_wait(barrier, patches - 1 + subtiles - 1)

    far = [
        pltpu.make_async_remote_copy(
            src_ref=x.at[0], dst_ref=held[3 * kind + 1 + side].at[pl.ds(0, pieces)],
            send_sem=far_send.at[2 * kind + side], recv_sem=far_recv.at[2 * kind + side],
            device_id={"patch": to * PLANE + flat}, device_id_type=MESH,
        )
        for kind, x in enumerate((image_in, variance_in))
        for side, to in enumerate((after, before))
    ]
    told = [
        pltpu.make_async_remote_copy(
            src_ref=index, dst_ref=near_index.at[side], send_sem=index_send.at[side],
            recv_sem=index_recv.at[side], device_id={"patch": to * PLANE + flat},
            device_id_type=MESH,
        )
        for side, to in enumerate((after, before))
    ]
    for c in told + far[0:2]:
        c.start()

    pairs = (
        (cells, got_cells, 1), (sent_image, got_image, BLOCK),
        (sent_first, got_first, PART), (sent_last, got_last, PART),
    )

    def rows_at(n, q):
        size = pairs[n][2]
        return pl.ds(pl.multiple_of(q * size, size), size)

    def send_to(n, block, to, source):
        src, dst, _ = pairs[n]
        pltpu.make_async_remote_copy(
            src_ref=src.at[rows_at(n, block)], dst_ref=dst.at[rows_at(n, source)],
            send_sem=send.at[n], recv_sem=recv.at[n],
            device_id={"patch": to}, device_id_type=MESH,
        ).start()

    def whole(n):
        src, dst, size = pairs[n]
        at = pl.ds(0, (patches - (1 if n == 0 else 3)) * size)
        return pltpu.make_async_remote_copy(
            src_ref=src.at[at], dst_ref=dst.at[at], send_sem=send.at[n], recv_sem=recv.at[n],
            device_id={"patch": lax.rem(me + 1, patches)}, device_id_type=MESH,
        )

    sources = [q * PLANE + flat for q in (z, before, after)]
    signs = (0, 1, planes - 1)
    half = planes // 2
    shares = ((1, half, half - 1), (1, half - 1, half))

    def first_block(kind, role):
        return PLANE * sum(shares[kind][0:role])

    def target(role, i):
        plane = lax.rem(z + signs[role] * (i // PLANE), planes)
        return plane * PLANE + lax.rem(i + flat, PLANE)

    def pack(kind, role):
        first = first_block(kind, role)

        def body(i, _):
            q = target(role, i)
            x = [held[3 * kind + role][index_of[role, 0, 2 * q + rank]] for rank in range(2)]
            if kind == 0:
                tall = [jnp.concatenate([a[:, h : h + 128] for a in x], axis=0) for h in (0, 128)]
                values = [(1, jnp.concatenate(tall, axis=0))]
            else:
                values = []
                for k in range(2):
                    cut = slice(k * RC, (k + 1) * RC)
                    tall = [jnp.concatenate([a[cut, h : h + 128] for a in x], axis=0) for h in (0, 128)]
                    values.append((2 + k, jnp.concatenate(tall, axis=0)))
            for n, value in values:
                pairs[n][0][rows_at(n, first + i), :] = value

            @pl.when(q == me)
            def _():
                for n, value in values:
                    pairs[n][1][rows_at(n, sources[role]), :] = value

            return 0

        lax.fori_loop(0, PLANE * shares[kind][role], body, 0)

    def dispatch(n, role):
        kind = min(n - 1, 1)
        first = first_block(kind, role)

        def body(i, _):
            q = target(role, i)

            @pl.when(q != me)
            def _():
                send_to(n, first + i, q, sources[role])

            return 0

        lax.fori_loop(0, PLANE * shares[kind][role], body, 0, unroll=4)

    def ring(n, src, dst):
        return [
            pltpu.make_async_remote_copy(
                src_ref=s, dst_ref=r, send_sem=ring_send.at[n, k], recv_sem=ring_recv.at[n, k],
                device_id={"sub": to}, device_id_type=MESH,
            )
            for k, (s, r, to) in enumerate(zip(src, dst, (next_sub, last_sub)))
        ]

    def tell_cells(d, _):
        q = lax.rem(me + d, patches)
        send_to(0, q, q, me)
        return 0

    table_ring = ring(0, (stamps, stamps), (got_stamps.at[0], got_stamps.at[1]))
    for c in table_ring + far[2:4]:
        c.start()
    for c in mine:
        c.wait()
    pack(0, 0)
    lax.fori_loop(1, patches, tell_cells, 0, unroll=9)
    pack(1, 0)
    dispatch(1, 0)
    moves = []
    for side, c in enumerate(told):
        c.wait()
        moves.append(pltpu.make_async_copy(near_index.at[side], index_of.at[1 + side], own.at[side]))
        moves[side].start()
    for c in moves:
        c.wait()
    for c in far[0:2]:
        c.wait_recv()
    for role in (1, 2):
        pack(0, role)
        dispatch(1, role)
    for c in far[2:4]:
        c.wait_recv()
    for role in (1, 2):
        pack(1, role)
        dispatch(2, role)
    dispatch(2, 0)
    for role in (1, 2, 0):
        dispatch(3, role)
    for c in far:
        c.wait_send()
    for c in table_ring:
        c.wait()
    stamp_mask(mask, stamps, got_stamps, sub, subtiles, slots)

    for c in range(NCELL):
        for k in range(2):
            half_mask[k, c * RC : (c + 1) * RC, :] = mask[c * CR + k * RC : c * CR + (k + 1) * RC, :]
    acc[...] = jnp.zeros_like(acc)
    for at in (slice(0, 16), slice(112, TE)):
        filt[:, at, :] = jnp.zeros((NT, 16, CW), jnp.float32)
        text[at, :] = jnp.zeros((16, CW), jnp.float32)
    for k in (NB,) + tuple(range(NB + 1 + V, XR)):
        for ref in (xleft, xright):
            ref[pl.ds(k, RT, stride=XR), :] = jnp.full((RT, 128), float(k == NB), jnp.float32)
    whole(0).wait_recv()
    whole(1).wait_recv()
    table = stamps[...]
    chosen = choose(got_cells)

    def put_science(v, field):
        science[v, SR : SR + RT, :] = field

    combine(chosen, patches, table, got_image, CR, put_science, left, right)
    inner = slice(SR, SR + RT)
    template[...] = (science[0, inner] + science[1, inner] + science[2, inner] + science[3, inner]) / V
    up[0:TH, :] = template[0:TH, :]
    down[0:TH, :] = template[RT - TH : RT, :]
    for v in range(V):
        at = TH + v * SR
        up[at : at + SR, :] = science[v, SR : 2 * SR, :]
        down[at : at + SR, :] = science[v, RT : RT + SR, :]
    rims = ring(1, (down, up), (above, below))
    for c in rims:
        c.start()
    text[32:96, :] = template[...]
    filter_columns(text, filt, (8, lambda i: i + 4))
    for c in rims:
        c.wait()
    text[8:32, :] = above[0:TH, :] * has_above
    text[96:120, :] = below[0:TH, :] * has_below
    filter_columns(text, filt, (4, lambda i: i + 2 + 8 * (i // 2)))

    def put(k, image):
        at = pl.ds(k, RT, stride=XR)
        xleft[at, :] = image[:, 0:128]
        xright[at, :] = image[:, 128:CW]

    def keep_inner(k, image):
        basis[k, SR : SR + RT, :] = image
        put(k, image)

    def keep_rim(k, image):
        basis[k, 0:SR, :] = image[0:SR, :]
        basis[k, SR + RT : CE, :] = image[SR : 2 * SR, :]

    filter_rows(row_bands, filt, 0, RT, keep_inner)
    for v in range(V):
        put(NB + 1 + v, science[v, SR : SR + RT, :])
    whole(0).wait_send()
    whole(1).wait_send()

    def invert(planes):
        q = (planes[0] + planes[1] + planes[2] + planes[3]) / (V * V)
        return [1.0 / (p + q + SKY_VAR) for p in planes]

    def put_wide(v, field):
        wide[v] = field

    wrims = ring(2, (wdown, wup), (wabove, wbelow))
    for k, got in enumerate((got_first, got_last)):
        whole(2 + k).wait_recv()
        combine(chosen, patches, table, got, RC, put_wide, left, right)
        for v in range(V):
            for c in range(SR // CR):
                at = slice(v * SR + c * CR + k * RC, v * SR + c * CR + (k + 1) * RC)
                low = NCELL - SR // CR + c
                wup[at, :] = wide[v, c * RC : (c + 1) * RC, :]
                wdown[at, :] = wide[v, low * RC : (low + 1) * RC, :]
        if k == 1:
            for c in wrims:
                c.start()
        for v, inv in enumerate(invert([wide[v] for v in range(V)])):
            weight[v] = half_mask[k] * inv
            for c in range(NCELL):
                first = v * CE + SR + c * CR + k * RC
                inverse[first : first + RC, :] = inv[c * RC : (c + 1) * RC, :]
        gram_of(k, weight, xleft, xright, acc)
    gram_total(acc, gram)
    parts = [
        pltpu.make_async_remote_copy(
            src_ref=gram, dst_ref=gathered.at[sub], send_sem=all_send.at[n], recv_sem=all_recv.at[n],
            device_id={"sub": s}, device_id_type=MESH,
        )
        for n, s in enumerate(peers)
    ]
    for c in parts:
        c.start()
    my_part = pltpu.make_async_copy(gram, gathered.at[sub], own.at[7])
    my_part.start()
    for c in wrims:
        c.wait()
    for ref, first, has in ((wabove, 0, has_above), (wbelow, SR + RT, has_below)):
        planes = [ref[v * SR : (v + 1) * SR, :] for v in range(V)]
        for v, inv in enumerate(invert(planes)):
            inverse[v * CE + first : v * CE + first + SR, :] = inv * has
    for v in range(V):
        at = TH + v * SR
        science[v, 0:SR, :] = above[at : at + SR, :] * has_above
        science[v, SR + RT : CE, :] = below[at : at + SR, :] * has_below
    filter_columns(text, filt, (2, lambda i: 1 + 13 * i))
    filter_rows(row_bands, filt, NT * RT, 2 * SR, keep_rim)
    for v, den in enumerate(smooth(inverse[...], cols[2], cols[3], rows[1])):
        root[v] = lax.rsqrt(den)
    my_part.wait()
    for n, c in enumerate(parts):
        c.wait_send()
        source = peers[subtiles - 2 - n]
        pltpu.make_async_remote_copy(
            src_ref=gram, dst_ref=gathered.at[source], send_sem=all_send.at[n],
            recv_sem=all_recv.at[n], device_id={"sub": source}, device_id_type=MESH,
        ).wait_recv()

    whole(2).wait_send()
    whole(3).wait_send()


def filter_columns(text, filt, blocks):
    taps = tap_values()
    col = lax.broadcasted_iota(jnp.int32, (8, CW), 1)

    def columns(i, _):
        rows = pl.ds(pl.multiple_of(i * 8, 8), 8)
        t = text[rows, :]
        sums = [None] * NT
        for u in range(0, KR + 1):
            if u:
                plus = jnp.where(col < CW - u, pltpu.roll(t, CW - u, 1), 0.0)
                minus = jnp.where(col >= u, pltpu.roll(t, u, 1), 0.0)
                even, odd = plus + minus, plus - minus
            first = 0
            for degree in DEGREES:
                for n in range(degree + 1):
                    j = first + n
                    h = float(np.float32(taps[j, KR + u]))
                    if u == 0:
                        sums[j] = t * h if n % 2 == 0 else None
                    else:
                        term = (even if n % 2 == 0 else odd) * h
                        sums[j] = term if sums[j] is None else sums[j] + term
                first += degree + 1
        for j in range(NT):
            filt[j, rows, :] = sums[j]
        return 0

    count, place = blocks
    lax.fori_loop(0, count, lambda i, _: columns(place(i), _), 0, unroll=2)


def filter_rows(row_bands, filt, first_row, size, keep):
    for first_tap, degree, index in members_of():
        for j in range(degree + 1):
            count = degree + 1 - j
            at = first_row + first_tap * size
            lhs = row_bands[at : at + count * size, :]
            fh, fl = split(filt[first_tap + j])
            y = mm(lhs, jnp.concatenate([fh, fh], axis=0)) + mm(lhs[:, 0:TE], fl)
            for i in range(count):
                keep(index[(i, j)], y[i * size : (i + 1) * size, :])


def gram_of(k, weight, xleft, xright, acc):
    def cell(i, _):
        lefts, rights = [], []
        for r0 in range(RC):
            r = i * CR + k * RC + r0
            at = pl.ds(pl.multiple_of(r * XR, 8), XR)
            x = jnp.concatenate([xleft[at, :], xright[at, :]], axis=1)
            xh, xl = split(x)
            rights.append(jnp.concatenate([xh, xl, jnp.zeros((32, CW), jnp.bfloat16)], axis=0))
            his, los = [], []
            for v in range(V):
                lh, ll = split(x * weight[v, pl.ds(i * RC + r0, 1), :])
                his.append(lh)
                los.append(ll)
            lefts.append(jnp.concatenate(his + los, axis=0))
        acc[...] += lax.dot_general(
            jnp.concatenate(lefts, axis=1), jnp.concatenate(rights, axis=1),
            (((1,), (1,)), ((), ())), preferred_element_type=jnp.float32,
        )
        return 0

    lax.fori_loop(0, NCELL, cell, 0, unroll=4)


def gram_total(acc, gram):
    high = acc[0 : V * XR, :]
    total = high + pltpu.roll(high, 128 - XR, 1) + acc[V * XR : 2 * V * XR, :]
    lane = lax.broadcasted_iota(jnp.int32, total.shape, 1)
    total = jnp.where(lane < XR, total, 0.0)
    gram[...] = total[0 : 2 * XR, :] + pltpu.roll(total[2 * XR : 4 * XR, :], 64, 1)


def pick(x, index):
    return jnp.take_along_axis(x, index, axis=1, mode="promise_in_bounds")


def final_kernel(
    normalizer, gathered, basis, science, inverse, root, cols_in, rows_in,
    difference, significance, coef, dplane, cols, rows, sems,
):
    copies = [
        pltpu.make_async_copy(x, y, sems.at[n])
        for n, (x, y) in enumerate(((cols_in.at[0:2], cols), (rows_in.at[0], rows)))
    ]
    for c in copies:
        c.start()
    total = gathered[0] + gathered[1] + gathered[2] + gathered[3]
    total = total * (1.0 / normalizer)
    row = lax.broadcasted_iota(jnp.int32, (XR, 128), 0)
    lane = lax.broadcasted_iota(jnp.int32, (XR, 128), 1)
    part = lane // 64
    j = lane - part * 64
    base = part * 64
    halves, scales = [], []
    for half in range(2):
        a = total[half * XR : (half + 1) * XR, :]
        v = half + 2 * part
        e_col = lax.rsqrt(pick(a, base + row) + EPS)
        diag = jnp.sum(jnp.where(row == j, a, 0.0), axis=0, keepdims=True)
        e_row = lax.rsqrt(diag + EPS)
        scaled = a * e_col
        system = jnp.where(j <= NB, scaled * e_row, jnp.where(j == NB + 1 + v, scaled, 0.0))
        system = system + jnp.where(row == j, RIDGE, 0.0)
        halves.append(system)
        scales.append(e_col)
    for k in range(0, NB, 2):
        for half in range(2):
            m = halves[half]
            top = jnp.broadcast_to(m[k : k + 1, :], (XR, 128))
            low = jnp.broadcast_to(m[k + 1 : k + 2, :], (XR, 128))
            a, b, d = pick(top, base + k), pick(top, base + k + 1), pick(low, base + k + 1)
            scale = 1.0 / (a * d - b * b)
            left, right = pick(m, base + k), pick(m, base + k + 1)
            left = jnp.where(row == k, a - 1.0, left)
            right = jnp.where(row == k + 1, d - 1.0, right)
            halves[half] = m - left * ((d * top - b * low) * scale) - right * ((a * low - b * top) * scale)
    for k in (NB,):
        for half in range(2):
            a = halves[half]
            pivot_row = jnp.broadcast_to(a[k : k + 1, :], (XR, 128))
            pivot = pick(pivot_row, base + k)
            column = pick(a, base + k)
            column = jnp.where(row == k, pivot - 1.0, column)
            halves[half] = a - column * (pivot_row / pivot)
    for half in range(2):
        v = half + 2 * part
        a = pick(halves[half], base + NB + 1 + v) * scales[half]
        coef[half * XR : (half + 1) * XR, :] = pick(a, lane * 0)
        coef[(half + 2) * XR : (half + 3) * XR, :] = pick(a, lane * 0 + 64)

    def block(b, _):
        at = pl.ds(pl.multiple_of(b * 8, 8), 8)
        sums = []
        for v in range(V):
            a = coef[v * XR + NB : v * XR + NB + 1, :]
            sums.append(science[v, at, :] - jnp.concatenate([a, a], axis=1))
        for k in range(NB):
            c = basis[k, at, :]
            for v in range(V):
                a = coef[v * XR + k : v * XR + k + 1, :]
                sums[v] = sums[v] - c * jnp.concatenate([a, a], axis=1)
        for v in range(V):
            plane = pl.ds(pl.multiple_of(v * CE + b * 8, 8), 8)
            dplane[plane, :] = sums[v] * inverse[plane, :]

        @pl.when((b >= SR // 8) & (b < (SR + RT) // 8))
        def _():
            inner = pl.ds(pl.multiple_of(b * 8 - SR, 8), 8)
            for v in range(V):
                difference[v, inner, :] = sums[v]

        return 0

    lax.fori_loop(0, CE // 8, block, 0)
    for c in copies:
        c.wait()
    for v, num in enumerate(smooth(dplane[...], cols[0], cols[1], rows[...])):
        significance[v] = num * root[v]


def shape(*dims, dtype=jnp.float32):
    return jax.ShapeDtypeStruct(dims, dtype)


def params(**more):
    return pltpu.CompilerParams(vmem_limit_bytes=VMEM_LIMIT, **more)


def local(
    pieces_image, pieces_variance, piece_patch, piece_cell,
    stamp_row, stamp_col, stamp_count, warp_offsets,
):
    patches = lax.axis_size("patch")
    subtiles = lax.axis_size("sub")
    pieces = pieces_image.shape[1]
    slots = stamp_row.shape[1]
    dma, vmem, smem = pltpu.SemaphoreType.DMA, pltpu.VMEM, pltpu.SMEM
    far = pl.BlockSpec(memory_space=pltpu.HBM)

    def keep(*arrays):
        return [pltpu.with_memory_space_constraint(a, pltpu.HBM) for a in arrays]

    f32, i32, bf16 = jnp.float32, jnp.int32, jnp.bfloat16

    sent_shape, part_shape = vmem((patches * BLOCK, 128), f32), vmem((patches * PART, 128), f32)
    pieces_image, pieces_variance = keep(pieces_image, pieces_variance)
    line = shape(1, 128, dtype=i32)
    index, sent_cell, table = pl.pallas_call(
        plan_kernel,
        out_shape=(line, shape(patches, 1, 128, dtype=i32), line),
        in_specs=[far] * 5 + [SCALARS],
        out_specs=(WHOLE,) * 3,
        scratch_shapes=[
            smem((pieces,), i32), smem((pieces,), i32),
            smem((1, slots), i32), smem((1, slots), i32), smem((V,), i32),
            smem((patches,), i32), smem((2 * patches,), i32), smem((2 * patches,), i32), dma((5,)),
        ],
        compiler_params=params(),
        name="plan",
    )(
        *keep(
            piece_patch.reshape(-1), piece_cell.reshape(-1), stamp_row, stamp_col, warp_offsets,
        ),
        stamp_count,
    )

    row_bands, cols, rows = keep(*[jnp.asarray(x) for x in constants()])
    rim, small_rim = vmem((HALO, CW), f32), vmem((V * SR, CW), f32)
    field = shape(V, RT, CW)
    science, inverse, basis, gathered, root = pl.pallas_call(
        functools.partial(front_kernel, slots),
        out_shape=(
            shape(V, CE, CW), shape(V * CE, CW), shape(NB, CE, CW), shape(subtiles, 2 * XR, 128), field,
        ),
        in_specs=[WHOLE] * 3 + [far] * 5,
        out_specs=(WHOLE,) * 5,
        scratch_shapes=[
            *[vmem((pieces + 1, CR, CW), f32)] * 6, vmem((2, 1, 128), i32), smem((3, 1, 128), i32),
            sent_shape, part_shape, part_shape, sent_shape, part_shape, part_shape,
            vmem((patches, 1, 128), i32), vmem((2, 1, 128), i32),
            vmem((V * RT, 128), f32), vmem((V * RT, 128), f32), vmem((RT, CW), f32),
            rim, rim, rim, rim,
            vmem((TE, CW), f32), vmem((NT, TE, CW), f32),
            vmem((RT * XR, 128), f32), vmem((RT * XR, 128), f32), vmem((RT, CW), f32),
            vmem((2, NCELL * RC, CW), f32), vmem((V, NCELL * RC, CW), f32), small_rim, small_rim, small_rim, small_rim,
            vmem((V, NCELL * RC, CW), f32), vmem((2 * V * XR, 128), f32), vmem((2 * XR, 128), f32),
            vmem(row_bands.shape, bf16), vmem(cols.shape, bf16), vmem(rows.shape, bf16),
            dma((4,)), dma((4,)), dma((3, 2)), dma((3, 2)),
            dma((subtiles - 1,)), dma((subtiles - 1,)),
            dma((4,)), dma((4,)), dma((2,)), dma((2,)), dma((8,)),
        ],
        compiler_params=pltpu.CompilerParams(
            vmem_limit_bytes=32 * 1024 * 1024, collective_id=0, has_side_effects=True
        ),
        name="front",
    )(index, sent_cell, table, pieces_image, pieces_variance, row_bands, cols, rows)

    normalizer = float(subtiles * slots * (2 * SH + 1) ** 2)
    difference, significance = pl.pallas_call(
        functools.partial(final_kernel, normalizer),
        out_shape=(field, field),
        in_specs=[WHOLE] * 5 + [far] * 2,
        out_specs=(WHOLE,) * 2,
        scratch_shapes=[
            vmem((V * XR, 128), f32), vmem((V * CE, CW), f32),
            vmem((2, CW, CW), bf16), vmem(rows.shape[1:], bf16), dma((2,)),
        ],
        compiler_params=params(),
        name="final",
    )(gathered, basis, science, inverse, root, cols, rows)
    return (difference[:, None], significance[:, None])


def solution(mesh):
    in_specs = (
        P("sub", "patch", None, None),
        P("sub", "patch", None, None),
        P("sub", "patch", None),
        P("sub", "patch"),
        P("patch", "sub"),
        P("patch", "sub"),
        P("patch", "sub"),
        P(),
    )
    out_specs = (P(None, "patch", "sub", None), P(None, "patch", "sub", None))
    return jax.shard_map(local, mesh=mesh, in_specs=in_specs, out_specs=out_specs, check_vma=False)
```
